32 devices in a mesh: tm: 8 (over z, x), rows: 4 (over y, core).
Axes of the slice: x: 2, y: 2, z: 4, core: 2. Of those that a mesh axis runs over, the one named last changes fastest.
Arguments:
- x_in: bfloat16 [8, 1024, 512], P('rows', 'tm'), may hold values from -24 to 24
- lengths: int32 [8, 16], P('rows'), may hold values from 1 to 512, 1024 in all within a row
- bn_gain: float32 [2, 512], replicated, may hold values from 0.25 to 1.75
- bn_bias: float32 [2, 512], replicated, may hold values from -3 to 3
- w_in: bfloat16 [2, 512, 512], replicated, may hold values from -0.25 to 0.25
- decay_rate: float32 [2, 256], replicated, may hold values from 0.00012207031 to 0.033
- phase: float32 [2, 256], replicated, may hold values from -3.140625 to 3.140625
- w_out: bfloat16 [2, 512, 512], replicated, may hold values from -0.25 to 0.25
- skip_gain: float32 [2, 512], replicated, may hold values from -4 to 4
- w_glu: bfloat16 [2, 512, 1024], replicated, may hold values from -0.5 to 0.5
- b_glu: float32 [2, 1024], replicated, may hold values from -2 to 2
- grad_out: bfloat16 [8, 1024, 512], P('rows', 'tm'), may hold values from -5 to 5
Outputs:
- out: bfloat16 [8, 1024, 512], P('rows', 'tm')
- grad_x: float32 [8, 1024, 512], P('rows', 'tm')
- g_bn_gain: float32 [2, 512], replicated
- g_bn_bias: float32 [2, 512], replicated
- g_w_in: float32 [2, 512, 512], replicated
- g_decay_rate: float32 [2, 256], replicated
- g_phase: float32 [2, 256], replicated
- g_w_out: float32 [2, 512, 512], replicated
- g_skip_gain: float32 [2, 512], replicated
- g_w_glu: float32 [2, 512, 1024], replicated
- g_b_glu: float32 [2, 1024], replicated
The draws below stay inside these ranges and needn't reach their ends.
All inputs are finite; a program needn't handle non-finite values.
Results may differ from the reference program's by a relative error of at most 0.015.
Values sent between devices are 32-bit elements; how exact they have to be, the bound alone decides.
No kernel may reach another device: no remote copies, remote signals or barrier semaphores. Data moves between devices by JAX's collectives and lax.ppermute only.
A program may use at most 128 MiB of HBM per device.

```python
import math
import jax
import jax.numpy as jnp
import numpy as np
from jax import lax

D = 512
NS = 256
SEQS_ROW = 16
ROWS = 8
LEN = 1024
MOST = 512


def draw_x_in(key, part):
    keys = jax.random.split(key, 4)
    shape = (ROWS, LEN, D)
    noise = jax.random.truncated_normal(keys[0], -4.0, 4.0, shape, jnp.float32)
    column = jnp.exp(jax.random.uniform(keys[1], (1, 1, D), jnp.float32, math.log(0.5), math.log(1.5)))
    center = 0.3 * jax.random.truncated_normal(keys[2], -3.0, 3.0, (1, 1, D), jnp.float32)
    place = jnp.arange(LEN, dtype=jnp.float32) / LEN
    rising = jnp.exp(math.log(3.0) * place)[None, :, None] * jax.random.uniform(keys[3], (ROWS, LEN, 1), jnp.float32, 0.8, 1.2)
    return (rising * column * noise + center).astype(jnp.bfloat16)


def steps_of(rng, shape, cuts, smallest, top_value):
    loudness, own = 1.0, jax.random.fold_in(rng, 6)
    for dim, blocks in cuts:
        steps = jnp.exp(jax.random.uniform(jax.random.fold_in(own, dim), (blocks,), jnp.float32, smallest / len(cuts), top_value / len(cuts)))
        loudness = loudness * jnp.repeat(steps, shape[dim] // blocks).reshape([-1 if axis == dim else 1 for axis in range(len(shape))])
    return loudness


def split_up(number_of, total, bound, lean):
    portions = [(1 << 20) // math.isqrt(standing ** lean) + 1 for standing in range(2, number_of + 1)]
    rest, holding = total - bound - (number_of - 1), [1] * (number_of - 1)
    while rest > 0:
        movable = [i for i in range(number_of - 1) if holding[i] < bound]
        whole, remaining = sum([portions[i] for i in movable]), rest
        for i in movable:
            extra = min(bound - holding[i], max(1, remaining * portions[i] // whole), rest)
            holding[i] = holding[i] + extra
            rest = rest - extra
    return np.array([bound] + holding)


def uneven_parts(rng, count, total, most, slope):
    if count == 2:
        one = jax.random.randint(rng, (), max(1, total - most), min(most, total - 1) + 1)
        return jnp.stack([one, total - one])
    sizes = jnp.asarray(split_up(count, total, most, slope), jnp.int32)
    couples = (count - 1) // 2
    giver, receiver = sizes[1:1 + 2 * couples:2], sizes[2:2 + 2 * couples:2]
    room = jnp.minimum(giver - 1, most - receiver)
    shifted = jax.random.randint(jax.random.fold_in(rng, 1), (couples,), 0, 1 << 20) % (room + 1)
    sizes = sizes.at[1:1 + 2 * couples:2].set(giver - shifted).at[2:2 + 2 * couples:2].set(receiver + shifted)
    return sizes[jax.random.permutation(jax.random.fold_in(rng, 2), count)]


def bell_draw(key, dims, spread, limit, cuts=(), kind=jnp.bfloat16):
    values = spread * jax.random.normal(key, dims, jnp.float32)
    if cuts:
        values = values * steps_of(key, dims, cuts, -0.22, 0.18)
    return jnp.clip(values, -limit, limit).astype(kind)


def setup_inputs(seed: int = 0) -> dict:
    key_of = jax.random.split(jax.random.key(seed), 13)
    return {
        "x_in": draw_x_in(jax.random.fold_in(key_of[12], 71), 0),
        "lengths": jax.vmap(lambda own: uneven_parts(own, SEQS_ROW, LEN, MOST, 2))(jax.random.split(key_of[1], ROWS)).reshape((ROWS, SEQS_ROW)).astype(jnp.int32),
        "bn_gain": jnp.clip(1.0 + 0.15 * jax.random.normal(key_of[2], (2, D), jnp.float32), 0.25, 1.75),
        "bn_bias": bell_draw(key_of[3], (2, D), 0.5, 3.0, (), jnp.float32),
        "w_in": bell_draw(key_of[4], (2, D, 2 * NS), D ** -0.5, 0.25),
        "decay_rate": jnp.clip(jnp.exp(jax.random.uniform(key_of[5], (2, NS), jnp.float32, math.log(0.00012207031), math.log(0.033))), 0.00012207031, 0.033),
        "phase": jnp.clip(jax.random.uniform(key_of[6], (2, NS), jnp.float32, -3.140625, 3.140625), -3.140625, 3.140625),
        "w_out": bell_draw(key_of[7], (2, 2 * NS, D), (2 * NS) ** -0.5, 0.25),
        "skip_gain": bell_draw(key_of[8], (2, D), 1.0, 4.0, (), jnp.float32),
        "w_glu": bell_draw(key_of[9], (2, D, 2 * D), (D // 4) ** -0.5, 0.5),
        "b_glu": bell_draw(key_of[10], (2, 2 * D), 0.3, 2.0, (), jnp.float32),
        "grad_out": bell_draw(key_of[11], (ROWS, LEN, D), 1.0, 5.0, ((0, 4), (1, 8))),
    }


@jax.custom_vjp
def low(v):
    return lax.optimization_barrier(v.astype(jnp.bfloat16)).astype(jnp.float32)

@jax.custom_vjp
def low_back(v):
    return v

def low_keep(v):
    return (low(v), None)

def low_pass(kept, grad):
    return (grad,)

def back_keep(v):
    return (v, None)

def back_low(kept, grad):
    return (low(grad),)
low.defvjp(low_keep, low_pass)
low_back.defvjp(back_keep, back_low)
norm_eps = 1e-05

def lam_terms(rate_vec, angle_vec):
    magnitude = jnp.exp(-rate_vec)
    return (magnitude * jnp.cos(angle_vec), magnitude * jnp.sin(angle_vec), jnp.sqrt(1.0 - jnp.exp(-2.0 * rate_vec)))

def glu_gate(pre_act):
    half_width = pre_act.shape[-1] // 2
    return pre_act[..., :half_width] * jax.nn.sigmoid(pre_act[..., half_width:])

def gelu_exact(values):
    return jax.nn.gelu(values, approximate=False)

def run_recurrence(coef_re, coef_im, drive_re, drive_im):
    rows_now, length, width = drive_re.shape
    block_len = 64

    def arrange(values):
        return values.reshape(rows_now, length // block_len, block_len, width).transpose(1, 2, 0, 3)

    def advance(state, element):
        state_re, state_im = state
        factor_re, factor_im, push_re, push_im = element
        next_re = factor_re * state_re - factor_im * state_im + push_re
        next_im = factor_re * state_im + factor_im * state_re + push_im
        return ((next_re, next_im), (next_re, next_im))

    @jax.checkpoint
    def block_step(state, element):
        return lax.scan(advance, state, element)
    initial = (jnp.zeros((rows_now, width), jnp.float32), jnp.zeros((rows_now, width), jnp.float32))
    _, (result_re, result_im) = lax.scan(block_step, initial, (arrange(coef_re), arrange(coef_im), arrange(drive_re), arrange(drive_im)))

    def restore(values):
        return values.transpose(2, 0, 1, 3).reshape(rows_now, length, width)
    return (restore(result_re), restore(result_im))

def run_block(current, params, keep_mask, backward_time):
    gain_vec, bias_vec, w_in, rate_vec, angle_vec, w_out, skip_vec, w_glu, b_glu = params
    states = w_in.shape[1] // 2
    mean_vec = lax.optimization_barrier(jnp.mean(current, axis=(0, 1)))
    var_vec = lax.optimization_barrier(jnp.mean(current * current, axis=(0, 1))) - mean_vec * mean_vec
    normed = (current - mean_vec) * lax.rsqrt(var_vec + norm_eps)
    scaled = gain_vec * normed + bias_vec
    projected = low_back(jnp.einsum('rtd,dk->rtk', low(scaled), w_in, precision=lax.Precision.HIGHEST))
    lam_re, lam_im, norm_factor = lam_terms(rate_vec, angle_vec)
    coef_re = keep_mask[:, :, None] * lam_re
    coef_im = keep_mask[:, :, None] * lam_im
    drive_re = norm_factor * projected[:, :, :states]
    drive_im = norm_factor * projected[:, :, states:]
    if backward_time:
        state_re, state_im = run_recurrence(jnp.flip(coef_re, 1), jnp.flip(coef_im, 1), jnp.flip(drive_re, 1), jnp.flip(drive_im, 1))
        state_re = jnp.flip(state_re, 1)
        state_im = jnp.flip(state_im, 1)
    else:
        state_re, state_im = run_recurrence(coef_re, coef_im, drive_re, drive_im)
    state_cat = jnp.concatenate([state_re, state_im], axis=2)
    mixed = low_back(jnp.einsum('rtk,kd->rtd', low(state_cat), w_out, precision=lax.Precision.HIGHEST)) + skip_vec * scaled
    active = low(gelu_exact(mixed))
    gate_pre = low_back(jnp.einsum('rtd,dk->rtk', active, w_glu, precision=lax.Precision.HIGHEST)) + b_glu
    return current + glu_gate(gate_pre)

def reference(x_in, lengths, bn_gain, bn_bias, w_in, decay_rate, phase, w_out, skip_gain, w_glu, b_glu, grad_out):
    seq_ends = jnp.cumsum(lengths, axis=1).astype(jnp.int32)
    seq_starts = (seq_ends - lengths).astype(jnp.int32)
    seq_lasts = (seq_ends - 1).astype(jnp.int32)
    positions = jnp.arange(LEN, dtype=jnp.int32)

    def kept_where(table):
        matched = jnp.any(positions[None, :, None] == table[:, None, :], axis=2)
        return 1.0 - matched.astype(jnp.float32)
    keep_masks = (kept_where(seq_starts), kept_where(seq_lasts))
    params = (bn_gain, bn_bias, w_in.astype(jnp.float32), decay_rate, phase, w_out.astype(jnp.float32), skip_gain, w_glu.astype(jnp.float32), b_glu)

    def forward(inputs, weights):
        current = inputs
        for block_index in range(2):
            block_params = tuple((member[block_index] for member in weights))
            current = run_block(current, block_params, keep_masks[block_index], block_index == 1)
        return current
    result, pull = jax.vjp(forward, x_in.astype(jnp.float32), params)
    grad_input, grad_params = pull(grad_out.astype(jnp.float32))
    return (result.astype(jnp.bfloat16), grad_input, grad_params[0], grad_params[1], grad_params[2], grad_params[3], grad_params[4], grad_params[5], grad_params[6], grad_params[7], grad_params[8])
```

```python
import functools

import jax
import jax.numpy as jnp
from jax import lax
from jax.experimental import pallas as pl
from jax.experimental.pallas import tpu as pltpu
from jax.sharding import PartitionSpec as P

EPS = 1e-05
LANES = 128
CHUNKS = 8
TILE = 32
F32 = jnp.float32
BF16 = jnp.bfloat16
ROOT_HALF = 0.7071067811865476
ROOT_TWO_PI_INV = 0.3989422804014327


class Sizes:
    def __init__(self, rows, steps, width, states, count_tm, count_rows, per_row):
        self.R, self.S, self.D, self.N = rows, steps, width, states
        self.T = rows * steps
        self.L = steps // CHUNKS
        self.tm, self.rows = count_tm, count_rows
        self.all = count_tm * count_rows
        self.seqs = per_row
        self.half = states // LANES
        self.packed = rows * 2 * self.half
        self.stat = 2 * width // LANES
        self.tokens = self.T * self.all


def dot(a, b):
    return jnp.dot(a, b, preferred_element_type=F32)


def dot_t(a, b):
    return lax.dot_general(a, b, (((1,), (1,)), ((), ())), preferred_element_type=F32)


def dot_0(a, b):
    return lax.dot_general(a, b, (((0,), (0,)), ((), ())), preferred_element_type=F32)


def fold(a):
    return a.reshape(a.shape[0] // 8, 8, a.shape[1]).sum(0)


def wide(a, z):
    return jnp.concatenate([a] * z.half, axis=1)


def tiles(z, body, carry):
    def one(i, c):
        return body(pl.ds(pl.multiple_of(i * TILE, TILE), TILE), c)

    return lax.fori_loop(0, z.T // TILE, one, carry)


def pack(ref, rows):
    k = 0
    for row in rows:
        for i in range(row.shape[1] // LANES):
            ref[k : k + 1, :] = row[:, i * LANES : (i + 1) * LANES]
            k += 1


def unpack(ref, first, count):
    return jnp.concatenate([ref[first + i : first + i + 1, :] for i in range(count)], axis=1)


def spread(out_ref, tile_ref):
    value = tile_ref[...]
    for j in range(out_ref.shape[0]):
        out_ref[j] = value


def two_sums(recv_ref, tile_ref, z):
    tile_ref[...] = jnp.sum(recv_ref[...], axis=0)
    n = z.D // LANES
    return unpack(tile_ref, 0, n), unpack(tile_ref, n, n)


def step_rows(z, r, s):
    first = r * z.S + s * CHUNKS
    return slice(first, first + CHUNKS)


def to_steps(z, source, out_ref, natural_ref):
    lanes = z.D // LANES

    def split(rows, c):
        value = source(rows)
        for k in range(lanes):
            natural_ref[k, rows, :] = value[:, k * LANES : (k + 1) * LANES]
        return c

    tiles(z, split, 0)
    for r in range(z.R):
        for s in range(z.L):
            for k in range(lanes):
                out_ref[step_rows(z, r, s), k * LANES : (k + 1) * LANES] = natural_ref[k, pl.ds(r * z.S + s, CHUNKS, stride=z.L), :]


def to_time(z, source_ref, out_ref, natural_ref):
    lanes = z.D // LANES
    for r in range(z.R):
        for s in range(z.L):
            for k in range(lanes):
                natural_ref[k, pl.ds(r * z.S + s, CHUNKS, stride=z.L), :] = source_ref[step_rows(z, r, s), k * LANES : (k + 1) * LANES]

    def join(rows, c):
        value = jnp.concatenate([natural_ref[k, rows, :] for k in range(lanes)], axis=1)
        out_ref[rows, :] = value.astype(out_ref.dtype)
        return c

    tiles(z, join, 0)


def pair_store(z, ref):
    held = {}

    def put(r, s, re, im):
        if (r, s ^ 1) not in held:
            held[r, s] = (re, im)
            return
        other = held.pop((r, s ^ 1))
        low, high = (other, (re, im)) if s & 1 else ((re, im), other)
        rows = slice(r * z.S + (s & ~1) * CHUNKS, r * z.S + ((s & ~1) + 2) * CHUNKS)
        ref[rows, 0 : z.N] = jnp.concatenate([low[0], high[0]], axis=0).astype(ref.dtype)
        ref[rows, z.N : 2 * z.N] = jnp.concatenate([low[1], high[1]], axis=0).astype(ref.dtype)

    return put


def scan(z, drive_ref, gain, lr, li, keep_ref, state, reverse, visit=None):
    for step in range(z.L):
        s = z.L - 1 - step if reverse else step
        for r in range(z.R):
            rows = step_rows(z, r, s)
            keep = wide(keep_ref[rows, :], z)
            ur = drive_ref[rows, 0 : z.N]
            ui = drive_ref[rows, z.N : 2 * z.N]
            if gain is not None:
                ur, ui = ur * gain, ui * gain
            hr, hi = keep * state[r][0], keep * state[r][1]
            state[r] = (lr * hr - li * hi + ur, lr * hi + li * hr + ui)
            if visit is not None:
                visit(r, s, rows, *state[r])
    return state


def zeros_state(z):
    return [(jnp.zeros((CHUNKS, z.N), F32), jnp.zeros((CHUNKS, z.N), F32)) for _ in range(z.R)]


def chunk_order(reverse):
    return range(CHUNKS - 1, -1, -1) if reverse else range(CHUNKS)


def end_state(z, state, ends_ref, chunk_keep_ref, pr, pi, reverse):
    rows = []
    for r in range(z.R):
        ends_ref[r * CHUNKS : (r + 1) * CHUNKS, 0 : z.N] = state[r][0]
        ends_ref[r * CHUNKS : (r + 1) * CHUNKS, z.N : 2 * z.N] = state[r][1]
    for r in range(z.R):
        cr = ci = None
        for c in chunk_order(reverse):
            k = r * CHUNKS + c
            er, ei = ends_ref[k : k + 1, 0 : z.N], ends_ref[k : k + 1, z.N : 2 * z.N]
            if cr is None:
                cr, ci = er, ei
            else:
                keep = wide(chunk_keep_ref[k : k + 1, :], z)
                cr, ci = keep * cr, keep * ci
                cr, ci = pr * cr - pi * ci + er, pr * ci + pi * cr + ei
        rows += [cr, ci]
    return rows


def carries(z, recv_ref, device_keep_ref, power_ref, b, sign, ends_ref, chunk_keep_ref, pr, pi, tile_ref, carry_ref, reverse):
    place = lax.axis_index("tm")
    pow_re = power_ref[2 * b]
    pow_im = sign * power_ref[2 * b + 1]
    is_re = (lax.broadcasted_iota(jnp.int32, (z.packed, LANES), 0) // z.half) % 2 == 0

    def hop(i, c):
        j = z.tm - 1 - i if reverse else i
        other = jnp.where(is_re, pltpu.roll(c, z.packed - z.half, 0), pltpu.roll(c, z.half, 0))
        return device_keep_ref[j] * (pow_re * c + pow_im * other) + recv_ref[j]

    ahead = z.tm - 1 - place if reverse else place
    tile_ref[...] = lax.fori_loop(0, ahead, hop, jnp.zeros((z.packed, LANES), F32))
    for r in range(z.R):
        cr = unpack(tile_ref, r * 2 * z.half, z.half)
        ci = unpack(tile_ref, r * 2 * z.half + z.half, z.half)
        order = list(chunk_order(reverse))
        for c in order:
            k = r * CHUNKS + c
            carry_ref[k : k + 1, 0 : z.N] = cr
            carry_ref[k : k + 1, z.N : 2 * z.N] = ci
            if c != order[-1]:
                keep = wide(chunk_keep_ref[k : k + 1, :], z)
                er, ei = ends_ref[k : k + 1, 0 : z.N], ends_ref[k : k + 1, z.N : 2 * z.N]
                cr, ci = keep * cr, keep * ci
                cr, ci = pr * cr - pi * ci + er, pr * ci + pi * cr + ei
    state = []
    for r in range(z.R):
        span = slice(r * CHUNKS, (r + 1) * CHUNKS)
        state.append((carry_ref[span, 0 : z.N], carry_ref[span, z.N : 2 * z.N]))
    return state


def lam_rows(z, tab_ref, b):
    def row(i):
        return tab_ref[b * 8 + i : b * 8 + i + 1, :]

    def full(i):
        return jnp.broadcast_to(row(i), (CHUNKS, z.N))

    return full(0), full(1), full(2), row(3), row(4)


def prepare(z, len_ref, x_ref, gout_ref, rate_ref, phase_ref, v_ref, up_ref, stat_ref, keep_f, keep_r, chunk_f, chunk_r, dev_f, dev_r, tab_ref, power_ref, tile_ref, natural_ref):
    to_steps(z, lambda rows: x_ref[rows, :].astype(F32), v_ref, natural_ref)
    to_steps(z, lambda rows: gout_ref[rows, :].astype(F32), up_ref, natural_ref)

    def body(rows, c):
        v = v_ref[rows, :]
        return c[0] + fold(v), c[1] + fold(v * v)

    zero = jnp.zeros((8, z.D), F32)
    s0, s1 = tiles(z, body, (zero, zero))
    pack(tile_ref, [jnp.sum(s0, 0, keepdims=True), jnp.sum(s1, 0, keepdims=True)])
    spread(stat_ref, tile_ref)
    base = lax.axis_index("tm") * z.S
    place = lax.broadcasted_iota(jnp.int32, (z.S, LANES), 0)
    at = base + (place % CHUNKS) * z.L + place // CHUNKS
    chunk_at = base + z.L * lax.broadcasted_iota(jnp.int32, (CHUNKS, LANES), 0)
    dev_at = z.S * lax.broadcasted_iota(jnp.int32, (z.tm, LANES), 0)
    for r in range(z.R):
        end = jnp.int32(0)
        hit = [jnp.zeros(a.shape, jnp.bool_) for a in (at, at, chunk_at, chunk_at, dev_at, dev_at)]
        for q in range(z.seqs):
            start = end
            end = end + len_ref[r, q]
            last = end - 1
            hit[0] = hit[0] | (at == start)
            hit[1] = hit[1] | (at == last)
            for i, mark in ((2, start), (3, last)):
                hit[i] = hit[i] | ((chunk_at <= mark) & (mark < chunk_at + z.L))
            for i, mark in ((4, start), (5, last)):
                hit[i] = hit[i] | ((dev_at <= mark) & (mark < dev_at + z.S))
        keep = [1.0 - h.astype(F32) for h in hit]
        keep_f[r * z.S : (r + 1) * z.S, :] = keep[0]
        keep_r[r * z.S : (r + 1) * z.S, :] = keep[1]
        chunk_f[r * CHUNKS : (r + 1) * CHUNKS, :] = keep[2]
        chunk_r[r * CHUNKS : (r + 1) * CHUNKS, :] = keep[3]
        each = 2 * z.half
        for j in range(z.tm):
            for ref, k in ((dev_f, keep[4]), (dev_r, keep[5])):
                ref[j, r * each : (r + 1) * each, :] = jnp.broadcast_to(k[j : j + 1, :], (each, LANES))
    for b in range(2):
        rate, angle = rate_ref[b : b + 1, :], phase_ref[b : b + 1, :]
        size = jnp.exp(-rate)
        lr, li = size * jnp.cos(angle), size * jnp.sin(angle)
        gamma = jnp.sqrt(1.0 - jnp.exp(-2.0 * rate))

        def power(n):
            out, br, bi = None, lr, li
            while n:
                if n & 1:
                    out = (br, bi) if out is None else (out[0] * br - out[1] * bi, out[0] * bi + out[1] * br)
                br, bi = br * br - bi * bi, 2.0 * br * bi
                n >>= 1
            return out

        chunk_power, device_power = power(z.L), power(z.S)
        rows = [lr, li, gamma, chunk_power[0], chunk_power[1], jnp.exp(-2.0 * rate) / gamma]
        for i, row in enumerate(rows):
            tab_ref[b * 8 + i : b * 8 + i + 1, :] = row
        for i in range(6, 8):
            tab_ref[b * 8 + i : b * 8 + i + 1, :] = jnp.zeros_like(lr)
        pack(power_ref.at[2 * b], [device_power[0], device_power[0]] * z.R)
        pack(power_ref.at[2 * b + 1], [-device_power[1], device_power[1]] * z.R)


def enter(z, b, stat_ref, v_ref, gain_ref, bias_ref, win_ref, keep_ref, chunk_ref, tab_ref,
          norm_ref, low_ref, proj_ref, ends_ref, send_ref, stat_tile, tile_ref):
    total, square = two_sums(stat_ref, stat_tile, z)
    mean = total / z.tokens
    rstd = lax.rsqrt(square / z.tokens - mean * mean + EPS)
    norm_ref[0:1, :] = mean
    norm_ref[1:2, :] = rstd
    gain, bias = gain_ref[b : b + 1, :], bias_ref[b : b + 1, :]

    def body(rows, c):
        xhat = (v_ref[rows, :] - mean) * rstd
        low_ref[rows, :] = (gain * xhat + bias).astype(BF16)
        return c

    tiles(z, body, 0)
    proj_ref[...] = dot(low_ref[...], win_ref[b])
    lr, li, gamma, pr, pi = lam_rows(z, tab_ref, b)
    state = scan(z, proj_ref, gamma, lr, li, keep_ref, zeros_state(z), b == 1)
    pack(tile_ref, end_state(z, state, ends_ref, chunk_ref, pr, pi, b == 1))
    spread(send_ref, tile_ref)


def gelu_pair(y):
    cdf = 0.5 + 0.5 * lax.erf(y * ROOT_HALF)
    return y * cdf, cdf + y * (ROOT_TWO_PI_INV * jnp.exp(-0.5 * y * y))


def mix(z, b, recv_ref, dev_ref, power_ref, ends_ref, chunk_ref, proj_ref, keep_ref, tab_ref, v_ref, norm_ref, gain_ref,
        bias_ref, skip_ref, wout_ref, wglu_ref, h_ref, hlow_ref, carry_ref, slope_ref, act_ref, tile_ref, wide_ref):
    lr, li, gamma, pr, pi = lam_rows(z, tab_ref, b)
    state = carries(z, recv_ref, dev_ref, power_ref, b, 1.0, ends_ref, chunk_ref, pr, pi, tile_ref, carry_ref, b == 1)

    put = pair_store(z, hlow_ref)

    def visit(r, s, rows, hr, hi):
        h_ref[rows, 0 : z.N] = hr
        h_ref[rows, z.N : 2 * z.N] = hi
        put(r, s, hr, hi)

    scan(z, proj_ref, gamma, lr, li, keep_ref, state, b == 1, visit)
    slope_ref[...] = dot(hlow_ref[...], wout_ref[b])
    mean, rstd = norm_ref[0:1, :], norm_ref[1:2, :]
    gain, bias, skip = gain_ref[b : b + 1, :], bias_ref[b : b + 1, :], skip_ref[b : b + 1, :]

    def body(rows, c):
        xn = gain * ((v_ref[rows, :] - mean) * rstd) + bias
        act, slope = gelu_pair(slope_ref[rows, :] + skip * xn)
        act_ref[rows, :] = act.astype(BF16)
        slope_ref[rows, :] = slope
        return c

    tiles(z, body, 0)
    wide_ref[...] = dot(act_ref[...], wglu_ref[b])


def middle(z, recv_ref, dev_ref, power_ref, ends_ref, chunk_ref, proj_ref, keep_ref, tab_ref, v_ref, norm_ref, gain_ref,
           bias_ref, skip_ref, wout_ref, wglu_ref, bglu_ref,
           h_ref, hlow_ref, carry_ref, slope_ref, act_ref, sig_ref, gate_ref, next_ref, stat_ref, tile_ref, wide_ref, stat_tile):
    mix(z, 0, recv_ref, dev_ref, power_ref, ends_ref, chunk_ref, proj_ref, keep_ref, tab_ref, v_ref, norm_ref, gain_ref,
        bias_ref, skip_ref, wout_ref, wglu_ref, h_ref, hlow_ref, carry_ref, slope_ref, act_ref, tile_ref, wide_ref)
    d = z.D
    b1, b2 = bglu_ref[0:1, 0:d], bglu_ref[0:1, d : 2 * d]

    def body(rows, c):
        z1 = wide_ref[rows, 0:d] + b1
        sig = jax.nn.sigmoid(wide_ref[rows, d : 2 * d] + b2)
        prod = z1 * sig
        sig_ref[rows, :] = sig
        gate_ref[rows, :] = prod * (1.0 - sig)
        v = v_ref[rows, :] + prod
        next_ref[rows, :] = v
        return c[0] + fold(v), c[1] + fold(v * v)

    zero = jnp.zeros((8, d), F32)
    s0, s1 = tiles(z, body, (zero, zero))
    pack(stat_tile, [jnp.sum(s0, 0, keepdims=True), jnp.sum(s1, 0, keepdims=True)])
    spread(stat_ref, stat_tile)


def descend(z, b, grad_bglu, dz_ref, slope_ref, v_ref, norm_ref, gain_ref, bias_ref, wglu_ref, wout_ref, keep_ref, chunk_ref, tab_ref,
            dy_ref, dylow_ref, dh_ref, ends_ref, send_ref, small_ref, tile_ref):
    dy_ref[...] = dot_t(dz_ref[...], wglu_ref[b])
    mean, rstd = norm_ref[0:1, :], norm_ref[1:2, :]
    gain, bias = gain_ref[b : b + 1, :], bias_ref[b : b + 1, :]

    def body(rows, c):
        xn = gain * ((v_ref[rows, :] - mean) * rstd) + bias
        dy = dy_ref[rows, :] * slope_ref[rows, :]
        dy_ref[rows, :] = dy
        dylow_ref[rows, :] = dy.astype(BF16)
        return c + fold(dy * xn)

    grad_skip = tiles(z, body, jnp.zeros((8, z.D), F32))
    small_ref[0:1, :] = jnp.sum(grad_skip, 0, keepdims=True)
    total = jnp.sum(grad_bglu, 0, keepdims=True)
    small_ref[1:2, :] = total[:, 0 : z.D]
    small_ref[2:3, :] = total[:, z.D : 2 * z.D]
    dh_ref[...] = dot_t(dylow_ref[...], wout_ref[b])
    lr, li, _, pr, pi = lam_rows(z, tab_ref, b)
    state = scan(z, dh_ref, None, lr, -li, keep_ref, zeros_state(z), b == 0)
    pack(tile_ref, end_state(z, state, ends_ref, chunk_ref, pr, -pi, b == 0))
    spread(send_ref, tile_ref)


def turn(z, recv_ref, dev_ref, power_ref, ends_ref, chunk_ref, proj_ref, keep_ref, tab_ref, v_ref, norm_ref, gain_ref,
         bias_ref, skip_ref, wout_ref, wglu_ref, bglu_ref, gout_ref, adj_keep_ref, adj_chunk_ref,
         h_ref, hlow_ref, carry_ref, act_ref, out_ref, dz_ref, dy_ref, dylow_ref, dh_ref, adj_ends_ref, send_ref, small_ref,
         tile_ref, wide_ref, slope_ref, natural_ref):
    mix(z, 1, recv_ref, dev_ref, power_ref, ends_ref, chunk_ref, proj_ref, keep_ref, tab_ref, v_ref, norm_ref, gain_ref,
        bias_ref, skip_ref, wout_ref, wglu_ref, h_ref, hlow_ref, carry_ref, slope_ref, act_ref, tile_ref, wide_ref)
    d = z.D
    b1, b2 = bglu_ref[1:2, 0:d], bglu_ref[1:2, d : 2 * d]

    def body(rows, c):
        z1 = wide_ref[rows, 0:d] + b1
        sig = jax.nn.sigmoid(wide_ref[rows, d : 2 * d] + b2)
        prod = z1 * sig
        dy_ref[rows, :] = v_ref[rows, :] + prod
        e = gout_ref[rows, :]
        d1, d2 = e * sig, e * (prod * (1.0 - sig))
        dz_ref[rows, 0:d] = d1.astype(BF16)
        dz_ref[rows, d : 2 * d] = d2.astype(BF16)
        return c[0] + fold(d1), c[1] + fold(d2)

    zero = jnp.zeros((8, d), F32)
    s0, s1 = tiles(z, body, (zero, zero))
    to_time(z, dy_ref, out_ref, natural_ref)
    descend(z, 1, jnp.concatenate([s0, s1], axis=1), dz_ref, slope_ref, v_ref, norm_ref, gain_ref, bias_ref, wglu_ref, wout_ref,
            adj_keep_ref, adj_chunk_ref, tab_ref, dy_ref, dylow_ref, dh_ref, adj_ends_ref, send_ref, small_ref, tile_ref)


def finish(z, b, recv_ref, dev_ref, power_ref, ends_ref, chunk_ref, dh_ref, keep_ref, tab_ref, proj_ref, h_ref, carry_ref,
           fwd_keep_ref, dy_ref, v_ref, norm_ref, skip_ref, win_ref,
           dplow_ref, dxn_ref, stat_ref, lam_ref, tile_ref, adj_carry_ref, stat_tile):
    lr, li, gamma, pr, pi = lam_rows(z, tab_ref, b)
    reverse = b == 0
    state = carries(z, recv_ref, dev_ref, power_ref, b, -1.0, ends_ref, chunk_ref, pr, -pi, tile_ref, adj_carry_ref, reverse)
    zero = jnp.zeros((CHUNKS, z.N), F32)
    sums = [zero, zero, zero]
    put = pair_store(z, dplow_ref)

    def visit(r, s, rows, gr, gi):
        put(r, s, gamma * gr, gamma * gi)
        sums[2] = sums[2] + gr * proj_ref[rows, 0 : z.N] + gi * proj_ref[rows, z.N : 2 * z.N]
        if s == (0 if b == 0 else z.L - 1):
            span = slice(r * CHUNKS, (r + 1) * CHUNKS)
            nr, ni = carry_ref[span, 0 : z.N], carry_ref[span, z.N : 2 * z.N]
        else:
            near = step_rows(z, r, s - 1 if b == 0 else s + 1)
            nr, ni = h_ref[near, 0 : z.N], h_ref[near, z.N : 2 * z.N]
        keep = wide(fwd_keep_ref[rows, :], z)
        nr, ni = keep * nr, keep * ni
        sums[0] = sums[0] + (gr * nr + gi * ni)
        sums[1] = sums[1] + (gi * nr - gr * ni)

    scan(z, dh_ref, None, lr, -li, keep_ref, state, reverse, visit)
    dr, di, dg = (jnp.sum(s, 0, keepdims=True) for s in sums)
    r0, i0 = lr[0:1, :], li[0:1, :]
    lam_ref[0:1, :] = dg * tab_ref[b * 8 + 5 : b * 8 + 6, :] - (dr * r0 + di * i0)
    lam_ref[1:2, :] = di * r0 - dr * i0

    dxn_ref[...] = dot_t(dplow_ref[...], win_ref[b])
    mean, rstd = norm_ref[0:1, :], norm_ref[1:2, :]
    skip = skip_ref[b : b + 1, :]

    def body(rows, c):
        xhat = (v_ref[rows, :] - mean) * rstd
        dxn = dxn_ref[rows, :] + skip * dy_ref[rows, :]
        dxn_ref[rows, :] = dxn
        return c[0] + fold(dxn), c[1] + fold(dxn * xhat)

    zero = jnp.zeros((8, z.D), F32)
    s0, s1 = tiles(z, body, (zero, zero))
    pack(stat_tile, [jnp.sum(s0, 0, keepdims=True), jnp.sum(s1, 0, keepdims=True)])
    spread(stat_ref, stat_tile)


def norm_grad(z, b, stat_ref, stat_tile, norm_ref, gain_ref, total_ref):
    bias_sum, gain_sum = two_sums(stat_ref, stat_tile, z)
    total_ref[0:1, :] = bias_sum
    total_ref[1:2, :] = gain_sum
    mean, rstd = norm_ref[0:1, :], norm_ref[1:2, :]
    gain = gain_ref[b : b + 1, :]
    scale, shift, slope = rstd * gain, rstd * gain * bias_sum / z.tokens, rstd * gain * gain_sum / z.tokens

    def grad(dxn, v, up):
        return scale * dxn - shift - ((v - mean) * rstd) * slope + up

    return grad


def lower_block(z, stat_ref, dxn_ref, v1_ref, norm1_ref, gout_ref, sig_ref, gate_ref, slope_ref, v_ref, norm_ref, gain_ref, bias_ref,
                wglu_ref, wout_ref, keep_ref, chunk_ref, tab_ref,
                total_ref, e_ref, dz_ref, dy_ref, dylow_ref, dh_ref, ends_ref, send_ref, small_ref, tile_ref, stat_tile):
    grad = norm_grad(z, 1, stat_ref, stat_tile, norm1_ref, gain_ref, total_ref)
    d = z.D

    def body(rows, c):
        e = grad(dxn_ref[rows, :], v1_ref[rows, :], gout_ref[rows, :])
        e_ref[rows, :] = e
        d1, d2 = e * sig_ref[rows, :], e * gate_ref[rows, :]
        dz_ref[rows, 0:d] = d1.astype(BF16)
        dz_ref[rows, d : 2 * d] = d2.astype(BF16)
        return c[0] + fold(d1), c[1] + fold(d2)

    zero = jnp.zeros((8, d), F32)
    s0, s1 = tiles(z, body, (zero, zero))
    descend(z, 0, jnp.concatenate([s0, s1], axis=1), dz_ref, slope_ref, v_ref, norm_ref, gain_ref, bias_ref, wglu_ref, wout_ref,
            keep_ref, chunk_ref, tab_ref, dy_ref, dylow_ref, dh_ref, ends_ref, send_ref, small_ref, tile_ref)


def last(z, stat_ref, dxn_ref, v_ref, norm_ref, gain_ref, e_ref, total_ref, grad_ref, stat_tile, natural_ref, work_ref):
    grad = norm_grad(z, 0, stat_ref, stat_tile, norm_ref, gain_ref, total_ref)

    def body(rows, c):
        work_ref[rows, :] = grad(dxn_ref[rows, :], v_ref[rows, :], e_ref[rows, :])
        return c

    tiles(z, body, 0)
    to_time(z, work_ref, grad_ref, natural_ref)


def outer(z, act_ref, dz_ref, hlow_ref, dylow_ref, wglu_ref, wout_ref):
    wglu_ref[...] = dot_0(act_ref[...], dz_ref[...])
    wout_ref[...] = dot_0(hlow_ref[...], dylow_ref[...])


def outer_in(z, low_ref, dplow_ref, win_ref):
    win_ref[...] = dot_0(low_ref[...], dplow_ref[...])


def run(kernel, name, outs, args, scratch=(), smem=0):
    spaces = [pltpu.SMEM] * smem + [pltpu.VMEM] * (len(args) - smem)
    return pl.pallas_call(
        kernel,
        out_shape=[jax.ShapeDtypeStruct(s, t) for s, t in outs],
        in_specs=[pl.BlockSpec(memory_space=m) for m in spaces],
        out_specs=[pl.BlockSpec(memory_space=pltpu.VMEM)] * len(outs),
        scratch_shapes=[pltpu.VMEM(s, t) for s, t in scratch],
        compiler_params=pltpu.CompilerParams(vmem_limit_bytes=24 << 20),
        name=name,
    )(*args)


def body(x_in, lengths, bn_gain, bn_bias, w_in, decay_rate, phase, w_out, skip_gain, w_glu, b_glu, grad_out):
    rows, steps, width = x_in.shape
    z = Sizes(rows, steps, width, w_in.shape[2] // 2, lax.axis_size("tm"), lax.axis_size("rows"), lengths.shape[1])
    T, D, N = z.T, z.D, z.N
    everyone = ("tm", "rows")

    def swap(a, axis):
        return lax.all_to_all(a, axis, 0, 0)

    stat_shape = ((z.all, z.stat, LANES), F32)
    send_shape = ((z.tm, z.packed, LANES), F32)
    tile = ((z.packed, LANES), F32)
    stat_tile = ((z.stat, LANES), F32)
    full, low = ((T, D), F32), ((T, D), BF16)
    full_n, low_n = ((T, 2 * N), F32), ((T, 2 * N), BF16)
    chunk = ((z.R * CHUNKS, 2 * N), F32)
    mask = ((T, LANES), F32)
    chunk_mask = ((z.R * CHUNKS, LANES), F32)
    norm_shape = ((8, D), F32)
    small_shape = ((8, D), F32)
    lam_shape = ((8, N), F32)
    wide_f, wide_b = ((T, 2 * D), F32), ((T, 2 * D), BF16)
    bind = functools.partial

    natural = ((D // LANES, T, LANES), F32)
    x, gout, stat0, keep_f, keep_r, chunk_f, chunk_r, dev_f, dev_r, tab, power = run(
        bind(prepare, z), "prepare",
        [full, full, stat_shape, mask, mask, chunk_mask, chunk_mask, send_shape, send_shape, ((16, N), F32), ((4, z.packed, LANES), F32)],
        (lengths, x_in.reshape(T, D), grad_out.reshape(T, D), decay_rate, phase), [stat_tile, natural], smem=1)
    stat0 = swap(stat0, everyone)
    norm0, low0, proj0, ends0, send0 = run(
        bind(enter, z, 0), "enter0", [norm_shape, low, full_n, chunk, send_shape],
        (stat0, x, bn_gain, bn_bias, w_in, keep_f, chunk_f, tab), [stat_tile, tile])
    send0 = swap(send0, "tm")
    h0, hlow0, carry0, slope0, act0, sig0, gate0, v1, stat1 = run(
        bind(middle, z), "middle", [full_n, low_n, chunk, full, low, full, full, full, stat_shape],
        (send0, dev_f, power, ends0, chunk_f, proj0, keep_f, tab, x, norm0, bn_gain, bn_bias, skip_gain, w_out, w_glu, b_glu),
        [tile, wide_f, stat_tile])
    stat1 = swap(stat1, everyone)
    norm1, low1, proj1, ends1, send1 = run(
        bind(enter, z, 1), "enter1", [norm_shape, low, full_n, chunk, send_shape],
        (stat1, v1, bn_gain, bn_bias, w_in, keep_r, chunk_r, tab), [stat_tile, tile])
    send1 = swap(send1, "tm")
    h1, hlow1, carry1, act1, out, dz1, dy1, dylow1, dh1, adj_ends1, adj1, small1 = run(
        bind(turn, z), "turn",
        [full_n, low_n, chunk, low, low, wide_b, full, low, full_n, chunk, send_shape, small_shape],
        (send1, dev_r, power, ends1, chunk_r, proj1, keep_r, tab, v1, norm1, bn_gain, bn_bias, skip_gain, w_out, w_glu, b_glu, gout,
         keep_f, chunk_f), [tile, wide_f, full, natural])
    adj1 = swap(adj1, "tm")
    gwglu1, gwout1 = run(bind(outer, z), "outer1", [((D, 2 * D), F32), ((2 * N, D), F32)], (act1, dz1, hlow1, dylow1))
    dplow1, dxn1, sum1, lam1 = run(
        bind(finish, z, 1), "finish1", [low_n, full, stat_shape, lam_shape],
        (adj1, dev_f, power, adj_ends1, chunk_f, dh1, keep_f, tab, proj1, h1, carry1, keep_r, dy1, v1, norm1, skip_gain, w_in),
        [tile, chunk, stat_tile])
    sum1 = swap(sum1, everyone)
    (gwin1,) = run(bind(outer_in, z), "outer_in1", [((D, 2 * N), F32)], (low1, dplow1))
    total1, e1, dz0, dy0, dylow0, dh0, adj_ends0, adj0, small0 = run(
        bind(lower_block, z), "lower_block",
        [norm_shape, full, wide_b, full, low, full_n, chunk, send_shape, small_shape],
        (sum1, dxn1, v1, norm1, gout, sig0, gate0, slope0, x, norm0, bn_gain, bn_bias, w_glu, w_out, keep_r, chunk_r, tab),
        [tile, stat_tile])
    adj0 = swap(adj0, "tm")
    gwglu0, gwout0 = run(bind(outer, z), "outer0", [((D, 2 * D), F32), ((2 * N, D), F32)], (act0, dz0, hlow0, dylow0))
    dplow0, dxn0, sum0, lam0 = run(
        bind(finish, z, 0), "finish0", [low_n, full, stat_shape, lam_shape],
        (adj0, dev_r, power, adj_ends0, chunk_r, dh0, keep_r, tab, proj0, h0, carry0, keep_f, dy0, x, norm0, skip_gain, w_in),
        [tile, chunk, stat_tile])
    sum0 = swap(sum0, everyone)
    (gwin0,) = run(bind(outer_in, z), "outer_in0", [((D, 2 * N), F32)], (low0, dplow0))
    total0, grad_x = run(
        bind(last, z), "last", [norm_shape, full], (sum0, dxn0, x, norm0, bn_gain, e1), [stat_tile, natural, full])
    summed = lax.psum(
        (jnp.stack([gwin0, gwin1]), jnp.stack([gwout0, gwout1]), jnp.stack([gwglu0, gwglu1]),
         jnp.stack([small0, small1]), jnp.stack([lam0, lam1])), everyone)
    gwin, gwout, gwglu, small, lam = summed
    totals = jnp.stack([total0, total1])
    return (
        out.reshape(rows, steps, width),
        grad_x.reshape(rows, steps, width),
        totals[:, 1],
        totals[:, 0],
        gwin,
        lam[:, 0],
        lam[:, 1],
        gwout,
        small[:, 0],
        gwglu,
        small[:, 1:3].reshape(2, 2 * D),
    )


def solution(mesh):
    split, rep = P("rows", "tm", None), P()
    return jax.shard_map(
        body,
        mesh=mesh,
        in_specs=(split, P("rows", None)) + (rep,) * 9 + (split,),
        out_specs=(split, split) + (rep,) * 9,
        check_vma=False,
    )
```

```python
import functools
import math

import jax
import jax.numpy as jnp
from jax import lax
from jax.experimental import pallas as pl
from jax.experimental.pallas import tpu as pltpu
from jax.sharding import PartitionSpec as P

EPS = 1e-05
LANES = 128
CHUNKS = 8
TILE = 32
F32 = jnp.float32
BF16 = jnp.bfloat16
ROOT_HALF = 0.7071067811865476
ROOT_TWO_PI_INV = 0.3989422804014327


class Sizes:
    def __init__(self, rows, steps, width, states, count_tm, count_rows, per_row):
        self.R, self.S, self.D, self.N = rows, steps, width, states
        self.T = rows * steps
        self.L = steps // CHUNKS
        self.tm, self.rows = count_tm, count_rows
        self.all = count_tm * count_rows
        self.seqs = per_row
        self.half = states // LANES
        self.packed = rows * 2 * self.half
        self.stat = 2 * width // LANES
        self.tokens = self.T * self.all
        self.bits = self.all.bit_length() - 1
        self.extra = 0


def dot(a, b):
    return jnp.dot(a, b, preferred_element_type=F32)


def dot_t(a, b):
    return lax.dot_general(a, b, (((1,), (1,)), ((), ())), preferred_element_type=F32)


def dot_0(a, b):
    return lax.dot_general(a, b, (((0,), (0,)), ((), ())), preferred_element_type=F32)


def fold(a):
    return a.reshape(a.shape[0] // 8, 8, a.shape[1]).sum(0)


def wide(a, z):
    return jnp.concatenate([a] * z.half, axis=1)


def tiles(z, body, carry):
    def one(i, c):
        return body(pl.ds(pl.multiple_of(i * TILE, TILE), TILE), c)

    return lax.fori_loop(0, z.T // TILE, one, carry)


def pack(ref, rows, k=0):
    w = ref.shape[1]
    for row in rows:
        for i in range(row.shape[1] // w):
            ref[k : k + 1, :] = row[:, i * w : (i + 1) * w]
            k += 1
    return k


def unpack(ref, first, count):
    return jnp.concatenate([ref[first + i : first + i + 1, :] for i in range(count)], axis=1)


def spread(out_ref, tile_ref):
    value = tile_ref[...]
    for j in range(out_ref.shape[0]):
        out_ref[j] = value


def two_sums(recv_ref, tile_ref, z):
    tile_ref[...] = jnp.sum(recv_ref[...], axis=0)
    n = z.D // LANES
    return unpack(tile_ref, 0, n), unpack(tile_ref, n, n)


def step_rows(z, r, s):
    first = r * z.S + s * CHUNKS
    return slice(first, first + CHUNKS)


def to_steps(z, source, out_ref, natural_ref):
    lanes = z.D // LANES

    def split(rows, c):
        value = source(rows)
        for k in range(lanes):
            natural_ref[k, rows, :] = value[:, k * LANES : (k + 1) * LANES]
        return c

    tiles(z, split, 0)
    for r in range(z.R):
        for s in range(z.L):
            for k in range(lanes):
                out_ref[step_rows(z, r, s), k * LANES : (k + 1) * LANES] = natural_ref[k, pl.ds(r * z.S + s, CHUNKS, stride=z.L), :]


def to_time(z, source_ref, out_ref, natural_ref):
    lanes = z.D // LANES
    for r in range(z.R):
        for s in range(z.L):
            for k in range(lanes):
                natural_ref[k, pl.ds(r * z.S + s, CHUNKS, stride=z.L), :] = source_ref[step_rows(z, r, s), k * LANES : (k + 1) * LANES]

    def join(rows, c):
        value = jnp.concatenate([natural_ref[k, rows, :] for k in range(lanes)], axis=1)
        out_ref[rows, :] = value.astype(out_ref.dtype)
        return c

    tiles(z, join, 0)


def pair_store(z, ref):
    held = {}

    def put(r, s, re, im):
        if (r, s ^ 1) not in held:
            held[r, s] = (re, im)
            return
        other = held.pop((r, s ^ 1))
        low, high = (other, (re, im)) if s & 1 else ((re, im), other)
        rows = slice(r * z.S + (s & ~1) * CHUNKS, r * z.S + ((s & ~1) + 2) * CHUNKS)
        ref[rows, 0 : z.N] = jnp.concatenate([low[0], high[0]], axis=0).astype(ref.dtype)
        ref[rows, z.N : 2 * z.N] = jnp.concatenate([low[1], high[1]], axis=0).astype(ref.dtype)

    return put


def scan(z, drive_ref, gain, lr, li, keep_ref, state, reverse, visit=None):
    for step in range(z.L):
        s = z.L - 1 - step if reverse else step
        for r in range(z.R):
            rows = step_rows(z, r, s)
            keep = wide(keep_ref[rows, :], z)
            ur = drive_ref[rows, 0 : z.N]
            ui = drive_ref[rows, z.N : 2 * z.N]
            if gain is not None:
                ur, ui = ur * gain, ui * gain
            hr, hi = keep * state[r][0], keep * state[r][1]
            state[r] = (lr * hr - li * hi + ur, lr * hi + li * hr + ui)
            if visit is not None:
                visit(r, s, rows, *state[r])
    return state


def zeros_state(z):
    return [(jnp.zeros((CHUNKS, z.N), F32), jnp.zeros((CHUNKS, z.N), F32)) for _ in range(z.R)]


def chunk_order(reverse):
    return range(CHUNKS - 1, -1, -1) if reverse else range(CHUNKS)


def end_state(z, state, ends_ref, chunk_keep_ref, pr, pi, reverse):
    rows = []
    for r in range(z.R):
        ends_ref[r * CHUNKS : (r + 1) * CHUNKS, 0 : z.N] = state[r][0]
        ends_ref[r * CHUNKS : (r + 1) * CHUNKS, z.N : 2 * z.N] = state[r][1]
    for r in range(z.R):
        cr = ci = None
        for c in chunk_order(reverse):
            k = r * CHUNKS + c
            er, ei = ends_ref[k : k + 1, 0 : z.N], ends_ref[k : k + 1, z.N : 2 * z.N]
            if cr is None:
                cr, ci = er, ei
            else:
                keep = wide(chunk_keep_ref[k : k + 1, :], z)
                cr, ci = keep * cr, keep * ci
                cr, ci = pr * cr - pi * ci + er, pr * ci + pi * cr + ei
        rows += [cr, ci]
    return rows


def carries(z, recv_ref, device_keep_ref, power_ref, b, sign, ends_ref, chunk_keep_ref, pr, pi, tile_ref, carry_ref, reverse):
    place = lax.axis_index("tm")
    pow_re = power_ref[2 * b]
    pow_im = sign * power_ref[2 * b + 1]
    is_re = (lax.broadcasted_iota(jnp.int32, (z.packed, LANES), 0) // z.half) % 2 == 0

    def hop(i, c):
        j = z.tm - 1 - i if reverse else i
        other = jnp.where(is_re, pltpu.roll(c, z.packed - z.half, 0), pltpu.roll(c, z.half, 0))
        return device_keep_ref[j] * (pow_re * c + pow_im * other) + recv_ref[j]

    ahead = z.tm - 1 - place if reverse else place
    tile_ref[...] = lax.fori_loop(0, ahead, hop, jnp.zeros((z.packed, LANES), F32))
    for r in range(z.R):
        cr = unpack(tile_ref, r * 2 * z.half, z.half)
        ci = unpack(tile_ref, r * 2 * z.half + z.half, z.half)
        order = list(chunk_order(reverse))
        for c in order:
            k = r * CHUNKS + c
            carry_ref[k : k + 1, 0 : z.N] = cr
            carry_ref[k : k + 1, z.N : 2 * z.N] = ci
            if c != order[-1]:
                keep = wide(chunk_keep_ref[k : k + 1, :], z)
                er, ei = ends_ref[k : k + 1, 0 : z.N], ends_ref[k : k + 1, z.N : 2 * z.N]
                cr, ci = keep * cr, keep * ci
                cr, ci = pr * cr - pi * ci + er, pr * ci + pi * cr + ei
    state = []
    for r in range(z.R):
        span = slice(r * CHUNKS, (r + 1) * CHUNKS)
        state.append((carry_ref[span, 0 : z.N], carry_ref[span, z.N : 2 * z.N]))
    return state


def lam_rows(z, tab_ref, b):
    def row(i):
        return tab_ref[b * 8 + i : b * 8 + i + 1, :]

    def full(i):
        return jnp.broadcast_to(row(i), (CHUNKS, z.N))

    return full(0), full(1), full(2), row(3), row(4)


def prepare(z, len_hbm, x_hbm, gout_hbm, rate_hbm, phase_hbm, gain_hbm, bias_hbm, skip_hbm, bglu_hbm, win_hbm, wout_hbm, wglu_hbm,
            v_ref, up_ref, stat_ref, keep_f, keep_r, chunk_f, chunk_r, dev_f, dev_r, tab_ref, power_ref,
            gain_ref, bias_ref, skip_ref, bglu_ref, win_ref, wout_ref, wglu_ref,
            tile_ref, natural_ref, x_ref, gout_ref, rate_ref, phase_ref, len_ref, sem):
    moves = [(x_hbm, x_ref), (len_hbm, len_ref), (rate_hbm, rate_ref), (phase_hbm, phase_ref), (gout_hbm, gout_ref),
             (gain_hbm, gain_ref), (bias_hbm, bias_ref), (win_hbm, win_ref), (skip_hbm, skip_ref), (bglu_hbm, bglu_ref),
             (wout_hbm, wout_ref), (wglu_hbm, wglu_ref)]
    copies = [pltpu.make_async_copy(a, b, sem.at[i]) for i, (a, b) in enumerate(moves)]
    for c in copies:
        c.start()
    copies[0].wait()
    to_steps(z, lambda rows: x_ref[rows, :].astype(F32), v_ref, natural_ref)

    def body(rows, c):
        v = v_ref[rows, :]
        return c[0] + fold(v), c[1] + fold(v * v)

    zero = jnp.zeros((8, z.D), F32)
    s0, s1 = tiles(z, body, (zero, zero))
    pack(tile_ref, [jnp.sum(s0, 0, keepdims=True), jnp.sum(s1, 0, keepdims=True)])
    spread(stat_ref, tile_ref)
    for c in copies[1:5]:
        c.wait()
    to_steps(z, lambda rows: gout_ref[rows, :].astype(F32), up_ref, natural_ref)
    base = lax.axis_index("tm") * z.S
    place = lax.broadcasted_iota(jnp.int32, (z.S, LANES), 0)
    at = base + (place % CHUNKS) * z.L + place // CHUNKS
    chunk_at = base + z.L * lax.broadcasted_iota(jnp.int32, (CHUNKS, LANES), 0)
    dev_at = z.S * lax.broadcasted_iota(jnp.int32, (z.tm, LANES), 0)
    for r in range(z.R):
        end = jnp.int32(0)
        hit = [jnp.zeros(a.shape, jnp.bool_) for a in (at, at, chunk_at, chunk_at, dev_at, dev_at)]
        for q in range(z.seqs):
            start = end
            end = end + len_ref[r, q]
            last = end - 1
            hit[0] = hit[0] | (at == start)
            hit[1] = hit[1] | (at == last)
            for i, mark in ((2, start), (3, last)):
                hit[i] = hit[i] | ((chunk_at <= mark) & (mark < chunk_at + z.L))
            for i, mark in ((4, start), (5, last)):
                hit[i] = hit[i] | ((dev_at <= mark) & (mark < dev_at + z.S))
        keep = [1.0 - h.astype(F32) for h in hit]
        keep_f[r * z.S : (r + 1) * z.S, :] = keep[0]
        keep_r[r * z.S : (r + 1) * z.S, :] = keep[1]
        chunk_f[r * CHUNKS : (r + 1) * CHUNKS, :] = keep[2]
        chunk_r[r * CHUNKS : (r + 1) * CHUNKS, :] = keep[3]
        each = 2 * z.half
        for j in range(z.tm):
            for ref, k in ((dev_f, keep[4]), (dev_r, keep[5])):
                ref[j, r * each : (r + 1) * each, :] = jnp.broadcast_to(k[j : j + 1, :], (each, LANES))
    for b in range(2):
        rate, angle = rate_ref[b : b + 1, :], phase_ref[b : b + 1, :]
        size = jnp.exp(-rate)
        lr, li = size * jnp.cos(angle), size * jnp.sin(angle)
        gamma = jnp.sqrt(1.0 - jnp.exp(-2.0 * rate))

        def power(n):
            out, br, bi = None, lr, li
            while n:
                if n & 1:
                    out = (br, bi) if out is None else (out[0] * br - out[1] * bi, out[0] * bi + out[1] * br)
                br, bi = br * br - bi * bi, 2.0 * br * bi
                n >>= 1
            return out

        chunk_power, device_power = power(z.L), power(z.S)
        rows = [lr, li, gamma, chunk_power[0], chunk_power[1], jnp.exp(-2.0 * rate) / gamma]
        for i, row in enumerate(rows):
            tab_ref[b * 8 + i : b * 8 + i + 1, :] = row
        for i in range(6, 8):
            tab_ref[b * 8 + i : b * 8 + i + 1, :] = jnp.zeros_like(lr)
        pack(power_ref.at[2 * b], [device_power[0], device_power[0]] * z.R)
        pack(power_ref.at[2 * b + 1], [-device_power[1], device_power[1]] * z.R)
    for c in copies[5:]:
        c.wait()


def enter(z, b, stat_ref, v_ref, gain_ref, bias_ref, win_ref, keep_ref, chunk_ref, tab_ref,
          norm_ref, low_ref, proj_ref, ends_ref, send_ref, stat_tile, tile_ref):
    total, square = two_sums(stat_ref, stat_tile, z)
    mean = total / z.tokens
    rstd = lax.rsqrt(square / z.tokens - mean * mean + EPS)
    norm_ref[0:1, :] = mean
    norm_ref[1:2, :] = rstd
    gain, bias = gain_ref[b : b + 1, :], bias_ref[b : b + 1, :]

    def body(rows, c):
        xhat = (v_ref[rows, :] - mean) * rstd
        low_ref[rows, :] = (gain * xhat + bias).astype(BF16)
        return c

    tiles(z, body, 0)
    proj_ref[...] = dot(low_ref[...], win_ref[b])
    lr, li, gamma, pr, pi = lam_rows(z, tab_ref, b)
    state = scan(z, proj_ref, gamma, lr, li, keep_ref, zeros_state(z), b == 1)
    pack(tile_ref, end_state(z, state, ends_ref, chunk_ref, pr, pi, b == 1))
    spread(send_ref, tile_ref)


def gelu_pair(y):
    cdf = 0.5 + 0.5 * lax.erf(y * ROOT_HALF)
    return y * cdf, cdf + y * (ROOT_TWO_PI_INV * jnp.exp(-0.5 * y * y))


def mix(z, b, recv_ref, dev_ref, power_ref, ends_ref, chunk_ref, proj_ref, keep_ref, tab_ref, v_ref, norm_ref, gain_ref,
        bias_ref, skip_ref, wout_ref, wglu_ref, h_ref, hlow_ref, carry_ref, slope_ref, act_ref, tile_ref, wide_ref):
    lr, li, gamma, pr, pi = lam_rows(z, tab_ref, b)
    state = carries(z, recv_ref, dev_ref, power_ref, b, 1.0, ends_ref, chunk_ref, pr, pi, tile_ref, carry_ref, b == 1)

    put = pair_store(z, hlow_ref)

    def visit(r, s, rows, hr, hi):
        h_ref[rows, 0 : z.N] = hr
        h_ref[rows, z.N : 2 * z.N] = hi
        put(r, s, hr, hi)

    scan(z, proj_ref, gamma, lr, li, keep_ref, state, b == 1, visit)
    slope_ref[...] = dot(hlow_ref[...], wout_ref[b])
    mean, rstd = norm_ref[0:1, :], norm_ref[1:2, :]
    gain, bias, skip = gain_ref[b : b + 1, :], bias_ref[b : b + 1, :], skip_ref[b : b + 1, :]

    def body(rows, c):
        xn = gain * ((v_ref[rows, :] - mean) * rstd) + bias
        act, slope = gelu_pair(slope_ref[rows, :] + skip * xn)
        act_ref[rows, :] = act.astype(BF16)
        slope_ref[rows, :] = slope
        return c

    tiles(z, body, 0)
    wide_ref[...] = dot(act_ref[...], wglu_ref[b])


def middle(z, recv_ref, dev_ref, power_ref, ends_ref, chunk_ref, proj_ref, keep_ref, tab_ref, v_ref, norm_ref, gain_ref,
           bias_ref, skip_ref, wout_ref, wglu_ref, bglu_ref,
           h_ref, hlow_ref, carry_ref, slope_ref, act_ref, sig_ref, gate_ref, next_ref, stat_ref, tile_ref, wide_ref, stat_tile):
    mix(z, 0, recv_ref, dev_ref, power_ref, ends_ref, chunk_ref, proj_ref, keep_ref, tab_ref, v_ref, norm_ref, gain_ref,
        bias_ref, skip_ref, wout_ref, wglu_ref, h_ref, hlow_ref, carry_ref, slope_ref, act_ref, tile_ref, wide_ref)
    d = z.D
    b1, b2 = bglu_ref[0:1, 0:d], bglu_ref[0:1, d : 2 * d]

    def body(rows, c):
        z1 = wide_ref[rows, 0:d] + b1
        sig = jax.nn.sigmoid(wide_ref[rows, d : 2 * d] + b2)
        prod = z1 * sig
        sig_ref[rows, :] = sig
        gate_ref[rows, :] = prod * (1.0 - sig)
        v = v_ref[rows, :] + prod
        next_ref[rows, :] = v
        return c[0] + fold(v), c[1] + fold(v * v)

    zero = jnp.zeros((8, d), F32)
    s0, s1 = tiles(z, body, (zero, zero))
    pack(stat_tile, [jnp.sum(s0, 0, keepdims=True), jnp.sum(s1, 0, keepdims=True)])
    spread(stat_ref, stat_tile)


def descend(z, b, grad_bglu, dz_ref, slope_ref, v_ref, norm_ref, gain_ref, bias_ref, wglu_ref, wout_ref, keep_ref, chunk_ref, tab_ref,
            dy_ref, dylow_ref, dh_ref, ends_ref, send_ref, small_ref, tile_ref):
    dy_ref[...] = dot_t(dz_ref[...], wglu_ref[b])
    mean, rstd = norm_ref[0:1, :], norm_ref[1:2, :]
    gain, bias = gain_ref[b : b + 1, :], bias_ref[b : b + 1, :]

    def body(rows, c):
        xn = gain * ((v_ref[rows, :] - mean) * rstd) + bias
        dy = dy_ref[rows, :] * slope_ref[rows, :]
        dy_ref[rows, :] = dy
        dylow_ref[rows, :] = dy.astype(BF16)
        return c + fold(dy * xn)

    grad_skip = tiles(z, body, jnp.zeros((8, z.D), F32))
    small_ref[0:1, :] = jnp.sum(grad_skip, 0, keepdims=True)
    total = jnp.sum(grad_bglu, 0, keepdims=True)
    small_ref[1:2, :] = total[:, 0 : z.D]
    small_ref[2:3, :] = total[:, z.D : 2 * z.D]
    dh_ref[...] = dot_t(dylow_ref[...], wout_ref[b])
    lr, li, _, pr, pi = lam_rows(z, tab_ref, b)
    state = scan(z, dh_ref, None, lr, -li, keep_ref, zeros_state(z), b == 0)
    pack(tile_ref, end_state(z, state, ends_ref, chunk_ref, pr, -pi, b == 0))
    spread(send_ref, tile_ref)


def turn(z, recv_ref, dev_ref, power_ref, ends_ref, chunk_ref, proj_ref, keep_ref, tab_ref, v_ref, norm_ref, gain_ref,
         bias_ref, skip_ref, wout_ref, wglu_ref, bglu_ref, gout_ref, adj_keep_ref, adj_chunk_ref,
         h_ref, hlow_ref, carry_ref, act_ref, out_ref, dz_ref, dy_ref, dylow_ref, dh_ref, adj_ends_ref, send_ref, small_ref,
         tile_ref, wide_ref, slope_ref, natural_ref):
    mix(z, 1, recv_ref, dev_ref, power_ref, ends_ref, chunk_ref, proj_ref, keep_ref, tab_ref, v_ref, norm_ref, gain_ref,
        bias_ref, skip_ref, wout_ref, wglu_ref, h_ref, hlow_ref, carry_ref, slope_ref, act_ref, tile_ref, wide_ref)
    d = z.D
    b1, b2 = bglu_ref[1:2, 0:d], bglu_ref[1:2, d : 2 * d]

    def body(rows, c):
        z1 = wide_ref[rows, 0:d] + b1
        sig = jax.nn.sigmoid(wide_ref[rows, d : 2 * d] + b2)
        prod = z1 * sig
        dy_ref[rows, :] = v_ref[rows, :] + prod
        e = gout_ref[rows, :]
        d1, d2 = e * sig, e * (prod * (1.0 - sig))
        dz_ref[rows, 0:d] = d1.astype(BF16)
        dz_ref[rows, d : 2 * d] = d2.astype(BF16)
        return c[0] + fold(d1), c[1] + fold(d2)

    zero = jnp.zeros((8, d), F32)
    s0, s1 = tiles(z, body, (zero, zero))
    to_time(z, dy_ref, out_ref, natural_ref)
    descend(z, 1, jnp.concatenate([s0, s1], axis=1), dz_ref, slope_ref, v_ref, norm_ref, gain_ref, bias_ref, wglu_ref, wout_ref,
            adj_keep_ref, adj_chunk_ref, tab_ref, dy_ref, dylow_ref, dh_ref, adj_ends_ref, send_ref, small_ref, tile_ref)


def finish(z, b, recv_ref, dev_ref, power_ref, ends_ref, chunk_ref, dh_ref, keep_ref, tab_ref, proj_ref, h_ref, carry_ref,
           fwd_keep_ref, dy_ref, v_ref, norm_ref, skip_ref, win_ref, emit,
           dplow_ref, dxn_ref, lam_ref, tile_ref, adj_carry_ref):
    lr, li, gamma, pr, pi = lam_rows(z, tab_ref, b)
    reverse = b == 0
    state = carries(z, recv_ref, dev_ref, power_ref, b, -1.0, ends_ref, chunk_ref, pr, -pi, tile_ref, adj_carry_ref, reverse)
    zero = jnp.zeros((CHUNKS, z.N), F32)
    sums = [zero, zero, zero]
    put = pair_store(z, dplow_ref)

    def visit(r, s, rows, gr, gi):
        put(r, s, gamma * gr, gamma * gi)
        sums[2] = sums[2] + gr * proj_ref[rows, 0 : z.N] + gi * proj_ref[rows, z.N : 2 * z.N]
        if s == (0 if b == 0 else z.L - 1):
            span = slice(r * CHUNKS, (r + 1) * CHUNKS)
            nr, ni = carry_ref[span, 0 : z.N], carry_ref[span, z.N : 2 * z.N]
        else:
            near = step_rows(z, r, s - 1 if b == 0 else s + 1)
            nr, ni = h_ref[near, 0 : z.N], h_ref[near, z.N : 2 * z.N]
        keep = wide(fwd_keep_ref[rows, :], z)
        nr, ni = keep * nr, keep * ni
        sums[0] = sums[0] + (gr * nr + gi * ni)
        sums[1] = sums[1] + (gi * nr - gr * ni)

    scan(z, dh_ref, None, lr, -li, keep_ref, state, reverse, visit)
    dr, di, dg = (jnp.sum(s, 0, keepdims=True) for s in sums)
    r0, i0 = lr[0:1, :], li[0:1, :]
    lam_ref[0:1, :] = dg * tab_ref[b * 8 + 5 : b * 8 + 6, :] - (dr * r0 + di * i0)
    lam_ref[1:2, :] = di * r0 - dr * i0

    dxn_ref[...] = dot_t(dplow_ref[...], win_ref[b])
    mean, rstd = norm_ref[0:1, :], norm_ref[1:2, :]
    skip = skip_ref[b : b + 1, :]

    def body(rows, c):
        xhat = (v_ref[rows, :] - mean) * rstd
        dxn = dxn_ref[rows, :] + skip * dy_ref[rows, :]
        dxn_ref[rows, :] = dxn
        return c[0] + fold(dxn), c[1] + fold(dxn * xhat)

    zero = jnp.zeros((8, z.D), F32)
    s0, s1 = tiles(z, body, (zero, zero))
    emit(jnp.sum(s0, 0, keepdims=True), jnp.sum(s1, 0, keepdims=True))


def norm_grad(z, b, bias_sum, gain_sum, norm_ref, gain_ref):
    mean, rstd = norm_ref[0:1, :], norm_ref[1:2, :]
    gain = gain_ref[b : b + 1, :]
    scale, shift, slope = rstd * gain, rstd * gain * bias_sum / z.tokens, rstd * gain * gain_sum / z.tokens

    def grad(dxn, v, up):
        return scale * dxn - shift - ((v - mean) * rstd) * slope + up

    return grad


def lower_block(z, stat_ref, dxn_ref, v1_ref, norm1_ref, gout_ref, sig_ref, gate_ref, slope_ref, v_ref, norm_ref, gain_ref, bias_ref,
                wglu_ref, wout_ref, keep_ref, chunk_ref, tab_ref, act_ref, hlow_ref,
                total_ref, e_ref, dy_ref, dylow_ref, dh_ref, ends_ref, send_ref, small_ref, half_keep, half_send, tile_ref, stat_tile, dz_ref):
    bias_sum, gain_sum = two_sums(stat_ref, stat_tile, z)
    grad = norm_grad(z, 1, bias_sum, gain_sum, norm1_ref, gain_ref)
    total_ref[0:1, :] = bias_sum
    total_ref[1:2, :] = gain_sum
    d = z.D

    def body(rows, c):
        e = grad(dxn_ref[rows, :], v1_ref[rows, :], gout_ref[rows, :])
        e_ref[rows, :] = e
        d1, d2 = e * sig_ref[rows, :], e * gate_ref[rows, :]
        dz_ref[rows, 0:d] = d1.astype(BF16)
        dz_ref[rows, d : 2 * d] = d2.astype(BF16)
        return c[0] + fold(d1), c[1] + fold(d2)

    zero = jnp.zeros((8, d), F32)
    s0, s1 = tiles(z, body, (zero, zero))
    descend(z, 0, jnp.concatenate([s0, s1], axis=1), dz_ref, slope_ref, v_ref, norm_ref, gain_ref, bias_ref, wglu_ref, wout_ref,
            keep_ref, chunk_ref, tab_ref, dy_ref, dylow_ref, dh_ref, ends_ref, send_ref, small_ref, tile_ref)
    glu, out = units(act_ref, dz_ref, half_keep), units(hlow_ref, dylow_ref, half_keep)
    cut = (len(glu) + len(out)) // 2
    first_split(z, half_keep, half_send, glu[:cut], glu[cut:] + out)


def units(a_ref, b_ref, like):
    w = like.shape[1]

    def strip(i):
        return lambda: dot_0(a_ref[...], b_ref[:, i * w : (i + 1) * w])

    return [strip(i) for i in range(b_ref.shape[1] // w)]


def finish_upper(z, *refs):
    ins, (act_ref, dz_ref, hlow_ref, dylow_ref, low_ref), outs = refs[:17], refs[17:22], refs[22:]
    dxn_ref, stat_ref, lam_ref, keep_ref, send_ref, dplow_ref, tile_ref, carry_ref, stat_tile = outs

    def emit(bias_sum, gain_sum):
        pack(stat_tile, [bias_sum, gain_sum])
        spread(stat_ref, stat_tile)

    finish(z, 1, *ins, emit, dplow_ref, dxn_ref, lam_ref, tile_ref, carry_ref)
    first_split(z, keep_ref, send_ref, units(act_ref, dz_ref, keep_ref),
                units(hlow_ref, dylow_ref, keep_ref) + units(low_ref, dplow_ref, keep_ref))


def finish_lower(z, *refs):
    ins, (low_ref, small0_ref, small1_ref, lam1_ref), outs = refs[:17], refs[17:21], refs[21:]
    dxn_ref, keep_ref, send_ref, dplow_ref, lam_ref, tile_ref, carry_ref = outs
    first = keep_ref.shape[0] - z.extra

    def emit(bias_sum, gain_sum):
        sums = [bias_sum, gain_sum]
        for small, lam in ((small0_ref, lam_ref), (small1_ref, lam1_ref)):
            sums += [small[0:1, :], small[1:2, :], small[2:3, :], lam[0:1, :], lam[1:2, :]]
        for ref in (keep_ref, send_ref):
            k = pack(ref, sums, first)
            if k < ref.shape[0]:
                ref[k:, :] = jnp.zeros((ref.shape[0] - k, ref.shape[1]), F32)

    finish(z, 0, *ins, emit, dplow_ref, dxn_ref, lam_ref, tile_ref, carry_ref)
    strips = units(low_ref, dplow_ref, keep_ref)
    first_split(z, keep_ref, send_ref, strips[: len(strips) // 2], strips[len(strips) // 2 :])


def last(z, small_ref, dxn_ref, v_ref, norm_ref, gain_ref, e_ref, total1_ref, grad_ref, gain_out, bias_out, rate_out, phase_out, skip_out,
         bglu_out, natural_ref, work_ref):
    w = small_ref.shape[1]
    at = [0]

    def take(width):
        row = unpack(small_ref, at[0], width // w)
        at[0] += width // w
        return row

    bias_sum, gain_sum = take(z.D), take(z.D)
    grad = norm_grad(z, 0, bias_sum, gain_sum, norm_ref, gain_ref)
    bias_out[0:1, :] = bias_sum
    gain_out[0:1, :] = gain_sum
    bias_out[1:2, :] = total1_ref[0:1, :]
    gain_out[1:2, :] = total1_ref[1:2, :]
    for b in range(2):
        for ref, width in ((skip_out, z.D), (bglu_out, 2 * z.D), (rate_out, z.N), (phase_out, z.N)):
            ref[b : b + 1, :] = take(width)

    def body(rows, c):
        work_ref[rows, :] = grad(dxn_ref[rows, :], v_ref[rows, :], e_ref[rows, :])
        return c

    tiles(z, body, 0)
    to_time(z, work_ref, grad_ref, natural_ref)


GRAD_TILE = 64
STRIP = 256


def own_bit(z, step):
    me = lax.axis_index("tm") * z.rows + lax.axis_index("rows")
    if step in (1, 2) and z.bits > 2:
        odd = me % 2
        bit = odd + 2 * (1 - odd) if step == 1 else 2 * odd + (1 - odd)
        return (me >> bit) % 2
    return (me >> step) % 2


def pairs(z, step):
    out = []
    for i in range(z.all):
        bit = step
        if step in (1, 2) and z.bits > 2:
            bit = (1 if i % 2 else 2) if step == 1 else (2 if i % 2 else 1)
        out.append((i, i ^ (1 << bit)))
    return out


def first_split(z, keep_ref, send_ref, low, high):
    bit = own_bit(z, 0)
    n = z.D

    def write(ref, products):
        for i, product in enumerate(products):
            ref[i * n : (i + 1) * n, :] = product()

    @pl.when(bit == 0)
    def _():
        write(keep_ref, low)
        write(send_ref, high)

    @pl.when(bit == 1)
    def _():
        write(keep_ref, high)
        write(send_ref, low)


def strips_of(n):
    size = math.gcd(GRAD_TILE, n)

    def rows(part, i):
        return pl.ds(pl.multiple_of(part * n + i * size, math.gcd(size, 8)), size)

    return n // size, rows


def halves(z, step, extra, keep_ref, recv_ref, next_ref, send_ref):
    n = next_ref.shape[0] - extra
    bit = own_bit(z, step)
    count, rows = strips_of(n)

    def one(i, c):
        for ref, part in ((send_ref, 1 - bit), (next_ref, bit)):
            ref[rows(0, i), :] = keep_ref[rows(part, i), :] + recv_ref[rows(part, i), :]
        return c

    lax.fori_loop(0, count, one, 0)
    if extra:
        both = keep_ref[2 * n :, :] + recv_ref[2 * n :, :]
        next_ref[n:, :] = both
        send_ref[n:, :] = both


def total(extra, keep_ref, recv_ref, out_ref, *extra_ref):
    n = out_ref.shape[0]
    out_ref[...] = keep_ref[0:n, :] + recv_ref[0:n, :]
    if extra:
        extra_ref[0][...] = keep_ref[n:, :] + recv_ref[n:, :]


def join(z, step, own_ref, recv_ref, out_ref):
    n = own_ref.shape[0]
    bit = own_bit(z, step)
    count, rows = strips_of(n)

    def one(i, c):
        for ref, part in ((own_ref, bit), (recv_ref, 1 - bit)):
            out_ref[rows(part, i), :] = ref[rows(0, i), :]
        return c

    lax.fori_loop(0, count, one, 0)


class Exchange:
    def __init__(self, z, keep, send, extra=0):
        self.z, self.keep, self.send, self.extra = z, keep, send, extra
        self.step, self.up, self.small = 0, False, None
        self.width = keep.shape[1]

    def go(self):
        self.got = lax.ppermute(self.send, ("tm", "rows"), pairs(self.z, self.step))

    def settle(self):
        z, x = self.z, self.extra
        n = self.keep.shape[0]
        if self.up:
            (self.keep,) = run(functools.partial(join, z, self.step), "join", [((2 * n, self.width), F32)], (self.keep, self.got))
            self.send = self.keep
            self.step -= 1
            return
        n -= x
        self.step += 1
        if self.step < z.bits:
            half = ((n // 2 + x, self.width), F32)
            self.keep, self.send = run(functools.partial(halves, z, self.step, x), "halves", [half, half], (self.keep, self.got))
            return
        outs = [((n, self.width), F32)] + ([((x, self.width), F32)] if x else [])
        self.keep, *self.small = run(functools.partial(total, x), "total", outs, (self.keep, self.got))
        self.send, self.up = self.keep, True
        self.step = z.bits - 1

    @property
    def closing(self):
        return self.up and self.step == 0


def assemble(z, own1, got1, owna, gota, ownb, gotb, win_out, wout_out, wglu_out, sem):
    bit = own_bit(z, 0)
    w = own1.shape[1]

    def strips(out, b):
        return [out.at[b, :, i * w : (i + 1) * w] for i in range(out.shape[2] // w)]

    places = [strips(wglu_out, 1) + strips(wout_out, 1) + strips(win_out, 1), strips(wglu_out, 0) + strips(wout_out, 0), strips(win_out, 0)]

    def place(halves_of):
        copies = []
        for (low, high), outs in zip(halves_of, places):
            cut = len(outs) // 2
            for ref, part in ((low, outs[:cut]), (high, outs[cut:])):
                for i, out in enumerate(part):
                    copies.append(pltpu.make_async_copy(ref.at[i * z.D : (i + 1) * z.D, :], out, sem.at[len(copies)]))
        for c in copies:
            c.start()
        for c in copies:
            c.wait()

    @pl.when(bit == 0)
    def _():
        place([(own1, got1), (owna, gota), (ownb, gotb)])

    @pl.when(bit == 1)
    def _():
        place([(got1, own1), (gota, owna), (gotb, ownb)])


def run(kernel, name, outs, args, scratch=(), sems=0, source=pltpu.VMEM, target=pltpu.VMEM):
    if source is pltpu.HBM:
        args = [pltpu.with_memory_space_constraint(a, source) for a in args]
    shapes = [pltpu.VMEM(s, t) if t != jnp.int32 else pltpu.SMEM(s, t) for s, t in scratch]
    return pl.pallas_call(
        kernel,
        out_shape=[jax.ShapeDtypeStruct(s, t) for s, t in outs],
        in_specs=[pl.BlockSpec(memory_space=source)] * len(args),
        out_specs=[pl.BlockSpec(memory_space=target)] * len(outs),
        scratch_shapes=shapes + ([pltpu.SemaphoreType.DMA((sems,))] if sems else []),
        compiler_params=pltpu.CompilerParams(vmem_limit_bytes=16 << 20),
        name=name,
    )(*args)


def body(x_in, lengths, bn_gain, bn_bias, w_in, decay_rate, phase, w_out, skip_gain, w_glu, b_glu, grad_out):
    rows, steps, width = x_in.shape
    z = Sizes(rows, steps, width, w_in.shape[2] // 2, lax.axis_size("tm"), lax.axis_size("rows"), lengths.shape[1])
    T, D, N = z.T, z.D, z.N
    everyone = ("tm", "rows")

    def swap(a, axis):
        return lax.all_to_all(a, axis, 0, 0)

    stat_shape = ((z.all, z.stat, LANES), F32)
    send_shape = ((z.tm, z.packed, LANES), F32)
    tile = ((z.packed, LANES), F32)
    stat_tile = ((z.stat, LANES), F32)
    full, low = ((T, D), F32), ((T, D), BF16)
    full_n, low_n = ((T, 2 * N), F32), ((T, 2 * N), BF16)
    chunk = ((z.R * CHUNKS, 2 * N), F32)
    mask = ((T, LANES), F32)
    chunk_mask = ((z.R * CHUNKS, LANES), F32)
    norm_shape = ((8, D), F32)
    small_shape = ((8, D), F32)
    lam_shape = ((8, N), F32)
    wide_f, wide_b = ((T, 2 * D), F32), ((T, 2 * D), BF16)
    bind = functools.partial

    natural = ((D // LANES, T, LANES), F32)
    (x, gout, stat0, keep_f, keep_r, chunk_f, chunk_r, dev_f, dev_r, tab, power,
     bn_gain, bn_bias, skip_gain, b_glu, w_in, w_out, w_glu) = run(
        bind(prepare, z), "prepare",
        [full, full, stat_shape, mask, mask, chunk_mask, chunk_mask, send_shape, send_shape, ((16, N), F32), ((4, z.packed, LANES), F32)]
        + [(a.shape, a.dtype) for a in (bn_gain, bn_bias, skip_gain, b_glu, w_in, w_out, w_glu)],
        (lengths, x_in.reshape(T, D), grad_out.reshape(T, D), decay_rate, phase, bn_gain, bn_bias, skip_gain, b_glu, w_in, w_out, w_glu),
        [stat_tile, natural, low, low, ((2, N), F32), ((2, N), F32), (lengths.shape, jnp.int32)], sems=12, source=pltpu.HBM)
    stat0 = swap(stat0, everyone)
    norm0, low0, proj0, ends0, send0 = run(
        bind(enter, z, 0), "enter0", [norm_shape, low, full_n, chunk, send_shape],
        (stat0, x, bn_gain, bn_bias, w_in, keep_f, chunk_f, tab), [stat_tile, tile])
    send0 = swap(send0, "tm")
    h0, hlow0, carry0, slope0, act0, sig0, gate0, v1, stat1 = run(
        bind(middle, z), "middle", [full_n, low_n, chunk, full, low, full, full, full, stat_shape],
        (send0, dev_f, power, ends0, chunk_f, proj0, keep_f, tab, x, norm0, bn_gain, bn_bias, skip_gain, w_out, w_glu, b_glu),
        [tile, wide_f, stat_tile])
    stat1 = swap(stat1, everyone)
    norm1, low1, proj1, ends1, send1 = run(
        bind(enter, z, 1), "enter1", [norm_shape, low, full_n, chunk, send_shape],
        (stat1, v1, bn_gain, bn_bias, w_in, keep_r, chunk_r, tab), [stat_tile, tile])
    send1 = swap(send1, "tm")
    h1, hlow1, carry1, act1, out, dz1, dy1, dylow1, dh1, adj_ends1, adj1, small1 = run(
        bind(turn, z), "turn",
        [full_n, low_n, chunk, low, low, wide_b, full, low, full_n, chunk, send_shape, small_shape],
        (send1, dev_r, power, ends1, chunk_r, proj1, keep_r, tab, v1, norm1, bn_gain, bn_bias, skip_gain, w_out, w_glu, b_glu, gout,
         keep_f, chunk_f), [tile, wide_f, full, natural])
    adj1 = swap(adj1, "tm")
    W = STRIP if D * D // STRIP % (8 * z.all) == 0 else LANES

    def part(count):
        return ((count * D // W * D // 2, W), F32)

    dxn1, sum1, lam1, keep1, send1 = run(
        bind(finish_upper, z), "finish1", [full, stat_shape, lam_shape, part(4), part(4)],
        (adj1, dev_f, power, adj_ends1, chunk_f, dh1, keep_f, tab, proj1, h1, carry1, keep_r, dy1, v1, norm1, skip_gain, w_in,
         act1, dz1, hlow1, dylow1, low1),
        [low_n, tile, chunk, stat_tile])
    one = Exchange(z, keep1, send1)
    one.go()
    sum1 = swap(sum1, everyone)
    one.got, sum1 = lax.optimization_barrier((one.got, sum1))
    one.settle()
    total1, e1, dy0, dylow0, dh0, adj_ends0, adj0, small0, keepa, senda = run(
        bind(lower_block, z), "lower_block",
        [norm_shape, full, full, low, full_n, chunk, send_shape, small_shape, part(3), part(3)],
        (sum1, dxn1, v1, norm1, gout, sig0, gate0, slope0, x, norm0, bn_gain, bn_bias, w_glu, w_out, keep_r, chunk_r, tab, act0, hlow0),
        [tile, stat_tile, wide_b])
    two = Exchange(z, keepa, senda)
    one.send, two.send, adj0 = lax.optimization_barrier((one.send, two.send, adj0))
    one.go()
    two.go()
    adj0 = swap(adj0, "tm")
    one.got, two.got, adj0 = lax.optimization_barrier((one.got, two.got, adj0))
    rows_sum = (2 * D + 2 * (3 * D + 2 * N)) // W
    z.extra = -(-rows_sum // 8) * 8
    last_part = ((D // W * D // 2 + z.extra, W), F32)
    dxn0, keepb, sendb = run(
        bind(finish_lower, z), "finish0", [full, last_part, last_part],
        (adj0, dev_r, power, adj_ends0, chunk_r, dh0, keep_r, tab, proj0, h0, carry0, keep_f, dy0, x, norm0, skip_gain, w_in,
         low0, small0, small1, lam1),
        [low_n, lam_shape, tile, chunk])
    one.settle()
    two.settle()
    three = Exchange(z, keepb, sendb, z.extra)
    one.send, two.send, three.send = lax.optimization_barrier((one.send, two.send, three.send))
    for e in (one, two, three):
        e.go()
    sets = [one, two, three]
    ahead = three.send
    while not all(e.closing for e in sets):
        for e in sets:
            if not e.closing:
                e.got, _ = lax.optimization_barrier((e.got, ahead))
                e.settle()
                e.go()
                ahead = e.send
    sums = (((2, D), F32), ((2, D), F32), ((2, N), F32), ((2, N), F32), ((2, D), F32), ((2, 2 * D), F32))
    grad_x, gain_out, bias_out, rate_out, phase_out, skip_out, bglu_out = run(
        bind(last, z), "last", [full, *sums], (three.small[0], dxn0, x, norm0, bn_gain, e1, total1), [natural, full])
    gwin, gwout, gwglu = run(
        bind(assemble, z), "assemble", [((2, D, 2 * N), F32), ((2, 2 * N, D), F32), ((2, D, 2 * D), F32)],
        (one.keep, one.got, two.keep, two.got, three.keep, three.got), sems=16, target=pltpu.HBM)
    return (
        out.reshape(rows, steps, width),
        grad_x.reshape(rows, steps, width),
        gain_out,
        bias_out,
        gwin,
        rate_out,
        phase_out,
        gwout,
        skip_out,
        gwglu,
        bglu_out,
    )


def solution(mesh):
    split, rep = P("rows", "tm", None), P()
    return jax.shard_map(
        body,
        mesh=mesh,
        in_specs=(split, P("rows", None)) + (rep,) * 9 + (split,),
        out_specs=(split, split) + (rep,) * 9,
        check_vma=False,
    )
```

```python
import functools
import math

import jax
import jax.numpy as jnp
from jax import lax
from jax.experimental import pallas as pl
from jax.experimental.pallas import tpu as pltpu
from jax.sharding import PartitionSpec as P

EPS = 1e-05
LANES = 128
CHUNKS = 8
TILE = 32
F32 = jnp.float32
BF16 = jnp.bfloat16
ROOT_HALF = 0.7071067811865476
ROOT_TWO_PI_INV = 0.3989422804014327


class Sizes:
    def __init__(self, rows, steps, width, states, count_tm, count_rows, per_row):
        self.R, self.S, self.D, self.N = rows, steps, width, states
        self.T = rows * steps
        self.L = steps // CHUNKS
        self.tm, self.rows = count_tm, count_rows
        self.all = count_tm * count_rows
        self.seqs = per_row
        self.half = states // LANES
        self.packed = rows * 2 * self.half
        self.stat = 2 * width // LANES
        self.tokens = self.T * self.all
        self.bits = self.all.bit_length() - 1
        self.extra = 0


def dot(a, b):
    return jnp.dot(a, b, preferred_element_type=F32)


def dot_t(a, b):
    return lax.dot_general(a, b, (((1,), (1,)), ((), ())), preferred_element_type=F32)


def dot_0(a, b):
    return lax.dot_general(a, b, (((0,), (0,)), ((), ())), preferred_element_type=F32)


def fold(a):
    return a.reshape(a.shape[0] // 8, 8, a.shape[1]).sum(0)


def wide(a, z):
    return jnp.concatenate([a] * z.half, axis=1)


def tiles(z, body, carry):
    def one(i, c):
        return body(pl.ds(pl.multiple_of(i * TILE, TILE), TILE), c)

    return lax.fori_loop(0, z.T // TILE, one, carry)


def pack(ref, rows, k=0):
    w = ref.shape[1]
    for row in rows:
        for i in range(row.shape[1] // w):
            ref[k : k + 1, :] = row[:, i * w : (i + 1) * w]
            k += 1
    return k


def unpack(ref, first, count):
    return jnp.concatenate([ref[first + i : first + i + 1, :] for i in range(count)], axis=1)


def spread(out_ref, tile_ref):
    value = tile_ref[...]
    for j in range(out_ref.shape[0]):
        out_ref[j] = value


def two_sums(recv_ref, tile_ref, z):
    tile_ref[...] = jnp.sum(recv_ref[...], axis=0)
    n = z.D // LANES
    return unpack(tile_ref, 0, n), unpack(tile_ref, n, n)


def step_rows(z, r, s):
    first = r * z.S + s * CHUNKS
    return slice(first, first + CHUNKS)


def to_steps(z, source, out_ref, natural_ref):
    lanes = z.D // LANES

    def split(rows, c):
        value = source(rows)
        for k in range(lanes):
            natural_ref[k, rows, :] = value[:, k * LANES : (k + 1) * LANES]
        return c

    tiles(z, split, 0)
    for r in range(z.R):
        for s in range(z.L):
            for k in range(lanes):
                out_ref[step_rows(z, r, s), k * LANES : (k + 1) * LANES] = natural_ref[k, pl.ds(r * z.S + s, CHUNKS, stride=z.L), :]


def to_time(z, source_ref, out_ref, natural_ref):
    lanes = z.D // LANES
    for r in range(z.R):
        for s in range(z.L):
            for k in range(lanes):
                natural_ref[k, pl.ds(r * z.S + s, CHUNKS, stride=z.L), :] = source_ref[step_rows(z, r, s), k * LANES : (k + 1) * LANES]

    def join(rows, c):
        value = jnp.concatenate([natural_ref[k, rows, :] for k in range(lanes)], axis=1)
        out_ref[rows, :] = value.astype(out_ref.dtype)
        return c

    tiles(z, join, 0)


def pair_store(z, ref):
    held = {}

    def put(r, s, re, im):
        if (r, s ^ 1) not in held:
            held[r, s] = (re, im)
            return
        other = held.pop((r, s ^ 1))
        low, high = (other, (re, im)) if s & 1 else ((re, im), other)
        rows = slice(r * z.S + (s & ~1) * CHUNKS, r * z.S + ((s & ~1) + 2) * CHUNKS)
        ref[rows, 0 : z.N] = jnp.concatenate([low[0], high[0]], axis=0).astype(ref.dtype)
        ref[rows, z.N : 2 * z.N] = jnp.concatenate([low[1], high[1]], axis=0).astype(ref.dtype)

    return put


def scan(z, drive_ref, gain, lr, li, keep_ref, state, reverse, visit=None):
    for step in range(z.L):
        s = z.L - 1 - step if reverse else step
        for r in range(z.R):
            rows = step_rows(z, r, s)
            keep = wide(keep_ref[rows, :], z)
            ur = drive_ref[rows, 0 : z.N]
            ui = drive_ref[rows, z.N : 2 * z.N]
            if gain is not None:
                ur, ui = ur * gain, ui * gain
            hr, hi = keep * state[r][0], keep * state[r][1]
            state[r] = (lr * hr - li * hi + ur, lr * hi + li * hr + ui)
            if visit is not None:
                visit(r, s, rows, *state[r])
    return state


def zeros_state(z):
    return [(jnp.zeros((CHUNKS, z.N), F32), jnp.zeros((CHUNKS, z.N), F32)) for _ in range(z.R)]


def chunk_order(reverse):
    return range(CHUNKS - 1, -1, -1) if reverse else range(CHUNKS)


def end_state(z, state, ends_ref, chunk_keep_ref, pr, pi, reverse):
    rows = []
    for r in range(z.R):
        ends_ref[r * CHUNKS : (r + 1) * CHUNKS, 0 : z.N] = state[r][0]
        ends_ref[r * CHUNKS : (r + 1) * CHUNKS, z.N : 2 * z.N] = state[r][1]
    for r in range(z.R):
        cr = ci = None
        for c in chunk_order(reverse):
            k = r * CHUNKS + c
            er, ei = ends_ref[k : k + 1, 0 : z.N], ends_ref[k : k + 1, z.N : 2 * z.N]
            if cr is None:
                cr, ci = er, ei
            else:
                keep = wide(chunk_keep_ref[k : k + 1, :], z)
                cr, ci = keep * cr, keep * ci
                cr, ci = pr * cr - pi * ci + er, pr * ci + pi * cr + ei
        rows += [cr, ci]
    return rows


def carries(z, recv_ref, device_keep_ref, power_ref, b, sign, ends_ref, chunk_keep_ref, pr, pi, tile_ref, carry_ref, reverse):
    place = lax.axis_index("tm")
    pow_re = power_ref[2 * b]
    pow_im = sign * power_ref[2 * b + 1]
    is_re = (lax.broadcasted_iota(jnp.int32, (z.packed, LANES), 0) // z.half) % 2 == 0

    def hop(i, c):
        j = z.tm - 1 - i if reverse else i
        other = jnp.where(is_re, pltpu.roll(c, z.packed - z.half, 0), pltpu.roll(c, z.half, 0))
        return device_keep_ref[j] * (pow_re * c + pow_im * other) + recv_ref[j]

    ahead = z.tm - 1 - place if reverse else place
    tile_ref[...] = lax.fori_loop(0, ahead, hop, jnp.zeros((z.packed, LANES), F32))
    for r in range(z.R):
        cr = unpack(tile_ref, r * 2 * z.half, z.half)
        ci = unpack(tile_ref, r * 2 * z.half + z.half, z.half)
        order = list(chunk_order(reverse))
        for c in order:
            k = r * CHUNKS + c
            carry_ref[k : k + 1, 0 : z.N] = cr
            carry_ref[k : k + 1, z.N : 2 * z.N] = ci
            if c != order[-1]:
                keep = wide(chunk_keep_ref[k : k + 1, :], z)
                er, ei = ends_ref[k : k + 1, 0 : z.N], ends_ref[k : k + 1, z.N : 2 * z.N]
                cr, ci = keep * cr, keep * ci
                cr, ci = pr * cr - pi * ci + er, pr * ci + pi * cr + ei
    state = []
    for r in range(z.R):
        span = slice(r * CHUNKS, (r + 1) * CHUNKS)
        state.append((carry_ref[span, 0 : z.N], carry_ref[span, z.N : 2 * z.N]))
    return state


def lam_rows(z, tab_ref, b):
    def row(i):
        return tab_ref[b * 8 + i : b * 8 + i + 1, :]

    def full(i):
        return jnp.broadcast_to(row(i), (CHUNKS, z.N))

    return full(0), full(1), full(2), row(3), row(4)


def prepare(z, len_hbm, x_hbm, gout_hbm, rate_hbm, phase_hbm, gain_hbm, bias_hbm, skip_hbm, bglu_hbm, win_hbm, wout_hbm, wglu_hbm,
            v_ref, up_ref, stat_ref, keep_f, keep_r, chunk_f, chunk_r, dev_f, dev_r, tab_ref, power_ref,
            gain_ref, bias_ref, skip_ref, bglu_ref, win_ref, wout_ref, wglu_ref,
            tile_ref, natural_ref, x_ref, gout_ref, rate_ref, phase_ref, len_ref, sem):
    moves = [(x_hbm, x_ref), (len_hbm, len_ref), (rate_hbm, rate_ref), (phase_hbm, phase_ref), (gout_hbm, gout_ref),
             (gain_hbm, gain_ref), (bias_hbm, bias_ref), (win_hbm, win_ref), (skip_hbm, skip_ref), (bglu_hbm, bglu_ref),
             (wout_hbm, wout_ref), (wglu_hbm, wglu_ref)]
    copies = [pltpu.make_async_copy(a, b, sem.at[i]) for i, (a, b) in enumerate(moves)]
    for c in copies:
        c.start()
    copies[0].wait()
    to_steps(z, lambda rows: x_ref[rows, :].astype(F32), v_ref, natural_ref)

    def body(rows, c):
        v = v_ref[rows, :]
        return c[0] + fold(v), c[1] + fold(v * v)

    zero = jnp.zeros((8, z.D), F32)
    s0, s1 = tiles(z, body, (zero, zero))
    pack(tile_ref, [jnp.sum(s0, 0, keepdims=True), jnp.sum(s1, 0, keepdims=True)])
    spread(stat_ref, tile_ref)
    for c in copies[1:5]:
        c.wait()
    to_steps(z, lambda rows: gout_ref[rows, :].astype(F32), up_ref, natural_ref)
    base = lax.axis_index("tm") * z.S
    place = lax.broadcasted_iota(jnp.int32, (z.S, LANES), 0)
    at = base + (place % CHUNKS) * z.L + place // CHUNKS
    chunk_at = base + z.L * lax.broadcasted_iota(jnp.int32, (CHUNKS, LANES), 0)
    dev_at = z.S * lax.broadcasted_iota(jnp.int32, (z.tm, LANES), 0)
    for r in range(z.R):
        end = jnp.int32(0)
        hit = [jnp.zeros(a.shape, jnp.bool_) for a in (at, at, chunk_at, chunk_at, dev_at, dev_at)]
        for q in range(z.seqs):
            start = end
            end = end + len_ref[r, q]
            last = end - 1
            hit[0] = hit[0] | (at == start)
            hit[1] = hit[1] | (at == last)
            for i, mark in ((2, start), (3, last)):
                hit[i] = hit[i] | ((chunk_at <= mark) & (mark < chunk_at + z.L))
            for i, mark in ((4, start), (5, last)):
                hit[i] = hit[i] | ((dev_at <= mark) & (mark < dev_at + z.S))
        keep = [1.0 - h.astype(F32) for h in hit]
        keep_f[r * z.S : (r + 1) * z.S, :] = keep[0]
        keep_r[r * z.S : (r + 1) * z.S, :] = keep[1]
        chunk_f[r * CHUNKS : (r + 1) * CHUNKS, :] = keep[2]
        chunk_r[r * CHUNKS : (r + 1) * CHUNKS, :] = keep[3]
        each = 2 * z.half
        for j in range(z.tm):
            for ref, k in ((dev_f, keep[4]), (dev_r, keep[5])):
                ref[j, r * each : (r + 1) * each, :] = jnp.broadcast_to(k[j : j + 1, :], (each, LANES))
    for b in range(2):
        rate, angle = rate_ref[b : b + 1, :], phase_ref[b : b + 1, :]
        size = jnp.exp(-rate)
        lr, li = size * jnp.cos(angle), size * jnp.sin(angle)
        gamma = jnp.sqrt(1.0 - jnp.exp(-2.0 * rate))

        def power(n):
            out, br, bi = None, lr, li
            while n:
                if n & 1:
                    out = (br, bi) if out is None else (out[0] * br - out[1] * bi, out[0] * bi + out[1] * br)
                br, bi = br * br - bi * bi, 2.0 * br * bi
                n >>= 1
            return out

        chunk_power, device_power = power(z.L), power(z.S)
        rows = [lr, li, gamma, chunk_power[0], chunk_power[1], jnp.exp(-2.0 * rate) / gamma]
        for i, row in enumerate(rows):
            tab_ref[b * 8 + i : b * 8 + i + 1, :] = row
        for i in range(6, 8):
            tab_ref[b * 8 + i : b * 8 + i + 1, :] = jnp.zeros_like(lr)
        pack(power_ref.at[2 * b], [device_power[0], device_power[0]] * z.R)
        pack(power_ref.at[2 * b + 1], [-device_power[1], device_power[1]] * z.R)
    for c in copies[5:]:
        c.wait()


def enter(z, b, stat_ref, v_ref, gain_ref, bias_ref, win_ref, keep_ref, chunk_ref, tab_ref,
          norm_ref, low_ref, proj_ref, ends_ref, send_ref, stat_tile, tile_ref):
    total, square = two_sums(stat_ref, stat_tile, z)
    mean = total / z.tokens
    rstd = lax.rsqrt(square / z.tokens - mean * mean + EPS)
    norm_ref[0:1, :] = mean
    norm_ref[1:2, :] = rstd
    gain, bias = gain_ref[b : b + 1, :], bias_ref[b : b + 1, :]

    def body(rows, c):
        xhat = (v_ref[rows, :] - mean) * rstd
        low_ref[rows, :] = (gain * xhat + bias).astype(BF16)
        return c

    tiles(z, body, 0)
    proj_ref[...] = dot(low_ref[...], win_ref[b])
    lr, li, gamma, pr, pi = lam_rows(z, tab_ref, b)
    state = scan(z, proj_ref, gamma, lr, li, keep_ref, zeros_state(z), b == 1)
    pack(tile_ref, end_state(z, state, ends_ref, chunk_ref, pr, pi, b == 1))
    spread(send_ref, tile_ref)


def gelu_pair(y):
    cdf = 0.5 + 0.5 * lax.erf(y * ROOT_HALF)
    return y * cdf, cdf + y * (ROOT_TWO_PI_INV * jnp.exp(-0.5 * y * y))


def mix(z, b, recv_ref, dev_ref, power_ref, ends_ref, chunk_ref, proj_ref, keep_ref, tab_ref, v_ref, norm_ref, gain_ref,
        bias_ref, skip_ref, wout_ref, wglu_ref, h_ref, hlow_ref, carry_ref, slope_ref, act_ref, tile_ref, wide_ref):
    lr, li, gamma, pr, pi = lam_rows(z, tab_ref, b)
    state = carries(z, recv_ref, dev_ref, power_ref, b, 1.0, ends_ref, chunk_ref, pr, pi, tile_ref, carry_ref, b == 1)

    put = pair_store(z, hlow_ref)

    def visit(r, s, rows, hr, hi):
        h_ref[rows, 0 : z.N] = hr
        h_ref[rows, z.N : 2 * z.N] = hi
        put(r, s, hr, hi)

    scan(z, proj_ref, gamma, lr, li, keep_ref, state, b == 1, visit)
    slope_ref[...] = dot(hlow_ref[...], wout_ref[b])
    mean, rstd = norm_ref[0:1, :], norm_ref[1:2, :]
    gain, bias, skip = gain_ref[b : b + 1, :], bias_ref[b : b + 1, :], skip_ref[b : b + 1, :]

    def body(rows, c):
        xn = gain * ((v_ref[rows, :] - mean) * rstd) + bias
        act, slope = gelu_pair(slope_ref[rows, :] + skip * xn)
        act_ref[rows, :] = act.astype(BF16)
        slope_ref[rows, :] = slope
        return c

    tiles(z, body, 0)
    wide_ref[...] = dot(act_ref[...], wglu_ref[b])


def middle(z, recv_ref, dev_ref, power_ref, ends_ref, chunk_ref, proj_ref, keep_ref, tab_ref, v_ref, norm_ref, gain_ref,
           bias_ref, skip_ref, wout_ref, wglu_ref, bglu_ref,
           h_ref, hlow_ref, carry_ref, slope_ref, act_ref, sig_ref, gate_ref, next_ref, stat_ref, tile_ref, wide_ref, stat_tile):
    mix(z, 0, recv_ref, dev_ref, power_ref, ends_ref, chunk_ref, proj_ref, keep_ref, tab_ref, v_ref, norm_ref, gain_ref,
        bias_ref, skip_ref, wout_ref, wglu_ref, h_ref, hlow_ref, carry_ref, slope_ref, act_ref, tile_ref, wide_ref)
    d = z.D
    b1, b2 = bglu_ref[0:1, 0:d], bglu_ref[0:1, d : 2 * d]

    def body(rows, c):
        z1 = wide_ref[rows, 0:d] + b1
        sig = jax.nn.sigmoid(wide_ref[rows, d : 2 * d] + b2)
        prod = z1 * sig
        sig_ref[rows, :] = sig
        gate_ref[rows, :] = prod * (1.0 - sig)
        v = v_ref[rows, :] + prod
        next_ref[rows, :] = v
        return c[0] + fold(v), c[1] + fold(v * v)

    zero = jnp.zeros((8, d), F32)
    s0, s1 = tiles(z, body, (zero, zero))
    pack(stat_tile, [jnp.sum(s0, 0, keepdims=True), jnp.sum(s1, 0, keepdims=True)])
    spread(stat_ref, stat_tile)


def descend(z, b, grad_bglu, dz_ref, slope_ref, v_ref, norm_ref, gain_ref, bias_ref, wglu_ref, wout_ref, keep_ref, chunk_ref, tab_ref,
            dy_ref, dylow_ref, dh_ref, ends_ref, send_ref, small_ref, tile_ref):
    dy_ref[...] = dot_t(dz_ref[...], wglu_ref[b])
    mean, rstd = norm_ref[0:1, :], norm_ref[1:2, :]
    gain, bias = gain_ref[b : b + 1, :], bias_ref[b : b + 1, :]

    def body(rows, c):
        xn = gain * ((v_ref[rows, :] - mean) * rstd) + bias
        dy = dy_ref[rows, :] * slope_ref[rows, :]
        dy_ref[rows, :] = dy
        dylow_ref[rows, :] = dy.astype(BF16)
        return c + fold(dy * xn)

    grad_skip = tiles(z, body, jnp.zeros((8, z.D), F32))
    small_ref[0:1, :] = jnp.sum(grad_skip, 0, keepdims=True)
    total = jnp.sum(grad_bglu, 0, keepdims=True)
    small_ref[1:2, :] = total[:, 0 : z.D]
    small_ref[2:3, :] = total[:, z.D : 2 * z.D]
    dh_ref[...] = dot_t(dylow_ref[...], wout_ref[b])
    lr, li, _, pr, pi = lam_rows(z, tab_ref, b)
    state = scan(z, dh_ref, None, lr, -li, keep_ref, zeros_state(z), b == 0)
    pack(tile_ref, end_state(z, state, ends_ref, chunk_ref, pr, -pi, b == 0))
    spread(send_ref, tile_ref)


def turn(z, recv_ref, dev_ref, power_ref, ends_ref, chunk_ref, proj_ref, keep_ref, tab_ref, v_ref, norm_ref, gain_ref,
         bias_ref, skip_ref, wout_ref, wglu_ref, bglu_ref, gout_ref, adj_keep_ref, adj_chunk_ref,
         h_ref, carry_ref, out_ref, dy_ref, dh_ref, adj_ends_ref, send_ref, small_ref, half_keep, half_send,
         tile_ref, wide_ref, slope_ref, natural_ref, hlow_ref, act_ref, dz_ref, dylow_ref):
    mix(z, 1, recv_ref, dev_ref, power_ref, ends_ref, chunk_ref, proj_ref, keep_ref, tab_ref, v_ref, norm_ref, gain_ref,
        bias_ref, skip_ref, wout_ref, wglu_ref, h_ref, hlow_ref, carry_ref, slope_ref, act_ref, tile_ref, wide_ref)
    d = z.D
    b1, b2 = bglu_ref[1:2, 0:d], bglu_ref[1:2, d : 2 * d]

    def body(rows, c):
        z1 = wide_ref[rows, 0:d] + b1
        sig = jax.nn.sigmoid(wide_ref[rows, d : 2 * d] + b2)
        prod = z1 * sig
        dy_ref[rows, :] = v_ref[rows, :] + prod
        e = gout_ref[rows, :]
        d1, d2 = e * sig, e * (prod * (1.0 - sig))
        dz_ref[rows, 0:d] = d1.astype(BF16)
        dz_ref[rows, d : 2 * d] = d2.astype(BF16)
        return c[0] + fold(d1), c[1] + fold(d2)

    zero = jnp.zeros((8, d), F32)
    s0, s1 = tiles(z, body, (zero, zero))
    to_time(z, dy_ref, out_ref, natural_ref)
    descend(z, 1, jnp.concatenate([s0, s1], axis=1), dz_ref, slope_ref, v_ref, norm_ref, gain_ref, bias_ref, wglu_ref, wout_ref,
            adj_keep_ref, adj_chunk_ref, tab_ref, dy_ref, dylow_ref, dh_ref, adj_ends_ref, send_ref, small_ref, tile_ref)
    split_strips(z, half_keep, half_send, units(act_ref, dz_ref, half_keep) + units(hlow_ref, dylow_ref, half_keep))


def finish(z, b, recv_ref, dev_ref, power_ref, ends_ref, chunk_ref, dh_ref, keep_ref, tab_ref, proj_ref, h_ref, carry_ref,
           fwd_keep_ref, dy_ref, v_ref, norm_ref, skip_ref, win_ref, emit,
           dplow_ref, dxn_ref, lam_ref, tile_ref, adj_carry_ref):
    lr, li, gamma, pr, pi = lam_rows(z, tab_ref, b)
    reverse = b == 0
    state = carries(z, recv_ref, dev_ref, power_ref, b, -1.0, ends_ref, chunk_ref, pr, -pi, tile_ref, adj_carry_ref, reverse)
    zero = jnp.zeros((CHUNKS, z.N), F32)
    sums = [zero, zero, zero]
    put = pair_store(z, dplow_ref)

    def visit(r, s, rows, gr, gi):
        put(r, s, gamma * gr, gamma * gi)
        sums[2] = sums[2] + gr * proj_ref[rows, 0 : z.N] + gi * proj_ref[rows, z.N : 2 * z.N]
        if s == (0 if b == 0 else z.L - 1):
            span = slice(r * CHUNKS, (r + 1) * CHUNKS)
            nr, ni = carry_ref[span, 0 : z.N], carry_ref[span, z.N : 2 * z.N]
        else:
            near = step_rows(z, r, s - 1 if b == 0 else s + 1)
            nr, ni = h_ref[near, 0 : z.N], h_ref[near, z.N : 2 * z.N]
        keep = wide(fwd_keep_ref[rows, :], z)
        nr, ni = keep * nr, keep * ni
        sums[0] = sums[0] + (gr * nr + gi * ni)
        sums[1] = sums[1] + (gi * nr - gr * ni)

    scan(z, dh_ref, None, lr, -li, keep_ref, state, reverse, visit)
    dr, di, dg = (jnp.sum(s, 0, keepdims=True) for s in sums)
    r0, i0 = lr[0:1, :], li[0:1, :]
    lam_ref[0:1, :] = dg * tab_ref[b * 8 + 5 : b * 8 + 6, :] - (dr * r0 + di * i0)
    lam_ref[1:2, :] = di * r0 - dr * i0

    dxn_ref[...] = dot_t(dplow_ref[...], win_ref[b])
    mean, rstd = norm_ref[0:1, :], norm_ref[1:2, :]
    skip = skip_ref[b : b + 1, :]

    def body(rows, c):
        xhat = (v_ref[rows, :] - mean) * rstd
        dxn = dxn_ref[rows, :] + skip * dy_ref[rows, :]
        dxn_ref[rows, :] = dxn
        return c[0] + fold(dxn), c[1] + fold(dxn * xhat)

    zero = jnp.zeros((8, z.D), F32)
    s0, s1 = tiles(z, body, (zero, zero))
    emit(jnp.sum(s0, 0, keepdims=True), jnp.sum(s1, 0, keepdims=True))


def norm_grad(z, b, bias_sum, gain_sum, norm_ref, gain_ref):
    mean, rstd = norm_ref[0:1, :], norm_ref[1:2, :]
    gain = gain_ref[b : b + 1, :]
    scale, shift, slope = rstd * gain, rstd * gain * bias_sum / z.tokens, rstd * gain * gain_sum / z.tokens

    def grad(dxn, v, up):
        return scale * dxn - shift - ((v - mean) * rstd) * slope + up

    return grad


def lower_block(z, stat_ref, dxn_ref, v1_ref, norm1_ref, gout_ref, sig_ref, gate_ref, slope_ref, v_ref, norm_ref, gain_ref, bias_ref,
                wglu_ref, wout_ref, keep_ref, chunk_ref, tab_ref, act_ref, hlow_ref,
                total_ref, e_ref, dy_ref, dh_ref, ends_ref, send_ref, small_ref, half_keep, half_send, tile_ref, stat_tile, dz_ref, dylow_ref):
    bias_sum, gain_sum = two_sums(stat_ref, stat_tile, z)
    grad = norm_grad(z, 1, bias_sum, gain_sum, norm1_ref, gain_ref)
    total_ref[0:1, :] = bias_sum
    total_ref[1:2, :] = gain_sum
    d = z.D

    def body(rows, c):
        e = grad(dxn_ref[rows, :], v1_ref[rows, :], gout_ref[rows, :])
        e_ref[rows, :] = e
        d1, d2 = e * sig_ref[rows, :], e * gate_ref[rows, :]
        dz_ref[rows, 0:d] = d1.astype(BF16)
        dz_ref[rows, d : 2 * d] = d2.astype(BF16)
        return c[0] + fold(d1), c[1] + fold(d2)

    zero = jnp.zeros((8, d), F32)
    s0, s1 = tiles(z, body, (zero, zero))
    descend(z, 0, jnp.concatenate([s0, s1], axis=1), dz_ref, slope_ref, v_ref, norm_ref, gain_ref, bias_ref, wglu_ref, wout_ref,
            keep_ref, chunk_ref, tab_ref, dy_ref, dylow_ref, dh_ref, ends_ref, send_ref, small_ref, tile_ref)
    split_strips(z, half_keep, half_send, units(act_ref, dz_ref, half_keep) + units(hlow_ref, dylow_ref, half_keep))


def units(a_ref, b_ref, like):
    w = like.shape[1]

    def strip(i):
        return lambda: dot_0(a_ref[...], b_ref[:, i * w : (i + 1) * w])

    return [strip(i) for i in range(b_ref.shape[1] // w)]


def finish_upper(z, *refs):
    ins, outs = refs[:17], refs[17:]
    dxn_ref, dplow_ref, stat_ref, lam_ref, tile_ref, carry_ref, stat_tile = outs

    def emit(bias_sum, gain_sum):
        pack(stat_tile, [bias_sum, gain_sum])
        spread(stat_ref, stat_tile)

    finish(z, 1, *ins, emit, dplow_ref, dxn_ref, lam_ref, tile_ref, carry_ref)


def finish_lower(z, *refs):
    ins, (low_ref, low1_ref, dplow1_ref, small0_ref, small1_ref, lam1_ref), outs = refs[:17], refs[17:23], refs[23:]
    dxn_ref, keep_ref, send_ref, dplow_ref, lam_ref, tile_ref, carry_ref = outs
    first = keep_ref.shape[0] - z.extra

    def emit(bias_sum, gain_sum):
        sums = [bias_sum, gain_sum]
        for small, lam in ((small0_ref, lam_ref), (small1_ref, lam1_ref)):
            sums += [small[0:1, :], small[1:2, :], small[2:3, :], lam[0:1, :], lam[1:2, :]]
        for ref in (keep_ref, send_ref):
            k = pack(ref, sums, first)
            if k < ref.shape[0]:
                ref[k:, :] = jnp.zeros((ref.shape[0] - k, ref.shape[1]), F32)

    finish(z, 0, *ins, emit, dplow_ref, dxn_ref, lam_ref, tile_ref, carry_ref)
    split_strips(z, keep_ref, send_ref, units(low1_ref, dplow1_ref, keep_ref) + units(low_ref, dplow_ref, keep_ref))


def last(z, small_ref, dxn_ref, v_ref, norm_ref, gain_ref, e_ref, total1_ref, grad_ref, gain_out, bias_out, rate_out, phase_out, skip_out,
         bglu_out, natural_ref, work_ref):
    w = small_ref.shape[1]
    at = [0]

    def take(width):
        row = unpack(small_ref, at[0], width // w)
        at[0] += width // w
        return row

    bias_sum, gain_sum = take(z.D), take(z.D)
    grad = norm_grad(z, 0, bias_sum, gain_sum, norm_ref, gain_ref)
    bias_out[0:1, :] = bias_sum
    gain_out[0:1, :] = gain_sum
    bias_out[1:2, :] = total1_ref[0:1, :]
    gain_out[1:2, :] = total1_ref[1:2, :]
    for b in range(2):
        for ref, width in ((skip_out, z.D), (bglu_out, 2 * z.D), (rate_out, z.N), (phase_out, z.N)):
            ref[b : b + 1, :] = take(width)

    def body(rows, c):
        work_ref[rows, :] = grad(dxn_ref[rows, :], v_ref[rows, :], e_ref[rows, :])
        return c

    tiles(z, body, 0)
    to_time(z, work_ref, grad_ref, natural_ref)


GRAD_TILE = 64
SEQ = (2, 1, 0)
ORDERS = ((0, 1, 2, 3, 4), (0, 1, 2, 3, 4), (0, 1, 2, 3, 4))
STRIP = 256


def bit_of(z, place, parity):
    if place in (1, 2) and z.bits > 2:
        return place if parity else 3 - place
    return place


def own_bit(z, place):
    me = lax.axis_index("tm") * z.rows + lax.axis_index("rows")
    odd = me % 2
    return (me >> (odd * bit_of(z, place, 1) + (1 - odd) * bit_of(z, place, 0))) % 2


def pairs(z, place):
    return [(i, i ^ (1 << bit_of(z, place, i % 2))) for i in range(z.all)]


def split_strips(z, keep_ref, send_ref, strips):
    bit = own_bit(z, 0)
    cut = len(strips) // 2

    def write(ref, products):
        for i, product in enumerate(products):
            ref[i * z.D : (i + 1) * z.D, :] = product()

    @pl.when(bit == 0)
    def _():
        write(keep_ref, strips[:cut])
        write(send_ref, strips[cut:])

    @pl.when(bit == 1)
    def _():
        write(keep_ref, strips[cut:])
        write(send_ref, strips[:cut])


def strips_of(n):
    size = math.gcd(GRAD_TILE, n)

    def rows(part, i):
        return pl.ds(pl.multiple_of(part * n + i * size, math.gcd(size, 8)), size)

    return n // size, rows


def halves(z, step, extra, keep_ref, recv_ref, next_ref, send_ref):
    n = next_ref.shape[0] - extra
    bit = own_bit(z, step)
    count, rows = strips_of(n)

    def one(i, c):
        for ref, part in ((send_ref, 1 - bit), (next_ref, bit)):
            ref[rows(0, i), :] = keep_ref[rows(part, i), :] + recv_ref[rows(part, i), :]
        return c

    lax.fori_loop(0, count, one, 0)
    if extra:
        both = keep_ref[2 * n :, :] + recv_ref[2 * n :, :]
        next_ref[n:, :] = both
        send_ref[n:, :] = both


def total(extra, keep_ref, recv_ref, out_ref, *extra_ref):
    n = out_ref.shape[0]
    out_ref[...] = keep_ref[0:n, :] + recv_ref[0:n, :]
    if extra:
        extra_ref[0][...] = keep_ref[n:, :] + recv_ref[n:, :]


def join(z, step, own_ref, recv_ref, out_ref):
    n = own_ref.shape[0]
    bit = own_bit(z, step)
    count, rows = strips_of(n)

    def one(i, c):
        for ref, part in ((own_ref, bit), (recv_ref, 1 - bit)):
            out_ref[rows(part, i), :] = ref[rows(0, i), :]
        return c

    lax.fori_loop(0, count, one, 0)


class Exchange:
    def __init__(self, z, keep, send, extra=0, order=()):
        self.z, self.keep, self.send, self.extra = z, keep, send, extra
        self.order = order if len(order) == z.bits else tuple(range(z.bits))
        self.step, self.up, self.small = 0, False, None
        self.width = keep.shape[1]

    def go(self):
        self.got = lax.ppermute(self.send, ("tm", "rows"), pairs(self.z, self.order[self.step]))

    def settle(self):
        z, x = self.z, self.extra
        n = self.keep.shape[0]
        if self.up:
            (self.keep,) = run(functools.partial(join, z, self.order[self.step]), "join", [((2 * n, self.width), F32)], (self.keep, self.got))
            self.send = self.keep
            self.step -= 1
            return
        n -= x
        self.step += 1
        if self.step < z.bits:
            half = ((n // 2 + x, self.width), F32)
            self.keep, self.send = run(functools.partial(halves, z, self.order[self.step], x), "halves", [half, half], (self.keep, self.got))
            return
        outs = [((n, self.width), F32)] + ([((x, self.width), F32)] if x else [])
        self.keep, *self.small = run(functools.partial(total, x), "total", outs, (self.keep, self.got))
        self.send, self.up = self.keep, True
        self.step = z.bits - 1

    @property
    def closing(self):
        return self.up and self.step == 0


def assemble(z, own1, got1, owna, gota, ownb, gotb, win_out, wout_out, wglu_out, sem):
    bit = own_bit(z, 0)
    w = own1.shape[1]

    def strips(out, b):
        return [out.at[b, :, i * w : (i + 1) * w] for i in range(out.shape[2] // w)]

    places = [strips(wglu_out, 1) + strips(wout_out, 1), strips(wglu_out, 0) + strips(wout_out, 0), strips(win_out, 1) + strips(win_out, 0)]

    def place(halves_of):
        copies = []
        for (low, high), outs in zip(halves_of, places):
            cut = len(outs) // 2
            for ref, part in ((low, outs[:cut]), (high, outs[cut:])):
                for i, out in enumerate(part):
                    copies.append(pltpu.make_async_copy(ref.at[i * z.D : (i + 1) * z.D, :], out, sem.at[len(copies)]))
        for c in copies:
            c.start()
        for c in copies:
            c.wait()

    @pl.when(bit == 0)
    def _():
        place([(own1, got1), (owna, gota), (ownb, gotb)])

    @pl.when(bit == 1)
    def _():
        place([(got1, own1), (gota, owna), (gotb, ownb)])


def run(kernel, name, outs, args, scratch=(), sems=0, source=pltpu.VMEM, target=pltpu.VMEM):
    if source is pltpu.HBM:
        args = [pltpu.with_memory_space_constraint(a, source) for a in args]
    shapes = [pltpu.VMEM(s, t) if t != jnp.int32 else pltpu.SMEM(s, t) for s, t in scratch]
    return pl.pallas_call(
        kernel,
        out_shape=[jax.ShapeDtypeStruct(s, t) for s, t in outs],
        in_specs=[pl.BlockSpec(memory_space=source)] * len(args),
        out_specs=[pl.BlockSpec(memory_space=target)] * len(outs),
        scratch_shapes=shapes + ([pltpu.SemaphoreType.DMA((sems,))] if sems else []),
        compiler_params=pltpu.CompilerParams(vmem_limit_bytes=16 << 20),
        name=name,
    )(*args)


def body(x_in, lengths, bn_gain, bn_bias, w_in, decay_rate, phase, w_out, skip_gain, w_glu, b_glu, grad_out):
    rows, steps, width = x_in.shape
    z = Sizes(rows, steps, width, w_in.shape[2] // 2, lax.axis_size("tm"), lax.axis_size("rows"), lengths.shape[1])
    T, D, N = z.T, z.D, z.N
    everyone = ("tm", "rows")

    def swap(a, axis):
        return lax.all_to_all(a, axis, 0, 0)

    stat_shape = ((z.all, z.stat, LANES), F32)
    send_shape = ((z.tm, z.packed, LANES), F32)
    tile = ((z.packed, LANES), F32)
    stat_tile = ((z.stat, LANES), F32)
    full, low = ((T, D), F32), ((T, D), BF16)
    full_n, low_n = ((T, 2 * N), F32), ((T, 2 * N), BF16)
    chunk = ((z.R * CHUNKS, 2 * N), F32)
    mask = ((T, LANES), F32)
    chunk_mask = ((z.R * CHUNKS, LANES), F32)
    norm_shape = ((8, D), F32)
    small_shape = ((8, D), F32)
    lam_shape = ((8, N), F32)
    wide_f, wide_b = ((T, 2 * D), F32), ((T, 2 * D), BF16)
    bind = functools.partial

    natural = ((D // LANES, T, LANES), F32)
    (x, gout, stat0, keep_f, keep_r, chunk_f, chunk_r, dev_f, dev_r, tab, power,
     bn_gain, bn_bias, skip_gain, b_glu, w_in, w_out, w_glu) = run(
        bind(prepare, z), "prepare",
        [full, full, stat_shape, mask, mask, chunk_mask, chunk_mask, send_shape, send_shape, ((16, N), F32), ((4, z.packed, LANES), F32)]
        + [(a.shape, a.dtype) for a in (bn_gain, bn_bias, skip_gain, b_glu, w_in, w_out, w_glu)],
        (lengths, x_in.reshape(T, D), grad_out.reshape(T, D), decay_rate, phase, bn_gain, bn_bias, skip_gain, b_glu, w_in, w_out, w_glu),
        [stat_tile, natural, low, low, ((2, N), F32), ((2, N), F32), (lengths.shape, jnp.int32)], sems=12, source=pltpu.HBM)
    stat0 = swap(stat0, everyone)
    norm0, low0, proj0, ends0, send0 = run(
        bind(enter, z, 0), "enter0", [norm_shape, low, full_n, chunk, send_shape],
        (stat0, x, bn_gain, bn_bias, w_in, keep_f, chunk_f, tab), [stat_tile, tile])
    send0 = swap(send0, "tm")
    h0, hlow0, carry0, slope0, act0, sig0, gate0, v1, stat1 = run(
        bind(middle, z), "middle", [full_n, low_n, chunk, full, low, full, full, full, stat_shape],
        (send0, dev_f, power, ends0, chunk_f, proj0, keep_f, tab, x, norm0, bn_gain, bn_bias, skip_gain, w_out, w_glu, b_glu),
        [tile, wide_f, stat_tile])
    stat1 = swap(stat1, everyone)
    norm1, low1, proj1, ends1, send1 = run(
        bind(enter, z, 1), "enter1", [norm_shape, low, full_n, chunk, send_shape],
        (stat1, v1, bn_gain, bn_bias, w_in, keep_r, chunk_r, tab), [stat_tile, tile])
    send1 = swap(send1, "tm")
    W = STRIP if D * D // STRIP % (8 * z.all) == 0 else LANES

    def part(count, extra=0):
        return ((count * D // W * D // 2 + extra, W), F32)

    def tie(*values):
        return lax.optimization_barrier(values)

    h1, carry1, out, dy1, dh1, adj_ends1, adj1, small1, keep1, send1 = run(
        bind(turn, z), "turn",
        [full_n, chunk, low, full, full_n, chunk, send_shape, small_shape, part(3), part(3)],
        (send1, dev_r, power, ends1, chunk_r, proj1, keep_r, tab, v1, norm1, bn_gain, bn_bias, skip_gain, w_out, w_glu, b_glu, gout,
         keep_f, chunk_f), [tile, wide_f, full, natural, low_n, low, wide_b, low])
    one = Exchange(z, keep1, send1, order=ORDERS[0])
    one.send, adj1 = tie(one.send, adj1)
    one.go()
    adj1 = swap(adj1, "tm")
    one.got, adj1 = tie(one.got, adj1)
    one.settle()
    dxn1, dplow1, sum1, lam1 = run(
        bind(finish_upper, z), "finish1", [full, low_n, stat_shape, lam_shape],
        (adj1, dev_f, power, adj_ends1, chunk_f, dh1, keep_f, tab, proj1, h1, carry1, keep_r, dy1, v1, norm1, skip_gain, w_in),
        [tile, chunk, stat_tile])
    one.send, sum1 = tie(one.send, sum1)
    one.go()
    sum1 = swap(sum1, everyone)
    one.got, sum1 = tie(one.got, sum1)
    one.settle()
    total1, e1, dy0, dh0, adj_ends0, adj0, small0, keepa, senda = run(
        bind(lower_block, z), "lower_block",
        [norm_shape, full, full, full_n, chunk, send_shape, small_shape, part(3), part(3)],
        (sum1, dxn1, v1, norm1, gout, sig0, gate0, slope0, x, norm0, bn_gain, bn_bias, w_glu, w_out, keep_r, chunk_r, tab, act0, hlow0),
        [tile, stat_tile, wide_b, low])
    two = Exchange(z, keepa, senda, order=ORDERS[1])
    one.send, two.send, adj0 = tie(one.send, two.send, adj0)
    one.go()
    two.go()
    adj0 = swap(adj0, "tm")
    one.got, two.got, adj0 = tie(one.got, two.got, adj0)
    rows_sum = (2 * D + 2 * (3 * D + 2 * N)) // W
    z.extra = -(-rows_sum // 8) * 8
    last_part = part(2, z.extra)
    dxn0, keepb, sendb = run(
        bind(finish_lower, z), "finish0", [full, last_part, last_part],
        (adj0, dev_r, power, adj_ends0, chunk_r, dh0, keep_r, tab, proj0, h0, carry0, keep_f, dy0, x, norm0, skip_gain, w_in,
         low0, low1, dplow1, small0, small1, lam1),
        [low_n, lam_shape, tile, chunk])
    one.settle()
    two.settle()
    three = Exchange(z, keepb, sendb, z.extra, ORDERS[2])
    one.send, two.send, three.send = tie(one.send, two.send, three.send)
    for e in (one, two, three):
        e.go()
    sets = [(one, two, three)[i] for i in SEQ]
    ahead = three.send
    while not all(e.closing for e in sets):
        for e in sets:
            if not e.closing:
                e.got, _ = tie(e.got, ahead)
                e.settle()
                e.go()
                ahead = e.send
    sums = (((2, D), F32), ((2, D), F32), ((2, N), F32), ((2, N), F32), ((2, D), F32), ((2, 2 * D), F32))
    grad_x, gain_out, bias_out, rate_out, phase_out, skip_out, bglu_out = run(
        bind(last, z), "last", [full, *sums], (three.small[0], dxn0, x, norm0, bn_gain, e1, total1), [natural, full])
    gwin, gwout, gwglu = run(
        bind(assemble, z), "assemble", [((2, D, 2 * N), F32), ((2, 2 * N, D), F32), ((2, D, 2 * D), F32)],
        (one.keep, one.got, two.keep, two.got, three.keep, three.got), sems=16, target=pltpu.HBM)
    return (
        out.reshape(rows, steps, width),
        grad_x.reshape(rows, steps, width),
        gain_out,
        bias_out,
        gwin,
        rate_out,
        phase_out,
        gwout,
        skip_out,
        gwglu,
        bglu_out,
    )


def solution(mesh):
    split, rep = P("rows", "tm", None), P()
    return jax.shard_map(
        body,
        mesh=mesh,
        in_specs=(split, P("rows", None)) + (rep,) * 9 + (split,),
        out_specs=(split, split) + (rep,) * 9,
        check_vma=False,
    )
```

```python
import functools
import math

import jax
import jax.numpy as jnp
from jax import lax
from jax.experimental import pallas as pl
from jax.experimental.pallas import tpu as pltpu
from jax.sharding import PartitionSpec as P

EPS = 1e-05
LANES = 128
CHUNKS = 8
TILE = 32
F32 = jnp.float32
BF16 = jnp.bfloat16
ROOT_HALF = 0.7071067811865476
ROOT_TWO_PI_INV = 0.3989422804014327


class Sizes:
    def __init__(self, rows, steps, width, states, count_tm, count_rows, per_row):
        self.R, self.S, self.D, self.N = rows, steps, width, states
        self.T = rows * steps
        self.L = steps // CHUNKS
        self.tm, self.rows = count_tm, count_rows
        self.all = count_tm * count_rows
        self.seqs = per_row
        self.half = states // LANES
        self.packed = rows * 2 * self.half
        self.stat = 2 * width // LANES
        self.tokens = self.T * self.all
        self.bits = self.all.bit_length() - 1
        self.extra = 0


def dot(a, b):
    return jnp.dot(a, b, preferred_element_type=F32)


def dot_t(a, b):
    return lax.dot_general(a, b, (((1,), (1,)), ((), ())), preferred_element_type=F32)


def dot_0(a, b):
    return lax.dot_general(a, b, (((0,), (0,)), ((), ())), preferred_element_type=F32)


def fold(a):
    return a.reshape(a.shape[0] // 8, 8, a.shape[1]).sum(0)


def wide(a, z):
    return jnp.concatenate([a] * z.half, axis=1)


def tiles(z, body, carry):
    def one(i, c):
        return body(pl.ds(pl.multiple_of(i * TILE, TILE), TILE), c)

    return lax.fori_loop(0, z.T // TILE, one, carry)


def pack(ref, rows, k=0):
    w = ref.shape[1]
    for row in rows:
        for i in range(row.shape[1] // w):
            ref[k : k + 1, :] = row[:, i * w : (i + 1) * w]
            k += 1
    return k


def unpack(ref, first, count):
    return jnp.concatenate([ref[first + i : first + i + 1, :] for i in range(count)], axis=1)


def spread(out_ref, tile_ref):
    value = tile_ref[...]
    for j in range(out_ref.shape[0]):
        out_ref[j] = value


def two_sums(recv_ref, tile_ref, z):
    tile_ref[...] = jnp.sum(recv_ref[...], axis=0)
    n = z.D // LANES
    return unpack(tile_ref, 0, n), unpack(tile_ref, n, n)


def step_rows(z, r, s):
    first = r * z.S + s * CHUNKS
    return slice(first, first + CHUNKS)


def to_steps(z, source, out_ref, natural_ref):
    lanes = z.D // LANES

    def split(rows, c):
        value = source(rows)
        for k in range(lanes):
            natural_ref[k, rows, :] = value[:, k * LANES : (k + 1) * LANES]
        return c

    tiles(z, split, 0)
    for r in range(z.R):
        for s in range(z.L):
            for k in range(lanes):
                out_ref[step_rows(z, r, s), k * LANES : (k + 1) * LANES] = natural_ref[k, pl.ds(r * z.S + s, CHUNKS, stride=z.L), :]


def to_time(z, source_ref, out_ref, natural_ref):
    lanes = z.D // LANES
    for r in range(z.R):
        for s in range(z.L):
            for k in range(lanes):
                natural_ref[k, pl.ds(r * z.S + s, CHUNKS, stride=z.L), :] = source_ref[step_rows(z, r, s), k * LANES : (k + 1) * LANES]

    def join(rows, c):
        value = jnp.concatenate([natural_ref[k, rows, :] for k in range(lanes)], axis=1)
        out_ref[rows, :] = value.astype(out_ref.dtype)
        return c

    tiles(z, join, 0)


def pair_store(z, ref):
    held = {}

    def put(r, s, re, im):
        if (r, s ^ 1) not in held:
            held[r, s] = (re, im)
            return
        other = held.pop((r, s ^ 1))
        low, high = (other, (re, im)) if s & 1 else ((re, im), other)
        rows = slice(r * z.S + (s & ~1) * CHUNKS, r * z.S + ((s & ~1) + 2) * CHUNKS)
        ref[rows, 0 : z.N] = jnp.concatenate([low[0], high[0]], axis=0).astype(ref.dtype)
        ref[rows, z.N : 2 * z.N] = jnp.concatenate([low[1], high[1]], axis=0).astype(ref.dtype)

    return put


def scan(z, drive_ref, gain, lr, li, keep_ref, state, reverse, visit=None):
    for step in range(z.L):
        s = z.L - 1 - step if reverse else step
        for r in range(z.R):
            rows = step_rows(z, r, s)
            keep = wide(keep_ref[rows, :], z)
            ur = drive_ref[rows, 0 : z.N]
            ui = drive_ref[rows, z.N : 2 * z.N]
            if gain is not None:
                ur, ui = ur * gain, ui * gain
            hr, hi = keep * state[r][0], keep * state[r][1]
            state[r] = (lr * hr - li * hi + ur, lr * hi + li * hr + ui)
            if visit is not None:
                visit(r, s, rows, *state[r])
    return state


def zeros_state(z):
    return [(jnp.zeros((CHUNKS, z.N), F32), jnp.zeros((CHUNKS, z.N), F32)) for _ in range(z.R)]


def chunk_order(reverse):
    return range(CHUNKS - 1, -1, -1) if reverse else range(CHUNKS)


def end_state(z, state, ends_ref, chunk_keep_ref, pr, pi, reverse):
    rows = []
    for r in range(z.R):
        ends_ref[r * CHUNKS : (r + 1) * CHUNKS, 0 : z.N] = state[r][0]
        ends_ref[r * CHUNKS : (r + 1) * CHUNKS, z.N : 2 * z.N] = state[r][1]
    for r in range(z.R):
        cr = ci = None
        for c in chunk_order(reverse):
            k = r * CHUNKS + c
            er, ei = ends_ref[k : k + 1, 0 : z.N], ends_ref[k : k + 1, z.N : 2 * z.N]
            if cr is None:
                cr, ci = er, ei
            else:
                keep = wide(chunk_keep_ref[k : k + 1, :], z)
                cr, ci = keep * cr, keep * ci
                cr, ci = pr * cr - pi * ci + er, pr * ci + pi * cr + ei
        rows += [cr, ci]
    return rows


def carries(z, recv_ref, device_keep_ref, power_ref, b, sign, ends_ref, chunk_keep_ref, pr, pi, tile_ref, carry_ref, reverse):
    place = lax.axis_index("tm")
    pow_re = power_ref[2 * b]
    pow_im = sign * power_ref[2 * b + 1]
    is_re = (lax.broadcasted_iota(jnp.int32, (z.packed, LANES), 0) // z.half) % 2 == 0

    def hop(i, c):
        j = z.tm - 1 - i if reverse else i
        other = jnp.where(is_re, pltpu.roll(c, z.packed - z.half, 0), pltpu.roll(c, z.half, 0))
        return device_keep_ref[j] * (pow_re * c + pow_im * other) + recv_ref[j]

    ahead = z.tm - 1 - place if reverse else place
    tile_ref[...] = lax.fori_loop(0, ahead, hop, jnp.zeros((z.packed, LANES), F32))
    for r in range(z.R):
        cr = unpack(tile_ref, r * 2 * z.half, z.half)
        ci = unpack(tile_ref, r * 2 * z.half + z.half, z.half)
        order = list(chunk_order(reverse))
        for c in order:
            k = r * CHUNKS + c
            carry_ref[k : k + 1, 0 : z.N] = cr
            carry_ref[k : k + 1, z.N : 2 * z.N] = ci
            if c != order[-1]:
                keep = wide(chunk_keep_ref[k : k + 1, :], z)
                er, ei = ends_ref[k : k + 1, 0 : z.N], ends_ref[k : k + 1, z.N : 2 * z.N]
                cr, ci = keep * cr, keep * ci
                cr, ci = pr * cr - pi * ci + er, pr * ci + pi * cr + ei
    state = []
    for r in range(z.R):
        span = slice(r * CHUNKS, (r + 1) * CHUNKS)
        state.append((carry_ref[span, 0 : z.N], carry_ref[span, z.N : 2 * z.N]))
    return state


def lam_rows(z, tab_ref, b):
    def row(i):
        return tab_ref[b * 8 + i : b * 8 + i + 1, :]

    def full(i):
        return jnp.broadcast_to(row(i), (CHUNKS, z.N))

    return full(0), full(1), full(2), row(3), row(4)


def prepare(z, len_hbm, x_hbm, gout_hbm, rate_hbm, phase_hbm, gain_hbm, bias_hbm, skip_hbm, bglu_hbm, win_hbm, wout_hbm, wglu_hbm,
            v_ref, up_ref, stat_ref, keep_f, keep_r, chunk_f, chunk_r, dev_f, dev_r, tab_ref, power_ref,
            gain_ref, bias_ref, skip_ref, bglu_ref, win_ref, wout_ref, wglu_ref,
            tile_ref, natural_ref, x_ref, gout_ref, rate_ref, phase_ref, len_ref, sem):
    moves = [(x_hbm, x_ref), (len_hbm, len_ref), (rate_hbm, rate_ref), (phase_hbm, phase_ref), (gout_hbm, gout_ref),
             (gain_hbm, gain_ref), (bias_hbm, bias_ref), (win_hbm, win_ref), (skip_hbm, skip_ref), (bglu_hbm, bglu_ref),
             (wout_hbm, wout_ref), (wglu_hbm, wglu_ref)]
    copies = [pltpu.make_async_copy(a, b, sem.at[i]) for i, (a, b) in enumerate(moves)]
    for c in copies:
        c.start()
    copies[0].wait()
    to_steps(z, lambda rows: x_ref[rows, :].astype(F32), v_ref, natural_ref)

    def body(rows, c):
        v = v_ref[rows, :]
        return c[0] + fold(v), c[1] + fold(v * v)

    zero = jnp.zeros((8, z.D), F32)
    s0, s1 = tiles(z, body, (zero, zero))
    pack(tile_ref, [jnp.sum(s0, 0, keepdims=True), jnp.sum(s1, 0, keepdims=True)])
    spread(stat_ref, tile_ref)
    for c in copies[1:5]:
        c.wait()
    to_steps(z, lambda rows: gout_ref[rows, :].astype(F32), up_ref, natural_ref)
    base = lax.axis_index("tm") * z.S
    place = lax.broadcasted_iota(jnp.int32, (z.S, LANES), 0)
    at = base + (place % CHUNKS) * z.L + place // CHUNKS
    chunk_at = base + z.L * lax.broadcasted_iota(jnp.int32, (CHUNKS, LANES), 0)
    dev_at = z.S * lax.broadcasted_iota(jnp.int32, (z.tm, LANES), 0)
    for r in range(z.R):
        end = jnp.int32(0)
        hit = [jnp.zeros(a.shape, jnp.bool_) for a in (at, at, chunk_at, chunk_at, dev_at, dev_at)]
        for q in range(z.seqs):
            start = end
            end = end + len_ref[r, q]
            last = end - 1
            hit[0] = hit[0] | (at == start)
            hit[1] = hit[1] | (at == last)
            for i, mark in ((2, start), (3, last)):
                hit[i] = hit[i] | ((chunk_at <= mark) & (mark < chunk_at + z.L))
            for i, mark in ((4, start), (5, last)):
                hit[i] = hit[i] | ((dev_at <= mark) & (mark < dev_at + z.S))
        keep = [1.0 - h.astype(F32) for h in hit]
        keep_f[r * z.S : (r + 1) * z.S, :] = keep[0]
        keep_r[r * z.S : (r + 1) * z.S, :] = keep[1]
        chunk_f[r * CHUNKS : (r + 1) * CHUNKS, :] = keep[2]
        chunk_r[r * CHUNKS : (r + 1) * CHUNKS, :] = keep[3]
        each = 2 * z.half
        for j in range(z.tm):
            for ref, k in ((dev_f, keep[4]), (dev_r, keep[5])):
                ref[j, r * each : (r + 1) * each, :] = jnp.broadcast_to(k[j : j + 1, :], (each, LANES))
    for b in range(2):
        rate, angle = rate_ref[b : b + 1, :], phase_ref[b : b + 1, :]
        size = jnp.exp(-rate)
        lr, li = size * jnp.cos(angle), size * jnp.sin(angle)
        gamma = jnp.sqrt(1.0 - jnp.exp(-2.0 * rate))

        def power(n):
            out, br, bi = None, lr, li
            while n:
                if n & 1:
                    out = (br, bi) if out is None else (out[0] * br - out[1] * bi, out[0] * bi + out[1] * br)
                br, bi = br * br - bi * bi, 2.0 * br * bi
                n >>= 1
            return out

        chunk_power, device_power = power(z.L), power(z.S)
        rows = [lr, li, gamma, chunk_power[0], chunk_power[1], jnp.exp(-2.0 * rate) / gamma]
        for i, row in enumerate(rows):
            tab_ref[b * 8 + i : b * 8 + i + 1, :] = row
        for i in range(6, 8):
            tab_ref[b * 8 + i : b * 8 + i + 1, :] = jnp.zeros_like(lr)
        pack(power_ref.at[2 * b], [device_power[0], device_power[0]] * z.R)
        pack(power_ref.at[2 * b + 1], [-device_power[1], device_power[1]] * z.R)
    for c in copies[5:]:
        c.wait()


def enter(z, b, stat_ref, v_ref, gain_ref, bias_ref, win_ref, keep_ref, chunk_ref, tab_ref,
          norm_ref, low_ref, proj_ref, ends_ref, send_ref, stat_tile, tile_ref):
    total, square = two_sums(stat_ref, stat_tile, z)
    mean = total / z.tokens
    rstd = lax.rsqrt(square / z.tokens - mean * mean + EPS)
    norm_ref[0:1, :] = mean
    norm_ref[1:2, :] = rstd
    gain, bias = gain_ref[b : b + 1, :], bias_ref[b : b + 1, :]

    def body(rows, c):
        xhat = (v_ref[rows, :] - mean) * rstd
        low_ref[rows, :] = (gain * xhat + bias).astype(BF16)
        return c

    tiles(z, body, 0)
    proj_ref[...] = dot(low_ref[...], win_ref[b])
    lr, li, gamma, pr, pi = lam_rows(z, tab_ref, b)
    state = scan(z, proj_ref, gamma, lr, li, keep_ref, zeros_state(z), b == 1)
    pack(tile_ref, end_state(z, state, ends_ref, chunk_ref, pr, pi, b == 1))
    spread(send_ref, tile_ref)


def gelu_pair(y):
    cdf = 0.5 + 0.5 * lax.erf(y * ROOT_HALF)
    return y * cdf, cdf + y * (ROOT_TWO_PI_INV * jnp.exp(-0.5 * y * y))


def mix(z, b, recv_ref, dev_ref, power_ref, ends_ref, chunk_ref, proj_ref, keep_ref, tab_ref, v_ref, norm_ref, gain_ref,
        bias_ref, skip_ref, wout_ref, wglu_ref, h_ref, hlow_ref, carry_ref, slope_ref, act_ref, tile_ref, wide_ref):
    lr, li, gamma, pr, pi = lam_rows(z, tab_ref, b)
    state = carries(z, recv_ref, dev_ref, power_ref, b, 1.0, ends_ref, chunk_ref, pr, pi, tile_ref, carry_ref, b == 1)

    put = pair_store(z, hlow_ref)

    def visit(r, s, rows, hr, hi):
        h_ref[rows, 0 : z.N] = hr
        h_ref[rows, z.N : 2 * z.N] = hi
        put(r, s, hr, hi)

    scan(z, proj_ref, gamma, lr, li, keep_ref, state, b == 1, visit)
    slope_ref[...] = dot(hlow_ref[...], wout_ref[b])
    mean, rstd = norm_ref[0:1, :], norm_ref[1:2, :]
    gain, bias, skip = gain_ref[b : b + 1, :], bias_ref[b : b + 1, :], skip_ref[b : b + 1, :]

    def body(rows, c):
        xn = gain * ((v_ref[rows, :] - mean) * rstd) + bias
        act, slope = gelu_pair(slope_ref[rows, :] + skip * xn)
        act_ref[rows, :] = act.astype(BF16)
        slope_ref[rows, :] = slope
        return c

    tiles(z, body, 0)
    wide_ref[...] = dot(act_ref[...], wglu_ref[b])


def middle(z, recv_ref, dev_ref, power_ref, ends_ref, chunk_ref, proj_ref, keep_ref, tab_ref, v_ref, norm_ref, gain_ref,
           bias_ref, skip_ref, wout_ref, wglu_ref, bglu_ref,
           h_ref, hlow_ref, carry_ref, slope_ref, act_ref, sig_ref, gate_ref, next_ref, stat_ref, tile_ref, wide_ref, stat_tile):
    mix(z, 0, recv_ref, dev_ref, power_ref, ends_ref, chunk_ref, proj_ref, keep_ref, tab_ref, v_ref, norm_ref, gain_ref,
        bias_ref, skip_ref, wout_ref, wglu_ref, h_ref, hlow_ref, carry_ref, slope_ref, act_ref, tile_ref, wide_ref)
    d = z.D
    b1, b2 = bglu_ref[0:1, 0:d], bglu_ref[0:1, d : 2 * d]

    def body(rows, c):
        z1 = wide_ref[rows, 0:d] + b1
        sig = jax.nn.sigmoid(wide_ref[rows, d : 2 * d] + b2)
        prod = z1 * sig
        sig_ref[rows, :] = sig
        gate_ref[rows, :] = prod * (1.0 - sig)
        v = v_ref[rows, :] + prod
        next_ref[rows, :] = v
        return c[0] + fold(v), c[1] + fold(v * v)

    zero = jnp.zeros((8, d), F32)
    s0, s1 = tiles(z, body, (zero, zero))
    pack(stat_tile, [jnp.sum(s0, 0, keepdims=True), jnp.sum(s1, 0, keepdims=True)])
    spread(stat_ref, stat_tile)


def descend(z, b, grad_bglu, dz_ref, slope_ref, v_ref, norm_ref, gain_ref, bias_ref, wglu_ref, wout_ref, keep_ref, chunk_ref, tab_ref,
            dy_ref, dylow_ref, dh_ref, ends_ref, send_ref, small_ref, tile_ref):
    dy_ref[...] = dot_t(dz_ref[...], wglu_ref[b])
    mean, rstd = norm_ref[0:1, :], norm_ref[1:2, :]
    gain, bias = gain_ref[b : b + 1, :], bias_ref[b : b + 1, :]

    def body(rows, c):
        xn = gain * ((v_ref[rows, :] - mean) * rstd) + bias
        dy = dy_ref[rows, :] * slope_ref[rows, :]
        dy_ref[rows, :] = dy
        dylow_ref[rows, :] = dy.astype(BF16)
        return c + fold(dy * xn)

    grad_skip = tiles(z, body, jnp.zeros((8, z.D), F32))
    small_ref[0:1, :] = jnp.sum(grad_skip, 0, keepdims=True)
    total = jnp.sum(grad_bglu, 0, keepdims=True)
    small_ref[1:2, :] = total[:, 0 : z.D]
    small_ref[2:3, :] = total[:, z.D : 2 * z.D]
    dh_ref[...] = dot_t(dylow_ref[...], wout_ref[b])
    lr, li, _, pr, pi = lam_rows(z, tab_ref, b)
    state = scan(z, dh_ref, None, lr, -li, keep_ref, zeros_state(z), b == 0)
    pack(tile_ref, end_state(z, state, ends_ref, chunk_ref, pr, -pi, b == 0))
    spread(send_ref, tile_ref)


def turn(z, recv_ref, dev_ref, power_ref, ends_ref, chunk_ref, proj_ref, keep_ref, tab_ref, v_ref, norm_ref, gain_ref,
         bias_ref, skip_ref, wout_ref, wglu_ref, bglu_ref, gout_ref, adj_keep_ref, adj_chunk_ref,
         h_ref, carry_ref, final_ref, dy_ref, dh_ref, adj_ends_ref, send_ref, small_ref, half_keep, half_send,
         tile_ref, wide_ref, slope_ref, hlow_ref, act_ref, dz_ref, dylow_ref):
    mix(z, 1, recv_ref, dev_ref, power_ref, ends_ref, chunk_ref, proj_ref, keep_ref, tab_ref, v_ref, norm_ref, gain_ref,
        bias_ref, skip_ref, wout_ref, wglu_ref, h_ref, hlow_ref, carry_ref, slope_ref, act_ref, tile_ref, wide_ref)
    d = z.D
    b1, b2 = bglu_ref[1:2, 0:d], bglu_ref[1:2, d : 2 * d]

    def body(rows, c):
        z1 = wide_ref[rows, 0:d] + b1
        sig = jax.nn.sigmoid(wide_ref[rows, d : 2 * d] + b2)
        prod = z1 * sig
        final_ref[rows, :] = v_ref[rows, :] + prod
        e = gout_ref[rows, :]
        d1, d2 = e * sig, e * (prod * (1.0 - sig))
        dz_ref[rows, 0:d] = d1.astype(BF16)
        dz_ref[rows, d : 2 * d] = d2.astype(BF16)
        return c[0] + fold(d1), c[1] + fold(d2)

    zero = jnp.zeros((8, d), F32)
    s0, s1 = tiles(z, body, (zero, zero))
    descend(z, 1, jnp.concatenate([s0, s1], axis=1), dz_ref, slope_ref, v_ref, norm_ref, gain_ref, bias_ref, wglu_ref, wout_ref,
            adj_keep_ref, adj_chunk_ref, tab_ref, dy_ref, dylow_ref, dh_ref, adj_ends_ref, send_ref, small_ref, tile_ref)
    split_strips(z, half_keep, half_send, units(act_ref, dz_ref, half_keep) + units(hlow_ref, dylow_ref, half_keep))


def finish(z, b, recv_ref, dev_ref, power_ref, ends_ref, chunk_ref, dh_ref, keep_ref, tab_ref, proj_ref, h_ref, carry_ref,
           fwd_keep_ref, dy_ref, v_ref, norm_ref, skip_ref, win_ref, emit,
           dplow_ref, dxn_ref, lam_ref, tile_ref, adj_carry_ref):
    lr, li, gamma, pr, pi = lam_rows(z, tab_ref, b)
    reverse = b == 0
    state = carries(z, recv_ref, dev_ref, power_ref, b, -1.0, ends_ref, chunk_ref, pr, -pi, tile_ref, adj_carry_ref, reverse)
    zero = jnp.zeros((CHUNKS, z.N), F32)
    sums = [zero, zero, zero]
    put = pair_store(z, dplow_ref)

    def visit(r, s, rows, gr, gi):
        put(r, s, gamma * gr, gamma * gi)
        sums[2] = sums[2] + gr * proj_ref[rows, 0 : z.N] + gi * proj_ref[rows, z.N : 2 * z.N]
        if s == (0 if b == 0 else z.L - 1):
            span = slice(r * CHUNKS, (r + 1) * CHUNKS)
            nr, ni = carry_ref[span, 0 : z.N], carry_ref[span, z.N : 2 * z.N]
        else:
            near = step_rows(z, r, s - 1 if b == 0 else s + 1)
            nr, ni = h_ref[near, 0 : z.N], h_ref[near, z.N : 2 * z.N]
        keep = wide(fwd_keep_ref[rows, :], z)
        nr, ni = keep * nr, keep * ni
        sums[0] = sums[0] + (gr * nr + gi * ni)
        sums[1] = sums[1] + (gi * nr - gr * ni)

    scan(z, dh_ref, None, lr, -li, keep_ref, state, reverse, visit)
    dr, di, dg = (jnp.sum(s, 0, keepdims=True) for s in sums)
    r0, i0 = lr[0:1, :], li[0:1, :]
    lam_ref[0:1, :] = dg * tab_ref[b * 8 + 5 : b * 8 + 6, :] - (dr * r0 + di * i0)
    lam_ref[1:2, :] = di * r0 - dr * i0

    dxn_ref[...] = dot_t(dplow_ref[...], win_ref[b])
    mean, rstd = norm_ref[0:1, :], norm_ref[1:2, :]
    skip = skip_ref[b : b + 1, :]

    def body(rows, c):
        xhat = (v_ref[rows, :] - mean) * rstd
        dxn = dxn_ref[rows, :] + skip * dy_ref[rows, :]
        dxn_ref[rows, :] = dxn
        return c[0] + fold(dxn), c[1] + fold(dxn * xhat)

    zero = jnp.zeros((8, z.D), F32)
    s0, s1 = tiles(z, body, (zero, zero))
    emit(jnp.sum(s0, 0, keepdims=True), jnp.sum(s1, 0, keepdims=True))


def norm_grad(z, b, bias_sum, gain_sum, norm_ref, gain_ref):
    mean, rstd = norm_ref[0:1, :], norm_ref[1:2, :]
    gain = gain_ref[b : b + 1, :]
    scale, shift, slope = rstd * gain, rstd * gain * bias_sum / z.tokens, rstd * gain * gain_sum / z.tokens

    def grad(dxn, v, up):
        return scale * dxn - shift - ((v - mean) * rstd) * slope + up

    return grad


def lower_block(z, stat_ref, dxn_ref, v1_ref, norm1_ref, gout_ref, sig_ref, gate_ref, slope_ref, v_ref, norm_ref, gain_ref, bias_ref,
                wglu_ref, wout_ref, keep_ref, chunk_ref, tab_ref, act_ref, hlow_ref,
                total_ref, e_ref, dy_ref, dh_ref, ends_ref, send_ref, small_ref, half_keep, half_send, tile_ref, stat_tile, dz_ref, dylow_ref):
    bias_sum, gain_sum = two_sums(stat_ref, stat_tile, z)
    grad = norm_grad(z, 1, bias_sum, gain_sum, norm1_ref, gain_ref)
    total_ref[0:1, :] = bias_sum
    total_ref[1:2, :] = gain_sum
    d = z.D

    def body(rows, c):
        e = grad(dxn_ref[rows, :], v1_ref[rows, :], gout_ref[rows, :])
        e_ref[rows, :] = e
        d1, d2 = e * sig_ref[rows, :], e * gate_ref[rows, :]
        dz_ref[rows, 0:d] = d1.astype(BF16)
        dz_ref[rows, d : 2 * d] = d2.astype(BF16)
        return c[0] + fold(d1), c[1] + fold(d2)

    zero = jnp.zeros((8, d), F32)
    s0, s1 = tiles(z, body, (zero, zero))
    descend(z, 0, jnp.concatenate([s0, s1], axis=1), dz_ref, slope_ref, v_ref, norm_ref, gain_ref, bias_ref, wglu_ref, wout_ref,
            keep_ref, chunk_ref, tab_ref, dy_ref, dylow_ref, dh_ref, ends_ref, send_ref, small_ref, tile_ref)
    split_strips(z, half_keep, half_send, units(act_ref, dz_ref, half_keep) + units(hlow_ref, dylow_ref, half_keep))


def units(a_ref, b_ref, like):
    w = like.shape[1]

    def strip(i):
        return lambda: dot_0(a_ref[...], b_ref[:, i * w : (i + 1) * w])

    return [strip(i) for i in range(b_ref.shape[1] // w)]


def finish_upper(z, *refs):
    ins, outs = refs[:17], refs[17:]
    dxn_ref, dplow_ref, stat_ref, lam_ref, tile_ref, carry_ref, stat_tile = outs

    def emit(bias_sum, gain_sum):
        pack(stat_tile, [bias_sum, gain_sum])
        spread(stat_ref, stat_tile)

    finish(z, 1, *ins, emit, dplow_ref, dxn_ref, lam_ref, tile_ref, carry_ref)


def finish_lower(z, *refs):
    ins, (low_ref, low1_ref, dplow1_ref, small0_ref, small1_ref, lam1_ref), outs = refs[:17], refs[17:23], refs[23:]
    dxn_ref, keep_ref, send_ref, dplow_ref, lam_ref, tile_ref, carry_ref = outs
    first = keep_ref.shape[0] - z.extra

    def emit(bias_sum, gain_sum):
        sums = [bias_sum, gain_sum]
        for small, lam in ((small0_ref, lam_ref), (small1_ref, lam1_ref)):
            sums += [small[0:1, :], small[1:2, :], small[2:3, :], lam[0:1, :], lam[1:2, :]]
        for ref in (keep_ref, send_ref):
            k = pack(ref, sums, first)
            if k < ref.shape[0]:
                ref[k:, :] = jnp.zeros((ref.shape[0] - k, ref.shape[1]), F32)

    finish(z, 0, *ins, emit, dplow_ref, dxn_ref, lam_ref, tile_ref, carry_ref)
    split_strips(z, keep_ref, send_ref, units(low1_ref, dplow1_ref, keep_ref) + units(low_ref, dplow_ref, keep_ref))


def last(z, small_ref, dxn_ref, v_ref, norm_ref, gain_ref, e_ref, total1_ref, final_ref, out_ref, grad_ref, gain_out, bias_out, rate_out, phase_out, skip_out,
         bglu_out, natural_ref, work_ref):
    w = small_ref.shape[1]
    at = [0]

    def take(width):
        row = unpack(small_ref, at[0], width // w)
        at[0] += width // w
        return row

    bias_sum, gain_sum = take(z.D), take(z.D)
    grad = norm_grad(z, 0, bias_sum, gain_sum, norm_ref, gain_ref)
    bias_out[0:1, :] = bias_sum
    gain_out[0:1, :] = gain_sum
    bias_out[1:2, :] = total1_ref[0:1, :]
    gain_out[1:2, :] = total1_ref[1:2, :]
    for b in range(2):
        for ref, width in ((skip_out, z.D), (bglu_out, 2 * z.D), (rate_out, z.N), (phase_out, z.N)):
            ref[b : b + 1, :] = take(width)

    def body(rows, c):
        work_ref[rows, :] = grad(dxn_ref[rows, :], v_ref[rows, :], e_ref[rows, :])
        return c

    tiles(z, body, 0)
    to_time(z, work_ref, grad_ref, natural_ref)
    to_time(z, final_ref, out_ref, natural_ref)


GRAD_TILE = 64
SEQ = (0, 2, 1)
FIRST = ()
COST = 1
FLOPS = 20000000000
TRANS = 0
FLAT = (1, 1, 1)
ORDERS = ((0, 1, 2, 3, 4), (0, 1, 2, 3, 4), (0, 1, 2, 3, 4))
STRIP = 256


def bit_of(z, place, parity):
    if place in (1, 2) and z.bits > 2:
        return place if parity else 3 - place
    return place


def own_bit(z, place):
    me = lax.axis_index("tm") * z.rows + lax.axis_index("rows")
    odd = me % 2
    return (me >> (odd * bit_of(z, place, 1) + (1 - odd) * bit_of(z, place, 0))) % 2


def pairs(z, place):
    return [(i, i ^ (1 << bit_of(z, place, i % 2))) for i in range(z.all)]


def split_strips(z, keep_ref, send_ref, strips):
    bit = own_bit(z, 0)
    cut = len(strips) // 2

    def write(ref, products):
        for i, product in enumerate(products):
            ref[i * z.D : (i + 1) * z.D, :] = product()

    @pl.when(bit == 0)
    def _():
        write(keep_ref, strips[:cut])
        write(send_ref, strips[cut:])

    @pl.when(bit == 1)
    def _():
        write(keep_ref, strips[cut:])
        write(send_ref, strips[:cut])


def strips_of(n):
    size = math.gcd(GRAD_TILE, n)

    def rows(part, i):
        return pl.ds(pl.multiple_of(part * n + i * size, math.gcd(size, 8)), size)

    return n // size, rows


def halves(z, step, extra, keep_ref, recv_ref, next_ref, send_ref):
    n = next_ref.shape[0] - extra
    bit = own_bit(z, step)
    count, rows = strips_of(n)

    def one(i, c):
        for ref, part in ((send_ref, 1 - bit), (next_ref, bit)):
            ref[rows(0, i), :] = keep_ref[rows(part, i), :] + recv_ref[rows(part, i), :]
        return c

    lax.fori_loop(0, count, one, 0)
    if extra:
        both = keep_ref[2 * n :, :] + recv_ref[2 * n :, :]
        next_ref[n:, :] = both
        send_ref[n:, :] = both


def total(extra, keep_ref, recv_ref, out_ref, *extra_ref):
    n = out_ref.shape[0]
    out_ref[...] = keep_ref[0:n, :] + recv_ref[0:n, :]
    if extra:
        extra_ref[0][...] = keep_ref[n:, :] + recv_ref[n:, :]


def join(z, step, own_ref, recv_ref, out_ref):
    n = own_ref.shape[0]
    bit = own_bit(z, step)
    count, rows = strips_of(n)

    def one(i, c):
        for ref, part in ((own_ref, bit), (recv_ref, 1 - bit)):
            out_ref[rows(part, i), :] = ref[rows(0, i), :]
        return c

    lax.fori_loop(0, count, one, 0)


def add(keep_ref, recv_ref, out_ref):
    out_ref[...] = keep_ref[...] + recv_ref[...]


class Exchange:
    def __init__(self, z, keep, send, extra=0, order=(), flat=1):
        self.z, self.keep, self.send, self.extra = z, keep, send, extra
        self.order = order if len(order) == z.bits else tuple(range(z.bits))
        self.width = keep.shape[1]
        self.small = None
        deep = z.bits - flat
        self.plan = [("halve", i) for i in range(deep)] + [("sum", i) for i in range(deep, z.bits)] + [("double", i) for i in range(deep - 1, -1, -1)]

    def go(self):
        self.got = lax.ppermute(self.send, ("tm", "rows"), pairs(self.z, self.order[self.plan[0][1]]))

    def settle(self):
        z, x = self.z, self.extra
        (kind, i), (after, j) = self.plan.pop(0), self.plan[0]
        n = self.keep.shape[0]
        both = (self.keep, self.got)
        if kind == "double":
            (self.keep,) = run(functools.partial(join, z, self.order[i]), "join", [((2 * n, self.width), F32)], both)
        elif after == "halve":
            half = (((n - x) // 2 + x, self.width), F32)
            self.keep, self.send = run(functools.partial(halves, z, self.order[j], x), "halves", [half, half], both)
            return
        elif after == "double" and x:
            self.keep, self.small = run(functools.partial(total, x), "total", [((n - x, self.width), F32), ((x, self.width), F32)], both)
        else:
            (self.keep,) = run(add, "add", [((n, self.width), F32)], both)
        self.send = self.keep

    @property
    def closing(self):
        return len(self.plan) == 1


def assemble(z, which, *refs):
    own, got, (win_out, wout_out, wglu_out, sem) = refs[0], refs[1], refs[-4:]
    bit = own_bit(z, 0)
    w = own.shape[1]

    def strips(out, b):
        return [out.at[b, :, i * w : (i + 1) * w] for i in range(out.shape[2] // w)]

    outs = strips(win_out, 1) + strips(win_out, 0) if which == 2 else strips(wglu_out, 1 - which) + strips(wout_out, 1 - which)
    cut = len(outs) // 2

    def place(low, high):
        copies = []
        for ref, part in ((low, outs[:cut]), (high, outs[cut:])):
            for k, out in enumerate(part):
                copies.append(pltpu.make_async_copy(ref.at[k * z.D : (k + 1) * z.D, :], out, sem.at[len(copies)]))
        for c in copies:
            c.start()
        for c in copies:
            c.wait()

    @pl.when(bit == 0)
    def _():
        place(own, got)

    @pl.when(bit == 1)
    def _():
        place(got, own)


def run(kernel, name, outs, args, scratch=(), sems=0, source=pltpu.VMEM, target=pltpu.VMEM, onto=()):
    if source is pltpu.HBM:
        args = [pltpu.with_memory_space_constraint(a, source) for a in args]
    shapes = [pltpu.VMEM(s, t) if t != jnp.int32 else pltpu.SMEM(s, t) for s, t in scratch]
    return pl.pallas_call(
        kernel,
        out_shape=[jax.ShapeDtypeStruct(s, t) for s, t in outs],
        in_specs=[pl.BlockSpec(memory_space=source)] * len(args) + [pl.BlockSpec(memory_space=target)] * len(onto),
        out_specs=[pl.BlockSpec(memory_space=target)] * len(outs),
        scratch_shapes=shapes + ([pltpu.SemaphoreType.DMA((sems,))] if sems else []),
        compiler_params=pltpu.CompilerParams(vmem_limit_bytes=16 << 20),
        cost_estimate=pl.CostEstimate(flops=FLOPS, bytes_accessed=COST, transcendentals=TRANS) if name in ("halves", "join", "add", "total") else None,
        input_output_aliases={len(args) + i: i for i in range(len(onto))},
        name=name,
    )(*args, *onto)


def body(x_in, lengths, bn_gain, bn_bias, w_in, decay_rate, phase, w_out, skip_gain, w_glu, b_glu, grad_out):
    rows, steps, width = x_in.shape
    z = Sizes(rows, steps, width, w_in.shape[2] // 2, lax.axis_size("tm"), lax.axis_size("rows"), lengths.shape[1])
    T, D, N = z.T, z.D, z.N
    everyone = ("tm", "rows")

    def swap(a, axis):
        return lax.all_to_all(a, axis, 0, 0)

    stat_shape = ((z.all, z.stat, LANES), F32)
    send_shape = ((z.tm, z.packed, LANES), F32)
    tile = ((z.packed, LANES), F32)
    stat_tile = ((z.stat, LANES), F32)
    full, low = ((T, D), F32), ((T, D), BF16)
    full_n, low_n = ((T, 2 * N), F32), ((T, 2 * N), BF16)
    chunk = ((z.R * CHUNKS, 2 * N), F32)
    mask = ((T, LANES), F32)
    chunk_mask = ((z.R * CHUNKS, LANES), F32)
    norm_shape = ((8, D), F32)
    small_shape = ((8, D), F32)
    lam_shape = ((8, N), F32)
    wide_f, wide_b = ((T, 2 * D), F32), ((T, 2 * D), BF16)
    bind = functools.partial

    natural = ((D // LANES, T, LANES), F32)
    (x, gout, stat0, keep_f, keep_r, chunk_f, chunk_r, dev_f, dev_r, tab, power,
     bn_gain, bn_bias, skip_gain, b_glu, w_in, w_out, w_glu) = run(
        bind(prepare, z), "prepare",
        [full, full, stat_shape, mask, mask, chunk_mask, chunk_mask, send_shape, send_shape, ((16, N), F32), ((4, z.packed, LANES), F32)]
        + [(a.shape, a.dtype) for a in (bn_gain, bn_bias, skip_gain, b_glu, w_in, w_out, w_glu)],
        (lengths, x_in.reshape(T, D), grad_out.reshape(T, D), decay_rate, phase, bn_gain, bn_bias, skip_gain, b_glu, w_in, w_out, w_glu),
        [stat_tile, natural, low, low, ((2, N), F32), ((2, N), F32), (lengths.shape, jnp.int32)], sems=12, source=pltpu.HBM)
    stat0 = swap(stat0, everyone)
    norm0, low0, proj0, ends0, send0 = run(
        bind(enter, z, 0), "enter0", [norm_shape, low, full_n, chunk, send_shape],
        (stat0, x, bn_gain, bn_bias, w_in, keep_f, chunk_f, tab), [stat_tile, tile])
    send0 = swap(send0, "tm")
    h0, hlow0, carry0, slope0, act0, sig0, gate0, v1, stat1 = run(
        bind(middle, z), "middle", [full_n, low_n, chunk, full, low, full, full, full, stat_shape],
        (send0, dev_f, power, ends0, chunk_f, proj0, keep_f, tab, x, norm0, bn_gain, bn_bias, skip_gain, w_out, w_glu, b_glu),
        [tile, wide_f, stat_tile])
    stat1 = swap(stat1, everyone)
    norm1, low1, proj1, ends1, send1 = run(
        bind(enter, z, 1), "enter1", [norm_shape, low, full_n, chunk, send_shape],
        (stat1, v1, bn_gain, bn_bias, w_in, keep_r, chunk_r, tab), [stat_tile, tile])
    send1 = swap(send1, "tm")
    W = STRIP if D * D // STRIP % (8 * z.all) == 0 else LANES

    def part(count, extra=0):
        return ((count * D // W * D // 2 + extra, W), F32)

    def tie(*values):
        return lax.optimization_barrier(values)

    h1, carry1, v2, dy1, dh1, adj_ends1, adj1, small1, keep1, send1 = run(
        bind(turn, z), "turn",
        [full_n, chunk, full, full, full_n, chunk, send_shape, small_shape, part(3), part(3)],
        (send1, dev_r, power, ends1, chunk_r, proj1, keep_r, tab, v1, norm1, bn_gain, bn_bias, skip_gain, w_out, w_glu, b_glu, gout,
         keep_f, chunk_f), [tile, wide_f, full, low_n, low, wide_b, low])
    one = Exchange(z, keep1, send1, order=ORDERS[0], flat=FLAT[0])
    one.send, adj1 = tie(one.send, adj1)
    one.go()
    adj1 = swap(adj1, "tm")
    one.got, adj1 = tie(one.got, adj1)
    one.settle()
    dxn1, dplow1, sum1, lam1 = run(
        bind(finish_upper, z), "finish1", [full, low_n, stat_shape, lam_shape],
        (adj1, dev_f, power, adj_ends1, chunk_f, dh1, keep_f, tab, proj1, h1, carry1, keep_r, dy1, v1, norm1, skip_gain, w_in),
        [tile, chunk, stat_tile])
    one.send, sum1 = tie(one.send, sum1)
    one.go()
    sum1 = swap(sum1, everyone)
    one.got, sum1 = tie(one.got, sum1)
    one.settle()
    total1, e1, dy0, dh0, adj_ends0, adj0, small0, keepa, senda = run(
        bind(lower_block, z), "lower_block",
        [norm_shape, full, full, full_n, chunk, send_shape, small_shape, part(3), part(3)],
        (sum1, dxn1, v1, norm1, gout, sig0, gate0, slope0, x, norm0, bn_gain, bn_bias, w_glu, w_out, keep_r, chunk_r, tab, act0, hlow0),
        [tile, stat_tile, wide_b, low])
    two = Exchange(z, keepa, senda, order=ORDERS[1], flat=FLAT[1])
    one.send, two.send, adj0 = tie(one.send, two.send, adj0)
    one.go()
    two.go()
    adj0 = swap(adj0, "tm")
    one.got, two.got, adj0 = tie(one.got, two.got, adj0)
    rows_sum = (2 * D + 2 * (3 * D + 2 * N)) // W
    z.extra = -(-rows_sum // 8) * 8
    last_part = part(2, z.extra)
    dxn0, keepb, sendb = run(
        bind(finish_lower, z), "finish0", [full, last_part, last_part],
        (adj0, dev_r, power, adj_ends0, chunk_r, dh0, keep_r, tab, proj0, h0, carry0, keep_f, dy0, x, norm0, skip_gain, w_in,
         low0, low1, dplow1, small0, small1, lam1),
        [low_n, lam_shape, tile, chunk])
    one.settle()
    two.settle()
    three = Exchange(z, keepb, sendb, z.extra, ORDERS[2], FLAT[2])
    one.send, two.send, three.send = tie(one.send, two.send, three.send)
    for e in (one, two, three):
        e.go()
    sets = (one, two, three)
    ahead = three.send
    placed, done, queue = (), [], list(FIRST) if z.bits == 5 else []
    while len(done) < len(sets):
        for i in queue or SEQ:
            e = sets[i]
            if i in done:
                continue
            e.got, _ = tie(e.got, ahead)
            if e.closing:
                placed = run(
                    bind(assemble, z, i), "assemble", [((2, D, 2 * N), F32), ((2, 2 * N, D), F32), ((2, D, 2 * D), F32)],
                    (e.keep, e.got), sems=8 * (STRIP // W), target=pltpu.HBM, onto=placed)
                ahead = placed[0]
                done.append(i)
            else:
                e.settle()
                e.go()
                ahead = e.send
        queue = []
    sums = (((2, D), F32), ((2, D), F32), ((2, N), F32), ((2, N), F32), ((2, D), F32), ((2, 2 * D), F32))
    out, grad_x, gain_out, bias_out, rate_out, phase_out, skip_out, bglu_out = run(
        bind(last, z), "last", [low, full, *sums], (three.small, dxn0, x, norm0, bn_gain, e1, total1, v2), [natural, full])
    gwin, gwout, gwglu = placed
    return (
        out.reshape(rows, steps, width),
        grad_x.reshape(rows, steps, width),
        gain_out,
        bias_out,
        gwin,
        rate_out,
        phase_out,
        gwout,
        skip_out,
        gwglu,
        bglu_out,
    )


def solution(mesh):
    split, rep = P("rows", "tm", None), P()
    return jax.shard_map(
        body,
        mesh=mesh,
        in_specs=(split, P("rows", None)) + (rep,) * 9 + (split,),
        out_specs=(split, split) + (rep,) * 9,
        check_vma=False,
    )
```

```python
import functools
import math

import jax
import jax.numpy as jnp
from jax import lax
from jax.experimental import pallas as pl
from jax.experimental.pallas import tpu as pltpu
from jax.sharding import PartitionSpec as P

EPS = 1e-05
LANES = 128
CHUNKS = 8
TILE = 128
F32 = jnp.float32
BF16 = jnp.bfloat16
ROOT_HALF = 0.7071067811865476
ROOT_TWO_PI_INV = 0.3989422804014327


class Sizes:
    def __init__(self, rows, steps, width, states, count_tm, count_rows, per_row):
        self.R, self.S, self.D, self.N = rows, steps, width, states
        self.T = rows * steps
        self.L = steps // CHUNKS
        self.tm, self.rows = count_tm, count_rows
        self.all = count_tm * count_rows
        self.seqs = per_row
        self.half = states // LANES
        self.packed = rows * 2 * self.half
        self.stat = 2 * width // LANES
        self.tokens = self.T * self.all
        self.bits = self.all.bit_length() - 1
        self.extra = 0


def dot(a, b):
    return jnp.dot(a, b, preferred_element_type=F32)


def dot_t(a, b):
    return lax.dot_general(a, b, (((1,), (1,)), ((), ())), preferred_element_type=F32)


def dot_0(a, b):
    return lax.dot_general(a, b, (((0,), (0,)), ((), ())), preferred_element_type=F32)


def fold(a):
    return a.reshape(a.shape[0] // 8, 8, a.shape[1]).sum(0)


def wide(a, z):
    return jnp.concatenate([a] * z.half, axis=1)


def tiles(z, body, carry):
    def one(i, c):
        return body(pl.ds(pl.multiple_of(i * TILE, TILE), TILE), c)

    return lax.fori_loop(0, z.T // TILE, one, carry)


def pack(ref, rows, k=0):
    w = ref.shape[1]
    for row in rows:
        for i in range(row.shape[1] // w):
            ref[k : k + 1, :] = row[:, i * w : (i + 1) * w]
            k += 1
    return k


def unpack(ref, first, count):
    return jnp.concatenate([ref[first + i : first + i + 1, :] for i in range(count)], axis=1)


def spread(out_ref, tile_ref):
    value = tile_ref[...]
    for j in range(out_ref.shape[0]):
        out_ref[j] = value


def two_sums(recv_ref, tile_ref, z):
    tile_ref[...] = jnp.sum(recv_ref[...], axis=0)
    n = z.D // LANES
    return unpack(tile_ref, 0, n), unpack(tile_ref, n, n)


def step_rows(z, r, s):
    first = r * z.S + s * CHUNKS
    return slice(first, first + CHUNKS)


def to_steps(z, source, out_ref, natural_ref):
    lanes = z.D // LANES

    def split(rows, c):
        value = source(rows)
        for k in range(lanes):
            natural_ref[k, rows, :] = value[:, k * LANES : (k + 1) * LANES]
        return c

    tiles(z, split, 0)
    for r in range(z.R):
        for s in range(z.L):
            for k in range(lanes):
                out_ref[step_rows(z, r, s), k * LANES : (k + 1) * LANES] = natural_ref[k, pl.ds(r * z.S + s, CHUNKS, stride=z.L), :]


def to_time(z, source_ref, out_ref, natural_ref):
    lanes = z.D // LANES
    for r in range(z.R):
        for s in range(z.L):
            for k in range(lanes):
                natural_ref[k, pl.ds(r * z.S + s, CHUNKS, stride=z.L), :] = source_ref[step_rows(z, r, s), k * LANES : (k + 1) * LANES]

    def join(rows, c):
        value = jnp.concatenate([natural_ref[k, rows, :] for k in range(lanes)], axis=1)
        out_ref[rows, :] = value.astype(out_ref.dtype)
        return c

    tiles(z, join, 0)


def pair_store(z, ref):
    held = {}

    def put(r, s, re, im):
        if (r, s ^ 1) not in held:
            held[r, s] = (re, im)
            return
        other = held.pop((r, s ^ 1))
        low, high = (other, (re, im)) if s & 1 else ((re, im), other)
        rows = slice(r * z.S + (s & ~1) * CHUNKS, r * z.S + ((s & ~1) + 2) * CHUNKS)
        ref[rows, 0 : z.N] = jnp.concatenate([low[0], high[0]], axis=0).astype(ref.dtype)
        ref[rows, z.N : 2 * z.N] = jnp.concatenate([low[1], high[1]], axis=0).astype(ref.dtype)

    return put


def scan(z, drive_ref, gain, lr, li, keep_ref, state, reverse, visit=None):
    for step in range(z.L):
        s = z.L - 1 - step if reverse else step
        for r in range(z.R):
            rows = step_rows(z, r, s)
            keep = wide(keep_ref[rows, :], z)
            ur = drive_ref[rows, 0 : z.N]
            ui = drive_ref[rows, z.N : 2 * z.N]
            if gain is not None:
                ur, ui = ur * gain, ui * gain
            hr, hi = keep * state[r][0], keep * state[r][1]
            state[r] = (lr * hr - li * hi + ur, lr * hi + li * hr + ui)
            if visit is not None:
                visit(r, s, rows, *state[r])
    return state


def zeros_state(z):
    return [(jnp.zeros((CHUNKS, z.N), F32), jnp.zeros((CHUNKS, z.N), F32)) for _ in range(z.R)]


def chunk_order(reverse):
    return range(CHUNKS - 1, -1, -1) if reverse else range(CHUNKS)


def end_state(z, state, ends_ref, chunk_keep_ref, pr, pi, reverse):
    rows = []
    for r in range(z.R):
        ends_ref[r * CHUNKS : (r + 1) * CHUNKS, 0 : z.N] = state[r][0]
        ends_ref[r * CHUNKS : (r + 1) * CHUNKS, z.N : 2 * z.N] = state[r][1]
    for r in range(z.R):
        cr = ci = None
        for c in chunk_order(reverse):
            k = r * CHUNKS + c
            er, ei = ends_ref[k : k + 1, 0 : z.N], ends_ref[k : k + 1, z.N : 2 * z.N]
            if cr is None:
                cr, ci = er, ei
            else:
                keep = wide(chunk_keep_ref[k : k + 1, :], z)
                cr, ci = keep * cr, keep * ci
                cr, ci = pr * cr - pi * ci + er, pr * ci + pi * cr + ei
        rows += [cr, ci]
    return rows


def carries(z, recv_ref, device_keep_ref, power_ref, b, sign, ends_ref, chunk_keep_ref, pr, pi, tile_ref, carry_ref, reverse):
    place = lax.axis_index("tm")
    pow_re = power_ref[2 * b]
    pow_im = sign * power_ref[2 * b + 1]
    is_re = (lax.broadcasted_iota(jnp.int32, (z.packed, LANES), 0) // z.half) % 2 == 0

    def hop(i, c):
        j = z.tm - 1 - i if reverse else i
        other = jnp.where(is_re, pltpu.roll(c, z.packed - z.half, 0), pltpu.roll(c, z.half, 0))
        return device_keep_ref[j] * (pow_re * c + pow_im * other) + recv_ref[j]

    ahead = z.tm - 1 - place if reverse else place
    tile_ref[...] = lax.fori_loop(0, ahead, hop, jnp.zeros((z.packed, LANES), F32))
    for r in range(z.R):
        cr = unpack(tile_ref, r * 2 * z.half, z.half)
        ci = unpack(tile_ref, r * 2 * z.half + z.half, z.half)
        order = list(chunk_order(reverse))
        for c in order:
            k = r * CHUNKS + c
            carry_ref[k : k + 1, 0 : z.N] = cr
            carry_ref[k : k + 1, z.N : 2 * z.N] = ci
            if c != order[-1]:
                keep = wide(chunk_keep_ref[k : k + 1, :], z)
                er, ei = ends_ref[k : k + 1, 0 : z.N], ends_ref[k : k + 1, z.N : 2 * z.N]
                cr, ci = keep * cr, keep * ci
                cr, ci = pr * cr - pi * ci + er, pr * ci + pi * cr + ei
    state = []
    for r in range(z.R):
        span = slice(r * CHUNKS, (r + 1) * CHUNKS)
        state.append((carry_ref[span, 0 : z.N], carry_ref[span, z.N : 2 * z.N]))
    return state


def lam_rows(z, tab_ref, b):
    def row(i):
        return tab_ref[b * 8 + i : b * 8 + i + 1, :]

    def full(i):
        return jnp.broadcast_to(row(i), (CHUNKS, z.N))

    return full(0), full(1), full(2), row(3), row(4)


def prepare(z, len_hbm, x_hbm, gout_hbm, rate_hbm, phase_hbm, gain_hbm, bias_hbm, skip_hbm, bglu_hbm, win_hbm, wout_hbm, wglu_hbm,
            v_ref, up_ref, stat_ref, keep_f, keep_r, chunk_f, chunk_r, dev_f, dev_r, tab_ref, power_ref,
            gain_ref, bias_ref, skip_ref, bglu_ref, win_ref, wout_ref, wglu_ref,
            tile_ref, natural_ref, x_ref, gout_ref, rate_ref, phase_ref, len_ref, sem):
    moves = [(x_hbm, x_ref), (len_hbm, len_ref), (rate_hbm, rate_ref), (phase_hbm, phase_ref), (gout_hbm, gout_ref),
             (gain_hbm, gain_ref), (bias_hbm, bias_ref), (win_hbm, win_ref), (skip_hbm, skip_ref), (bglu_hbm, bglu_ref),
             (wout_hbm, wout_ref), (wglu_hbm, wglu_ref)]
    copies = [pltpu.make_async_copy(a, b, sem.at[i]) for i, (a, b) in enumerate(moves)]
    for c in copies:
        c.start()
    copies[0].wait()
    to_steps(z, lambda rows: x_ref[rows, :].astype(F32), v_ref, natural_ref)

    def body(rows, c):
        v = v_ref[rows, :]
        return c[0] + fold(v), c[1] + fold(v * v)

    zero = jnp.zeros((8, z.D), F32)
    s0, s1 = tiles(z, body, (zero, zero))
    pack(tile_ref, [jnp.sum(s0, 0, keepdims=True), jnp.sum(s1, 0, keepdims=True)])
    spread(stat_ref, tile_ref)
    for c in copies[1:5]:
        c.wait()
    to_steps(z, lambda rows: gout_ref[rows, :].astype(F32), up_ref, natural_ref)
    base = lax.axis_index("tm") * z.S
    place = lax.broadcasted_iota(jnp.int32, (z.S, LANES), 0)
    at = base + (place % CHUNKS) * z.L + place // CHUNKS
    chunk_at = base + z.L * lax.broadcasted_iota(jnp.int32, (CHUNKS, LANES), 0)
    dev_at = z.S * lax.broadcasted_iota(jnp.int32, (z.tm, LANES), 0)
    for r in range(z.R):
        end = jnp.int32(0)
        hit = [jnp.zeros(a.shape, jnp.bool_) for a in (at, at, chunk_at, chunk_at, dev_at, dev_at)]
        for q in range(z.seqs):
            start = end
            end = end + len_ref[r, q]
            last = end - 1
            hit[0] = hit[0] | (at == start)
            hit[1] = hit[1] | (at == last)
            for i, mark in ((2, start), (3, last)):
                hit[i] = hit[i] | ((chunk_at <= mark) & (mark < chunk_at + z.L))
            for i, mark in ((4, start), (5, last)):
                hit[i] = hit[i] | ((dev_at <= mark) & (mark < dev_at + z.S))
        keep = [1.0 - h.astype(F32) for h in hit]
        keep_f[r * z.S : (r + 1) * z.S, :] = keep[0]
        keep_r[r * z.S : (r + 1) * z.S, :] = keep[1]
        chunk_f[r * CHUNKS : (r + 1) * CHUNKS, :] = keep[2]
        chunk_r[r * CHUNKS : (r + 1) * CHUNKS, :] = keep[3]
        each = 2 * z.half
        for j in range(z.tm):
            for ref, k in ((dev_f, keep[4]), (dev_r, keep[5])):
                ref[j, r * each : (r + 1) * each, :] = jnp.broadcast_to(k[j : j + 1, :], (each, LANES))
    for b in range(2):
        rate, angle = rate_ref[b : b + 1, :], phase_ref[b : b + 1, :]
        size = jnp.exp(-rate)
        lr, li = size * jnp.cos(angle), size * jnp.sin(angle)
        gamma = jnp.sqrt(1.0 - jnp.exp(-2.0 * rate))

        def power(n):
            out, br, bi = None, lr, li
            while n:
                if n & 1:
                    out = (br, bi) if out is None else (out[0] * br - out[1] * bi, out[0] * bi + out[1] * br)
                br, bi = br * br - bi * bi, 2.0 * br * bi
                n >>= 1
            return out

        chunk_power, device_power = power(z.L), power(z.S)
        rows = [lr, li, gamma, chunk_power[0], chunk_power[1], jnp.exp(-2.0 * rate) / gamma]
        for i, row in enumerate(rows):
            tab_ref[b * 8 + i : b * 8 + i + 1, :] = row
        for i in range(6, 8):
            tab_ref[b * 8 + i : b * 8 + i + 1, :] = jnp.zeros_like(lr)
        pack(power_ref.at[2 * b], [device_power[0], device_power[0]] * z.R)
        pack(power_ref.at[2 * b + 1], [-device_power[1], device_power[1]] * z.R)
    for c in copies[5:]:
        c.wait()


def enter(z, b, stat_ref, v_ref, gain_ref, bias_ref, win_ref, keep_ref, chunk_ref, tab_ref,
          norm_ref, low_ref, proj_ref, ends_ref, send_ref, stat_tile, tile_ref):
    total, square = two_sums(stat_ref, stat_tile, z)
    mean = total / z.tokens
    rstd = lax.rsqrt(square / z.tokens - mean * mean + EPS)
    norm_ref[0:1, :] = mean
    norm_ref[1:2, :] = rstd
    gain, bias = gain_ref[b : b + 1, :], bias_ref[b : b + 1, :]

    def body(rows, c):
        xhat = (v_ref[rows, :] - mean) * rstd
        low_ref[rows, :] = (gain * xhat + bias).astype(BF16)
        return c

    tiles(z, body, 0)
    proj_ref[...] = dot(low_ref[...], win_ref[b])
    lr, li, gamma, pr, pi = lam_rows(z, tab_ref, b)
    state = scan(z, proj_ref, gamma, lr, li, keep_ref, zeros_state(z), b == 1)
    pack(tile_ref, end_state(z, state, ends_ref, chunk_ref, pr, pi, b == 1))
    spread(send_ref, tile_ref)


def gelu_pair(y):
    cdf = 0.5 + 0.5 * lax.erf(y * ROOT_HALF)
    return y * cdf, cdf + y * (ROOT_TWO_PI_INV * jnp.exp(-0.5 * y * y))


def mix(z, b, recv_ref, dev_ref, power_ref, ends_ref, chunk_ref, proj_ref, keep_ref, tab_ref, v_ref, norm_ref, gain_ref,
        bias_ref, skip_ref, wout_ref, wglu_ref, h_ref, hlow_ref, carry_ref, slope_ref, act_ref, tile_ref, wide_ref):
    lr, li, gamma, pr, pi = lam_rows(z, tab_ref, b)
    state = carries(z, recv_ref, dev_ref, power_ref, b, 1.0, ends_ref, chunk_ref, pr, pi, tile_ref, carry_ref, b == 1)

    put = pair_store(z, hlow_ref)

    def visit(r, s, rows, hr, hi):
        h_ref[rows, 0 : z.N] = hr
        h_ref[rows, z.N : 2 * z.N] = hi
        put(r, s, hr, hi)

    scan(z, proj_ref, gamma, lr, li, keep_ref, state, b == 1, visit)
    slope_ref[...] = dot(hlow_ref[...], wout_ref[b])
    mean, rstd = norm_ref[0:1, :], norm_ref[1:2, :]
    gain, bias, skip = gain_ref[b : b + 1, :], bias_ref[b : b + 1, :], skip_ref[b : b + 1, :]

    def body(rows, c):
        xn = gain * ((v_ref[rows, :] - mean) * rstd) + bias
        act, slope = gelu_pair(slope_ref[rows, :] + skip * xn)
        act_ref[rows, :] = act.astype(BF16)
        slope_ref[rows, :] = slope
        return c

    tiles(z, body, 0)
    wide_ref[...] = dot(act_ref[...], wglu_ref[b])


def middle(z, recv_ref, dev_ref, power_ref, ends_ref, chunk_ref, proj_ref, keep_ref, tab_ref, v_ref, norm_ref, gain_ref,
           bias_ref, skip_ref, wout_ref, wglu_ref, bglu_ref,
           h_ref, hlow_ref, carry_ref, slope_ref, act_ref, sig_ref, gate_ref, next_ref, stat_ref, tile_ref, wide_ref, stat_tile):
    mix(z, 0, recv_ref, dev_ref, power_ref, ends_ref, chunk_ref, proj_ref, keep_ref, tab_ref, v_ref, norm_ref, gain_ref,
        bias_ref, skip_ref, wout_ref, wglu_ref, h_ref, hlow_ref, carry_ref, slope_ref, act_ref, tile_ref, wide_ref)
    d = z.D
    b1, b2 = bglu_ref[0:1, 0:d], bglu_ref[0:1, d : 2 * d]

    def body(rows, c):
        z1 = wide_ref[rows, 0:d] + b1
        sig = jax.nn.sigmoid(wide_ref[rows, d : 2 * d] + b2)
        prod = z1 * sig
        sig_ref[rows, :] = sig
        gate_ref[rows, :] = prod * (1.0 - sig)
        v = v_ref[rows, :] + prod
        next_ref[rows, :] = v
        return c[0] + fold(v), c[1] + fold(v * v)

    zero = jnp.zeros((8, d), F32)
    s0, s1 = tiles(z, body, (zero, zero))
    pack(stat_tile, [jnp.sum(s0, 0, keepdims=True), jnp.sum(s1, 0, keepdims=True)])
    spread(stat_ref, stat_tile)


def descend(z, b, grad_bglu, dz_ref, slope_ref, v_ref, norm_ref, gain_ref, bias_ref, wglu_ref, wout_ref, keep_ref, chunk_ref, tab_ref,
            dy_ref, dylow_ref, dh_ref, ends_ref, send_ref, small_ref, tile_ref):
    dy_ref[...] = dot_t(dz_ref[...], wglu_ref[b])
    mean, rstd = norm_ref[0:1, :], norm_ref[1:2, :]
    gain, bias = gain_ref[b : b + 1, :], bias_ref[b : b + 1, :]

    def body(rows, c):
        xn = gain * ((v_ref[rows, :] - mean) * rstd) + bias
        dy = dy_ref[rows, :] * slope_ref[rows, :]
        dy_ref[rows, :] = dy
        dylow_ref[rows, :] = dy.astype(BF16)
        return c + fold(dy * xn)

    grad_skip = tiles(z, body, jnp.zeros((8, z.D), F32))
    small_ref[0:1, :] = jnp.sum(grad_skip, 0, keepdims=True)
    total = jnp.sum(grad_bglu, 0, keepdims=True)
    small_ref[1:2, :] = total[:, 0 : z.D]
    small_ref[2:3, :] = total[:, z.D : 2 * z.D]
    dh_ref[...] = dot_t(dylow_ref[...], wout_ref[b])
    lr, li, _, pr, pi = lam_rows(z, tab_ref, b)
    state = scan(z, dh_ref, None, lr, -li, keep_ref, zeros_state(z), b == 0)
    pack(tile_ref, end_state(z, state, ends_ref, chunk_ref, pr, -pi, b == 0))
    spread(send_ref, tile_ref)


def turn(z, recv_ref, dev_ref, power_ref, ends_ref, chunk_ref, proj_ref, keep_ref, tab_ref, v_ref, norm_ref, gain_ref,
         bias_ref, skip_ref, wout_ref, wglu_ref, bglu_ref, gout_ref, adj_keep_ref, adj_chunk_ref,
         h_ref, carry_ref, final_ref, dy_ref, dh_ref, adj_ends_ref, send_ref, small_ref, half_keep, half_send,
         tile_ref, wide_ref, slope_ref, hlow_ref, act_ref, dz_ref, dylow_ref):
    mix(z, 1, recv_ref, dev_ref, power_ref, ends_ref, chunk_ref, proj_ref, keep_ref, tab_ref, v_ref, norm_ref, gain_ref,
        bias_ref, skip_ref, wout_ref, wglu_ref, h_ref, hlow_ref, carry_ref, slope_ref, act_ref, tile_ref, wide_ref)
    d = z.D
    b1, b2 = bglu_ref[1:2, 0:d], bglu_ref[1:2, d : 2 * d]

    def body(rows, c):
        z1 = wide_ref[rows, 0:d] + b1
        sig = jax.nn.sigmoid(wide_ref[rows, d : 2 * d] + b2)
        prod = z1 * sig
        final_ref[rows, :] = v_ref[rows, :] + prod
        e = gout_ref[rows, :]
        d1, d2 = e * sig, e * (prod * (1.0 - sig))
        dz_ref[rows, 0:d] = d1.astype(BF16)
        dz_ref[rows, d : 2 * d] = d2.astype(BF16)
        return c[0] + fold(d1), c[1] + fold(d2)

    zero = jnp.zeros((8, d), F32)
    s0, s1 = tiles(z, body, (zero, zero))
    descend(z, 1, jnp.concatenate([s0, s1], axis=1), dz_ref, slope_ref, v_ref, norm_ref, gain_ref, bias_ref, wglu_ref, wout_ref,
            adj_keep_ref, adj_chunk_ref, tab_ref, dy_ref, dylow_ref, dh_ref, adj_ends_ref, send_ref, small_ref, tile_ref)
    split_strips(z, half_keep, half_send, units(act_ref, dz_ref, half_keep) + units(hlow_ref, dylow_ref, half_keep))


def finish(z, b, recv_ref, dev_ref, power_ref, ends_ref, chunk_ref, dh_ref, keep_ref, tab_ref, proj_ref, h_ref, carry_ref,
           fwd_keep_ref, dy_ref, v_ref, norm_ref, skip_ref, win_ref, emit,
           dplow_ref, dxn_ref, lam_ref, tile_ref, adj_carry_ref):
    lr, li, gamma, pr, pi = lam_rows(z, tab_ref, b)
    reverse = b == 0
    state = carries(z, recv_ref, dev_ref, power_ref, b, -1.0, ends_ref, chunk_ref, pr, -pi, tile_ref, adj_carry_ref, reverse)
    zero = jnp.zeros((CHUNKS, z.N), F32)
    sums = [zero, zero, zero]
    put = pair_store(z, dplow_ref)

    def visit(r, s, rows, gr, gi):
        put(r, s, gamma * gr, gamma * gi)
        sums[2] = sums[2] + gr * proj_ref[rows, 0 : z.N] + gi * proj_ref[rows, z.N : 2 * z.N]
        if s == (0 if b == 0 else z.L - 1):
            span = slice(r * CHUNKS, (r + 1) * CHUNKS)
            nr, ni = carry_ref[span, 0 : z.N], carry_ref[span, z.N : 2 * z.N]
        else:
            near = step_rows(z, r, s - 1 if b == 0 else s + 1)
            nr, ni = h_ref[near, 0 : z.N], h_ref[near, z.N : 2 * z.N]
        keep = wide(fwd_keep_ref[rows, :], z)
        nr, ni = keep * nr, keep * ni
        sums[0] = sums[0] + (gr * nr + gi * ni)
        sums[1] = sums[1] + (gi * nr - gr * ni)

    scan(z, dh_ref, None, lr, -li, keep_ref, state, reverse, visit)
    dr, di, dg = (jnp.sum(s, 0, keepdims=True) for s in sums)
    r0, i0 = lr[0:1, :], li[0:1, :]
    lam_ref[0:1, :] = dg * tab_ref[b * 8 + 5 : b * 8 + 6, :] - (dr * r0 + di * i0)
    lam_ref[1:2, :] = di * r0 - dr * i0

    dxn_ref[...] = dot_t(dplow_ref[...], win_ref[b])
    mean, rstd = norm_ref[0:1, :], norm_ref[1:2, :]
    skip = skip_ref[b : b + 1, :]

    def body(rows, c):
        xhat = (v_ref[rows, :] - mean) * rstd
        dxn = dxn_ref[rows, :] + skip * dy_ref[rows, :]
        dxn_ref[rows, :] = dxn
        return c[0] + fold(dxn), c[1] + fold(dxn * xhat)

    zero = jnp.zeros((8, z.D), F32)
    s0, s1 = tiles(z, body, (zero, zero))
    emit(jnp.sum(s0, 0, keepdims=True), jnp.sum(s1, 0, keepdims=True))


def norm_grad(z, b, bias_sum, gain_sum, norm_ref, gain_ref):
    mean, rstd = norm_ref[0:1, :], norm_ref[1:2, :]
    gain = gain_ref[b : b + 1, :]
    scale, shift, slope = rstd * gain, rstd * gain * bias_sum / z.tokens, rstd * gain * gain_sum / z.tokens

    def grad(dxn, v, up):
        return scale * dxn - shift - ((v - mean) * rstd) * slope + up

    return grad


def lower_block(z, stat_ref, dxn_ref, v1_ref, norm1_ref, gout_ref, sig_ref, gate_ref, slope_ref, v_ref, norm_ref, gain_ref, bias_ref,
                wglu_ref, wout_ref, keep_ref, chunk_ref, tab_ref, act_ref, hlow_ref,
                total_ref, e_ref, dy_ref, dh_ref, ends_ref, send_ref, small_ref, glu_keep, glu_send, out_keep, out_send,
                tile_ref, stat_tile, dz_ref, dylow_ref):
    bias_sum, gain_sum = two_sums(stat_ref, stat_tile, z)
    grad = norm_grad(z, 1, bias_sum, gain_sum, norm1_ref, gain_ref)
    total_ref[0:1, :] = bias_sum
    total_ref[1:2, :] = gain_sum
    d = z.D

    def body(rows, c):
        e = grad(dxn_ref[rows, :], v1_ref[rows, :], gout_ref[rows, :])
        e_ref[rows, :] = e
        d1, d2 = e * sig_ref[rows, :], e * gate_ref[rows, :]
        dz_ref[rows, 0:d] = d1.astype(BF16)
        dz_ref[rows, d : 2 * d] = d2.astype(BF16)
        return c[0] + fold(d1), c[1] + fold(d2)

    zero = jnp.zeros((8, d), F32)
    s0, s1 = tiles(z, body, (zero, zero))
    descend(z, 0, jnp.concatenate([s0, s1], axis=1), dz_ref, slope_ref, v_ref, norm_ref, gain_ref, bias_ref, wglu_ref, wout_ref,
            keep_ref, chunk_ref, tab_ref, dy_ref, dylow_ref, dh_ref, ends_ref, send_ref, small_ref, tile_ref)
    split_strips(z, glu_keep, glu_send, units(act_ref, dz_ref, glu_keep))
    split_strips(z, out_keep, out_send, units(hlow_ref, dylow_ref, out_keep))


def units(a_ref, b_ref, like):
    w = like.shape[1]

    def strip(i):
        return lambda: dot_0(a_ref[...], b_ref[:, i * w : (i + 1) * w])

    return [strip(i) for i in range(b_ref.shape[1] // w)]


def finish_upper(z, *refs):
    ins, outs = refs[:17], refs[17:]
    dxn_ref, dplow_ref, stat_ref, lam_ref, tile_ref, carry_ref, stat_tile = outs

    def emit(bias_sum, gain_sum):
        pack(stat_tile, [bias_sum, gain_sum])
        spread(stat_ref, stat_tile)

    finish(z, 1, *ins, emit, dplow_ref, dxn_ref, lam_ref, tile_ref, carry_ref)


def finish_lower(z, *refs):
    ins, (low_ref, low1_ref, dplow1_ref, small0_ref, small1_ref, lam1_ref), outs = refs[:17], refs[17:23], refs[23:]
    dxn_ref, keep_ref, send_ref, dplow_ref, lam_ref, tile_ref, carry_ref = outs
    first = keep_ref.shape[0] - z.extra

    def emit(bias_sum, gain_sum):
        sums = [bias_sum, gain_sum]
        for small, lam in ((small0_ref, lam_ref), (small1_ref, lam1_ref)):
            sums += [small[0:1, :], small[1:2, :], small[2:3, :], lam[0:1, :], lam[1:2, :]]
        for ref in (keep_ref, send_ref):
            k = pack(ref, sums, first)
            if k < ref.shape[0]:
                ref[k:, :] = jnp.zeros((ref.shape[0] - k, ref.shape[1]), F32)

    finish(z, 0, *ins, emit, dplow_ref, dxn_ref, lam_ref, tile_ref, carry_ref)
    split_strips(z, keep_ref, send_ref, units(low1_ref, dplow1_ref, keep_ref) + units(low_ref, dplow_ref, keep_ref))


def last(z, small_ref, dxn_ref, v_ref, norm_ref, gain_ref, e_ref, total1_ref, final_ref, out_ref, grad_ref, gain_out, bias_out, rate_out, phase_out, skip_out,
         bglu_out, natural_ref, work_ref):
    w = small_ref.shape[1]
    at = [0]

    def take(width):
        row = unpack(small_ref, at[0], width // w)
        at[0] += width // w
        return row

    bias_sum, gain_sum = take(z.D), take(z.D)
    grad = norm_grad(z, 0, bias_sum, gain_sum, norm_ref, gain_ref)
    bias_out[0:1, :] = bias_sum
    gain_out[0:1, :] = gain_sum
    bias_out[1:2, :] = total1_ref[0:1, :]
    gain_out[1:2, :] = total1_ref[1:2, :]
    for b in range(2):
        for ref, width in ((skip_out, z.D), (bglu_out, 2 * z.D), (rate_out, z.N), (phase_out, z.N)):
            ref[b : b + 1, :] = take(width)

    def body(rows, c):
        work_ref[rows, :] = grad(dxn_ref[rows, :], v_ref[rows, :], e_ref[rows, :])
        return c

    tiles(z, body, 0)
    to_time(z, work_ref, grad_ref, natural_ref)
    to_time(z, final_ref, out_ref, natural_ref)


GRAD_TILE = 64
SEQ = (0, 2, 1, 3)
FIRST = ()
COST = 1
FLOPS = 20000000000
HINTED = ("halves", "join", "add", "total", "finish1", "lower_block", "finish0")
TRANS = 0
FLAT = (1, 1, 1, 1)
ORDERS = ((0, 1, 2, 3, 4), (0, 1, 2, 3, 4), (0, 1, 2, 3, 4), (0, 3, 1, 2, 4))
STRIP = 256


def bit_of(z, place, parity):
    if place in (1, 2) and z.bits > 2:
        return place if parity else 3 - place
    return place


def own_bit(z, place):
    me = lax.axis_index("tm") * z.rows + lax.axis_index("rows")
    odd = me % 2
    return (me >> (odd * bit_of(z, place, 1) + (1 - odd) * bit_of(z, place, 0))) % 2


def pairs(z, place):
    return [(i, i ^ (1 << bit_of(z, place, i % 2))) for i in range(z.all)]


def split_strips(z, keep_ref, send_ref, strips):
    bit = own_bit(z, 0)
    cut = len(strips) // 2

    def write(ref, products):
        for i, product in enumerate(products):
            ref[i * z.D : (i + 1) * z.D, :] = product()

    @pl.when(bit == 0)
    def _():
        write(keep_ref, strips[:cut])
        write(send_ref, strips[cut:])

    @pl.when(bit == 1)
    def _():
        write(keep_ref, strips[cut:])
        write(send_ref, strips[:cut])


def strips_of(n):
    size = math.gcd(GRAD_TILE, n)

    def rows(part, i):
        return pl.ds(pl.multiple_of(part * n + i * size, math.gcd(size, 8)), size)

    return n // size, rows


def halves(z, step, extra, keep_ref, recv_ref, next_ref, send_ref):
    n = next_ref.shape[0] - extra
    bit = own_bit(z, step)
    count, rows = strips_of(n)

    def one(i, c):
        for ref, part in ((send_ref, 1 - bit), (next_ref, bit)):
            ref[rows(0, i), :] = keep_ref[rows(part, i), :] + recv_ref[rows(part, i), :]
        return c

    lax.fori_loop(0, count, one, 0)
    if extra:
        both = keep_ref[2 * n :, :] + recv_ref[2 * n :, :]
        next_ref[n:, :] = both
        send_ref[n:, :] = both


def total(extra, keep_ref, recv_ref, out_ref, *extra_ref):
    n = out_ref.shape[0]
    out_ref[...] = keep_ref[0:n, :] + recv_ref[0:n, :]
    if extra:
        extra_ref[0][...] = keep_ref[n:, :] + recv_ref[n:, :]


def join(z, step, own_ref, recv_ref, out_ref):
    n = own_ref.shape[0]
    bit = own_bit(z, step)
    count, rows = strips_of(n)

    def one(i, c):
        for ref, part in ((own_ref, bit), (recv_ref, 1 - bit)):
            out_ref[rows(part, i), :] = ref[rows(0, i), :]
        return c

    lax.fori_loop(0, count, one, 0)


def add(keep_ref, recv_ref, out_ref):
    out_ref[...] = keep_ref[...] + recv_ref[...]


class Exchange:
    def __init__(self, z, keep, send, extra=0, order=(), flat=1):
        self.z, self.keep, self.send, self.extra = z, keep, send, extra
        self.order = order if len(order) == z.bits else tuple(range(z.bits))
        self.width = keep.shape[1]
        self.small = None
        deep = z.bits - flat
        self.plan = [("halve", i) for i in range(deep)] + [("sum", i) for i in range(deep, z.bits)] + [("double", i) for i in range(deep - 1, -1, -1)]

    def go(self):
        self.got = lax.ppermute(self.send, ("tm", "rows"), pairs(self.z, self.order[self.plan[0][1]]))

    def settle(self):
        z, x = self.z, self.extra
        (kind, i), (after, j) = self.plan.pop(0), self.plan[0]
        n = self.keep.shape[0]
        both = (self.keep, self.got)
        if kind == "double":
            (self.keep,) = run(functools.partial(join, z, self.order[i]), "join", [((2 * n, self.width), F32)], both)
        elif after == "halve":
            half = (((n - x) // 2 + x, self.width), F32)
            self.keep, self.send = run(functools.partial(halves, z, self.order[j], x), "halves", [half, half], both)
            return
        elif after == "double" and x:
            self.keep, self.small = run(functools.partial(total, x), "total", [((n - x, self.width), F32), ((x, self.width), F32)], both)
        else:
            (self.keep,) = run(add, "add", [((n, self.width), F32)], both)
        self.send = self.keep

    @property
    def closing(self):
        return len(self.plan) == 1


def assemble(z, which, *refs):
    own, got, (win_out, wout_out, wglu_out, sem) = refs[0], refs[1], refs[-4:]
    bit = own_bit(z, 0)
    w = own.shape[1]

    def strips(out, b):
        return [out.at[b, :, i * w : (i + 1) * w] for i in range(out.shape[2] // w)]

    outs = (
        lambda: strips(wglu_out, 1) + strips(wout_out, 1),
        lambda: strips(wglu_out, 0),
        lambda: strips(win_out, 1) + strips(win_out, 0),
        lambda: strips(wout_out, 0),
    )[which]()
    cut = len(outs) // 2

    def place(low, high):
        copies = []
        for ref, part in ((low, outs[:cut]), (high, outs[cut:])):
            for k, out in enumerate(part):
                copies.append(pltpu.make_async_copy(ref.at[k * z.D : (k + 1) * z.D, :], out, sem.at[len(copies)]))
        for c in copies:
            c.start()
        for c in copies:
            c.wait()

    @pl.when(bit == 0)
    def _():
        place(own, got)

    @pl.when(bit == 1)
    def _():
        place(got, own)


def run(kernel, name, outs, args, scratch=(), sems=0, source=pltpu.VMEM, target=pltpu.VMEM, onto=()):
    if source is pltpu.HBM:
        args = [pltpu.with_memory_space_constraint(a, source) for a in args]
    shapes = [pltpu.VMEM(s, t) if t != jnp.int32 else pltpu.SMEM(s, t) for s, t in scratch]
    return pl.pallas_call(
        kernel,
        out_shape=[jax.ShapeDtypeStruct(s, t) for s, t in outs],
        in_specs=[pl.BlockSpec(memory_space=source)] * len(args) + [pl.BlockSpec(memory_space=target)] * len(onto),
        out_specs=[pl.BlockSpec(memory_space=target)] * len(outs),
        scratch_shapes=shapes + ([pltpu.SemaphoreType.DMA((sems,))] if sems else []),
        compiler_params=pltpu.CompilerParams(vmem_limit_bytes=16 << 20),
        cost_estimate=pl.CostEstimate(flops=FLOPS, bytes_accessed=COST, transcendentals=TRANS) if name in HINTED else None,
        input_output_aliases={len(args) + i: i for i in range(len(onto))},
        name=name,
    )(*args, *onto)


def body(x_in, lengths, bn_gain, bn_bias, w_in, decay_rate, phase, w_out, skip_gain, w_glu, b_glu, grad_out):
    rows, steps, width = x_in.shape
    z = Sizes(rows, steps, width, w_in.shape[2] // 2, lax.axis_size("tm"), lax.axis_size("rows"), lengths.shape[1])
    T, D, N = z.T, z.D, z.N
    everyone = ("tm", "rows")

    def swap(a, axis):
        return lax.all_to_all(a, axis, 0, 0)

    stat_shape = ((z.all, z.stat, LANES), F32)
    send_shape = ((z.tm, z.packed, LANES), F32)
    tile = ((z.packed, LANES), F32)
    stat_tile = ((z.stat, LANES), F32)
    full, low = ((T, D), F32), ((T, D), BF16)
    full_n, low_n = ((T, 2 * N), F32), ((T, 2 * N), BF16)
    chunk = ((z.R * CHUNKS, 2 * N), F32)
    mask = ((T, LANES), F32)
    chunk_mask = ((z.R * CHUNKS, LANES), F32)
    norm_shape = ((8, D), F32)
    small_shape = ((8, D), F32)
    lam_shape = ((8, N), F32)
    wide_f, wide_b = ((T, 2 * D), F32), ((T, 2 * D), BF16)
    bind = functools.partial

    natural = ((D // LANES, T, LANES), F32)
    (x, gout, stat0, keep_f, keep_r, chunk_f, chunk_r, dev_f, dev_r, tab, power,
     bn_gain, bn_bias, skip_gain, b_glu, w_in, w_out, w_glu) = run(
        bind(prepare, z), "prepare",
        [full, full, stat_shape, mask, mask, chunk_mask, chunk_mask, send_shape, send_shape, ((16, N), F32), ((4, z.packed, LANES), F32)]
        + [(a.shape, a.dtype) for a in (bn_gain, bn_bias, skip_gain, b_glu, w_in, w_out, w_glu)],
        (lengths, x_in.reshape(T, D), grad_out.reshape(T, D), decay_rate, phase, bn_gain, bn_bias, skip_gain, b_glu, w_in, w_out, w_glu),
        [stat_tile, natural, low, low, ((2, N), F32), ((2, N), F32), (lengths.shape, jnp.int32)], sems=12, source=pltpu.HBM)
    stat0 = swap(stat0, everyone)
    norm0, low0, proj0, ends0, send0 = run(
        bind(enter, z, 0), "enter0", [norm_shape, low, full_n, chunk, send_shape],
        (stat0, x, bn_gain, bn_bias, w_in, keep_f, chunk_f, tab), [stat_tile, tile])
    send0 = swap(send0, "tm")
    h0, hlow0, carry0, slope0, act0, sig0, gate0, v1, stat1 = run(
        bind(middle, z), "middle", [full_n, low_n, chunk, full, low, full, full, full, stat_shape],
        (send0, dev_f, power, ends0, chunk_f, proj0, keep_f, tab, x, norm0, bn_gain, bn_bias, skip_gain, w_out, w_glu, b_glu),
        [tile, wide_f, stat_tile])
    stat1 = swap(stat1, everyone)
    norm1, low1, proj1, ends1, send1 = run(
        bind(enter, z, 1), "enter1", [norm_shape, low, full_n, chunk, send_shape],
        (stat1, v1, bn_gain, bn_bias, w_in, keep_r, chunk_r, tab), [stat_tile, tile])
    send1 = swap(send1, "tm")
    W = STRIP if D * D // STRIP % (8 * z.all) == 0 else LANES

    def part(count, extra=0):
        return ((count * D // W * D // 2 + extra, W), F32)

    def tie(*values):
        return lax.optimization_barrier(values)

    h1, carry1, v2, dy1, dh1, adj_ends1, adj1, small1, keep1, send1 = run(
        bind(turn, z), "turn",
        [full_n, chunk, full, full, full_n, chunk, send_shape, small_shape, part(3), part(3)],
        (send1, dev_r, power, ends1, chunk_r, proj1, keep_r, tab, v1, norm1, bn_gain, bn_bias, skip_gain, w_out, w_glu, b_glu, gout,
         keep_f, chunk_f), [tile, wide_f, full, low_n, low, wide_b, low])
    one = Exchange(z, keep1, send1, order=ORDERS[0], flat=FLAT[0])
    one.send, adj1 = tie(one.send, adj1)
    one.go()
    adj1 = swap(adj1, "tm")
    one.got, adj1 = tie(one.got, adj1)
    one.settle()
    _, adj1 = tie(one.send, adj1)
    dxn1, dplow1, sum1, lam1 = run(
        bind(finish_upper, z), "finish1", [full, low_n, stat_shape, lam_shape],
        (adj1, dev_f, power, adj_ends1, chunk_f, dh1, keep_f, tab, proj1, h1, carry1, keep_r, dy1, v1, norm1, skip_gain, w_in),
        [tile, chunk, stat_tile])
    _, sum1 = tie(one.send, sum1)
    one.go()
    sum1 = swap(sum1, everyone)
    one.got, sum1 = tie(one.got, sum1)
    one.settle()
    _, sum1 = tie(one.send, sum1)
    total1, e1, dy0, dh0, adj_ends0, adj0, small0, keepa, senda, keepo, sendo = run(
        bind(lower_block, z), "lower_block",
        [norm_shape, full, full, full_n, chunk, send_shape, small_shape, part(2), part(2), part(1), part(1)],
        (sum1, dxn1, v1, norm1, gout, sig0, gate0, slope0, x, norm0, bn_gain, bn_bias, w_glu, w_out, keep_r, chunk_r, tab, act0, hlow0),
        [tile, stat_tile, wide_b, low])
    two = Exchange(z, keepa, senda, order=ORDERS[1], flat=FLAT[1])
    four = Exchange(z, keepo, sendo, order=ORDERS[3], flat=FLAT[3])
    *_, adj0 = tie(one.send, two.send, four.send, adj0)
    one.go()
    two.go()
    four.go()
    adj0 = swap(adj0, "tm")
    one.got, two.got, four.got, adj0 = tie(one.got, two.got, four.got, adj0)
    rows_sum = (2 * D + 2 * (3 * D + 2 * N)) // W
    z.extra = -(-rows_sum // 8) * 8
    last_part = part(2, z.extra)
    dxn0, keepb, sendb = run(
        bind(finish_lower, z), "finish0", [full, last_part, last_part],
        (adj0, dev_r, power, adj_ends0, chunk_r, dh0, keep_r, tab, proj0, h0, carry0, keep_f, dy0, x, norm0, skip_gain, w_in,
         low0, low1, dplow1, small0, small1, lam1),
        [low_n, lam_shape, tile, chunk])
    one.settle()
    two.settle()
    four.settle()
    three = Exchange(z, keepb, sendb, z.extra, ORDERS[2], FLAT[2])
    for e in (one, two, four, three):
        e.go()
    sets = (one, two, three, four)
    ahead = three.send
    placed, done, queue = (), [], list(FIRST) if z.bits == 5 else []
    while len(done) < len(sets):
        for i in queue or SEQ:
            e = sets[i]
            if i in done:
                continue
            e.got, _ = tie(e.got, ahead)
            if e.closing:
                placed = run(
                    bind(assemble, z, i), "assemble", [((2, D, 2 * N), F32), ((2, 2 * N, D), F32), ((2, D, 2 * D), F32)],
                    (e.keep, e.got), sems=8 * (STRIP // W), target=pltpu.HBM, onto=placed)
                ahead = placed[0]
                done.append(i)
            else:
                e.settle()
                e.go()
                ahead = e.send
        queue = []
    sums = (((2, D), F32), ((2, D), F32), ((2, N), F32), ((2, N), F32), ((2, D), F32), ((2, 2 * D), F32))
    out, grad_x, gain_out, bias_out, rate_out, phase_out, skip_out, bglu_out = run(
        bind(last, z), "last", [low, full, *sums], (three.small, dxn0, x, norm0, bn_gain, e1, total1, v2), [natural, full])
    gwin, gwout, gwglu = placed
    return (
        out.reshape(rows, steps, width),
        grad_x.reshape(rows, steps, width),
        gain_out,
        bias_out,
        gwin,
        rate_out,
        phase_out,
        gwout,
        skip_out,
        gwglu,
        bglu_out,
    )


def solution(mesh):
    split, rep = P("rows", "tm", None), P()
    return jax.shard_map(
        body,
        mesh=mesh,
        in_specs=(split, P("rows", None)) + (rep,) * 9 + (split,),
        out_specs=(split, split) + (rep,) * 9,
        check_vma=False,
    )
```

```python
import functools
import math

import jax
import jax.numpy as jnp
from jax import lax
from jax.experimental import pallas as pl
from jax.experimental.pallas import tpu as pltpu
from jax.sharding import PartitionSpec as P

EPS = 1e-05
LANES = 128
CHUNKS = 8
TILE = 128
F32 = jnp.float32
BF16 = jnp.bfloat16
ROOT_HALF = 0.7071067811865476
ROOT_TWO_PI_INV = 0.3989422804014327


class Sizes:
    def __init__(self, rows, steps, width, states, count_tm, count_rows, per_row):
        self.R, self.S, self.D, self.N = rows, steps, width, states
        self.T = rows * steps
        self.L = steps // CHUNKS
        self.tm, self.rows = count_tm, count_rows
        self.all = count_tm * count_rows
        self.seqs = per_row
        self.half = states // LANES
        self.packed = rows * 2 * self.half
        self.stat = 2 * width // LANES
        self.tokens = self.T * self.all
        self.bits = self.all.bit_length() - 1
        self.extra = 0


def dot(a, b):
    return jnp.dot(a, b, preferred_element_type=F32)


def dot_t(a, b):
    return lax.dot_general(a, b, (((1,), (1,)), ((), ())), preferred_element_type=F32)


def dot_0(a, b):
    return lax.dot_general(a, b, (((0,), (0,)), ((), ())), preferred_element_type=F32)


def fold(a):
    return a.reshape(a.shape[0] // 8, 8, a.shape[1]).sum(0)


def wide(a, z):
    return jnp.concatenate([a] * z.half, axis=1)


def tiles(z, body, carry):
    def one(i, c):
        return body(pl.ds(pl.multiple_of(i * TILE, TILE), TILE), c)

    return lax.fori_loop(0, z.T // TILE, one, carry)


def pack(ref, rows, k=0):
    w = ref.shape[1]
    for row in rows:
        for i in range(row.shape[1] // w):
            ref[k : k + 1, :] = row[:, i * w : (i + 1) * w]
            k += 1
    return k


def unpack(ref, first, count):
    return jnp.concatenate([ref[first + i : first + i + 1, :] for i in range(count)], axis=1)


def spread(out_ref, tile_ref):
    value = tile_ref[...]
    for j in range(out_ref.shape[0]):
        out_ref[j] = value


def two_sums(recv_ref, tile_ref, z):
    tile_ref[...] = jnp.sum(recv_ref[...], axis=0)
    n = z.D // LANES
    return unpack(tile_ref, 0, n), unpack(tile_ref, n, n)


def step_rows(z, r, s):
    first = r * z.S + s * CHUNKS
    return slice(first, first + CHUNKS)


def to_steps(z, source, out_ref, natural_ref):
    lanes = z.D // LANES

    def split(rows, c):
        value = source(rows)
        for k in range(lanes):
            natural_ref[k, rows, :] = value[:, k * LANES : (k + 1) * LANES]
        return c

    tiles(z, split, 0)
    for r in range(z.R):
        for s in range(z.L):
            for k in range(lanes):
                out_ref[step_rows(z, r, s), k * LANES : (k + 1) * LANES] = natural_ref[k, pl.ds(r * z.S + s, CHUNKS, stride=z.L), :]


def to_time(z, source_ref, out_ref, natural_ref):
    lanes = z.D // LANES
    for r in range(z.R):
        for s in range(z.L):
            for k in range(lanes):
                natural_ref[k, pl.ds(r * z.S + s, CHUNKS, stride=z.L), :] = source_ref[step_rows(z, r, s), k * LANES : (k + 1) * LANES]

    def join(rows, c):
        value = jnp.concatenate([natural_ref[k, rows, :] for k in range(lanes)], axis=1)
        out_ref[rows, :] = value.astype(out_ref.dtype)
        return c

    tiles(z, join, 0)


def pair_store(z, ref):
    held = {}

    def put(r, s, re, im):
        if (r, s ^ 1) not in held:
            held[r, s] = (re, im)
            return
        other = held.pop((r, s ^ 1))
        low, high = (other, (re, im)) if s & 1 else ((re, im), other)
        rows = slice(r * z.S + (s & ~1) * CHUNKS, r * z.S + ((s & ~1) + 2) * CHUNKS)
        ref[rows, 0 : z.N] = jnp.concatenate([low[0], high[0]], axis=0).astype(ref.dtype)
        ref[rows, z.N : 2 * z.N] = jnp.concatenate([low[1], high[1]], axis=0).astype(ref.dtype)

    return put


def scan(z, drive_ref, gain, lr, li, keep_ref, state, reverse, visit=None):
    for step in range(z.L):
        s = z.L - 1 - step if reverse else step
        for r in range(z.R):
            rows = step_rows(z, r, s)
            keep = wide(keep_ref[rows, :], z)
            ur = drive_ref[rows, 0 : z.N]
            ui = drive_ref[rows, z.N : 2 * z.N]
            if gain is not None:
                ur, ui = ur * gain, ui * gain
            hr, hi = keep * state[r][0], keep * state[r][1]
            state[r] = (lr * hr - li * hi + ur, lr * hi + li * hr + ui)
            if visit is not None:
                visit(r, s, rows, *state[r])
    return state


def zeros_state(z):
    return [(jnp.zeros((CHUNKS, z.N), F32), jnp.zeros((CHUNKS, z.N), F32)) for _ in range(z.R)]


def chunk_order(reverse):
    return range(CHUNKS - 1, -1, -1) if reverse else range(CHUNKS)


def end_state(z, state, ends_ref, chunk_keep_ref, pr, pi, reverse):
    rows = []
    for r in range(z.R):
        ends_ref[r * CHUNKS : (r + 1) * CHUNKS, 0 : z.N] = state[r][0]
        ends_ref[r * CHUNKS : (r + 1) * CHUNKS, z.N : 2 * z.N] = state[r][1]
    for r in range(z.R):
        cr = ci = None
        for c in chunk_order(reverse):
            k = r * CHUNKS + c
            er, ei = ends_ref[k : k + 1, 0 : z.N], ends_ref[k : k + 1, z.N : 2 * z.N]
            if cr is None:
                cr, ci = er, ei
            else:
                keep = wide(chunk_keep_ref[k : k + 1, :], z)
                cr, ci = keep * cr, keep * ci
                cr, ci = pr * cr - pi * ci + er, pr * ci + pi * cr + ei
        rows += [cr, ci]
    return rows


def carries(z, recv_ref, device_keep_ref, power_ref, b, sign, ends_ref, chunk_keep_ref, pr, pi, tile_ref, carry_ref, reverse):
    place = lax.axis_index("tm")
    pow_re = power_ref[2 * b]
    pow_im = sign * power_ref[2 * b + 1]
    is_re = (lax.broadcasted_iota(jnp.int32, (z.packed, LANES), 0) // z.half) % 2 == 0

    def hop(i, c):
        j = z.tm - 1 - i if reverse else i
        other = jnp.where(is_re, pltpu.roll(c, z.packed - z.half, 0), pltpu.roll(c, z.half, 0))
        return device_keep_ref[j] * (pow_re * c + pow_im * other) + recv_ref[j]

    ahead = z.tm - 1 - place if reverse else place
    tile_ref[...] = lax.fori_loop(0, ahead, hop, jnp.zeros((z.packed, LANES), F32))
    for r in range(z.R):
        cr = unpack(tile_ref, r * 2 * z.half, z.half)
        ci = unpack(tile_ref, r * 2 * z.half + z.half, z.half)
        order = list(chunk_order(reverse))
        for c in order:
            k = r * CHUNKS + c
            carry_ref[k : k + 1, 0 : z.N] = cr
            carry_ref[k : k + 1, z.N : 2 * z.N] = ci
            if c != order[-1]:
                keep = wide(chunk_keep_ref[k : k + 1, :], z)
                er, ei = ends_ref[k : k + 1, 0 : z.N], ends_ref[k : k + 1, z.N : 2 * z.N]
                cr, ci = keep * cr, keep * ci
                cr, ci = pr * cr - pi * ci + er, pr * ci + pi * cr + ei
    state = []
    for r in range(z.R):
        span = slice(r * CHUNKS, (r + 1) * CHUNKS)
        state.append((carry_ref[span, 0 : z.N], carry_ref[span, z.N : 2 * z.N]))
    return state


def lam_rows(z, tab_ref, b):
    def row(i):
        return tab_ref[b * 8 + i : b * 8 + i + 1, :]

    def full(i):
        return jnp.broadcast_to(row(i), (CHUNKS, z.N))

    return full(0), full(1), full(2), row(3), row(4)


def prepare(z, len_hbm, x_hbm, gout_hbm, rate_hbm, phase_hbm, gain_hbm, bias_hbm, skip_hbm, bglu_hbm, win_hbm, wout_hbm, wglu_hbm,
            v_ref, up_ref, stat_ref, keep_f, keep_r, chunk_f, chunk_r, dev_f, dev_r, tab_ref, power_ref,
            gain_ref, bias_ref, skip_ref, bglu_ref, win_ref, wout_ref, wglu_ref,
            tile_ref, natural_ref, x_ref, gout_ref, rate_ref, phase_ref, len_ref, sem):
    moves = [(x_hbm, x_ref), (len_hbm, len_ref), (rate_hbm, rate_ref), (phase_hbm, phase_ref), (gout_hbm, gout_ref),
             (gain_hbm, gain_ref), (bias_hbm, bias_ref), (win_hbm, win_ref), (skip_hbm, skip_ref), (bglu_hbm, bglu_ref),
             (wout_hbm, wout_ref), (wglu_hbm, wglu_ref)]
    copies = [pltpu.make_async_copy(a, b, sem.at[i]) for i, (a, b) in enumerate(moves)]
    for c in copies:
        c.start()
    copies[0].wait()
    to_steps(z, lambda rows: x_ref[rows, :].astype(F32), v_ref, natural_ref)

    def body(rows, c):
        v = v_ref[rows, :]
        return c[0] + fold(v), c[1] + fold(v * v)

    zero = jnp.zeros((8, z.D), F32)
    s0, s1 = tiles(z, body, (zero, zero))
    pack(tile_ref, [jnp.sum(s0, 0, keepdims=True), jnp.sum(s1, 0, keepdims=True)])
    spread(stat_ref, tile_ref)
    for c in copies[1:5]:
        c.wait()
    to_steps(z, lambda rows: gout_ref[rows, :].astype(F32), up_ref, natural_ref)
    base = lax.axis_index("tm") * z.S
    place = lax.broadcasted_iota(jnp.int32, (z.S, LANES), 0)
    at = base + (place % CHUNKS) * z.L + place // CHUNKS
    chunk_at = base + z.L * lax.broadcasted_iota(jnp.int32, (CHUNKS, LANES), 0)
    dev_at = z.S * lax.broadcasted_iota(jnp.int32, (z.tm, LANES), 0)
    for r in range(z.R):
        end = jnp.int32(0)
        hit = [jnp.zeros(a.shape, jnp.bool_) for a in (at, at, chunk_at, chunk_at, dev_at, dev_at)]
        for q in range(z.seqs):
            start = end
            end = end + len_ref[r, q]
            last = end - 1
            hit[0] = hit[0] | (at == start)
            hit[1] = hit[1] | (at == last)
            for i, mark in ((2, start), (3, last)):
                hit[i] = hit[i] | ((chunk_at <= mark) & (mark < chunk_at + z.L))
            for i, mark in ((4, start), (5, last)):
                hit[i] = hit[i] | ((dev_at <= mark) & (mark < dev_at + z.S))
        keep = [1.0 - h.astype(F32) for h in hit]
        keep_f[r * z.S : (r + 1) * z.S, :] = keep[0]
        keep_r[r * z.S : (r + 1) * z.S, :] = keep[1]
        chunk_f[r * CHUNKS : (r + 1) * CHUNKS, :] = keep[2]
        chunk_r[r * CHUNKS : (r + 1) * CHUNKS, :] = keep[3]
        each = 2 * z.half
        for j in range(z.tm):
            for ref, k in ((dev_f, keep[4]), (dev_r, keep[5])):
                ref[j, r * each : (r + 1) * each, :] = jnp.broadcast_to(k[j : j + 1, :], (each, LANES))
    for b in range(2):
        rate, angle = rate_ref[b : b + 1, :], phase_ref[b : b + 1, :]
        size = jnp.exp(-rate)
        lr, li = size * jnp.cos(angle), size * jnp.sin(angle)
        gamma = jnp.sqrt(1.0 - jnp.exp(-2.0 * rate))

        def power(n):
            out, br, bi = None, lr, li
            while n:
                if n & 1:
                    out = (br, bi) if out is None else (out[0] * br - out[1] * bi, out[0] * bi + out[1] * br)
                br, bi = br * br - bi * bi, 2.0 * br * bi
                n >>= 1
            return out

        chunk_power, device_power = power(z.L), power(z.S)
        rows = [lr, li, gamma, chunk_power[0], chunk_power[1], jnp.exp(-2.0 * rate) / gamma]
        for i, row in enumerate(rows):
            tab_ref[b * 8 + i : b * 8 + i + 1, :] = row
        for i in range(6, 8):
            tab_ref[b * 8 + i : b * 8 + i + 1, :] = jnp.zeros_like(lr)
        pack(power_ref.at[2 * b], [device_power[0], device_power[0]] * z.R)
        pack(power_ref.at[2 * b + 1], [-device_power[1], device_power[1]] * z.R)
    for c in copies[5:]:
        c.wait()


def enter(z, b, stat_ref, v_ref, gain_ref, bias_ref, win_ref, keep_ref, chunk_ref, tab_ref,
          norm_ref, low_ref, proj_ref, ends_ref, send_ref, stat_tile, tile_ref):
    total, square = two_sums(stat_ref, stat_tile, z)
    mean = total / z.tokens
    rstd = lax.rsqrt(square / z.tokens - mean * mean + EPS)
    norm_ref[0:1, :] = mean
    norm_ref[1:2, :] = rstd
    gain, bias = gain_ref[b : b + 1, :], bias_ref[b : b + 1, :]

    def body(rows, c):
        xhat = (v_ref[rows, :] - mean) * rstd
        low_ref[rows, :] = (gain * xhat + bias).astype(BF16)
        return c

    tiles(z, body, 0)
    proj_ref[...] = dot(low_ref[...], win_ref[b])
    lr, li, gamma, pr, pi = lam_rows(z, tab_ref, b)
    state = scan(z, proj_ref, gamma, lr, li, keep_ref, zeros_state(z), b == 1)
    pack(tile_ref, end_state(z, state, ends_ref, chunk_ref, pr, pi, b == 1))
    spread(send_ref, tile_ref)


def gelu_pair(y):
    cdf = 0.5 + 0.5 * lax.erf(y * ROOT_HALF)
    return y * cdf, cdf + y * (ROOT_TWO_PI_INV * jnp.exp(-0.5 * y * y))


def mix(z, b, recv_ref, dev_ref, power_ref, ends_ref, chunk_ref, proj_ref, keep_ref, tab_ref, v_ref, norm_ref, gain_ref,
        bias_ref, skip_ref, wout_ref, wglu_ref, h_ref, hlow_ref, carry_ref, slope_ref, act_ref, tile_ref, wide_ref):
    lr, li, gamma, pr, pi = lam_rows(z, tab_ref, b)
    state = carries(z, recv_ref, dev_ref, power_ref, b, 1.0, ends_ref, chunk_ref, pr, pi, tile_ref, carry_ref, b == 1)

    put = pair_store(z, hlow_ref)

    def visit(r, s, rows, hr, hi):
        h_ref[rows, 0 : z.N] = hr
        h_ref[rows, z.N : 2 * z.N] = hi
        put(r, s, hr, hi)

    scan(z, proj_ref, gamma, lr, li, keep_ref, state, b == 1, visit)
    slope_ref[...] = dot(hlow_ref[...], wout_ref[b])
    mean, rstd = norm_ref[0:1, :], norm_ref[1:2, :]
    gain, bias, skip = gain_ref[b : b + 1, :], bias_ref[b : b + 1, :], skip_ref[b : b + 1, :]

    def body(rows, c):
        xn = gain * ((v_ref[rows, :] - mean) * rstd) + bias
        act, slope = gelu_pair(slope_ref[rows, :] + skip * xn)
        act_ref[rows, :] = act.astype(BF16)
        slope_ref[rows, :] = slope
        return c

    tiles(z, body, 0)
    wide_ref[...] = dot(act_ref[...], wglu_ref[b])


def middle(z, recv_ref, dev_ref, power_ref, ends_ref, chunk_ref, proj_ref, keep_ref, tab_ref, v_ref, norm_ref, gain_ref,
           bias_ref, skip_ref, wout_ref, wglu_ref, bglu_ref,
           h_ref, hlow_ref, carry_ref, slope_ref, act_ref, sig_ref, gate_ref, next_ref, stat_ref, tile_ref, wide_ref, stat_tile):
    mix(z, 0, recv_ref, dev_ref, power_ref, ends_ref, chunk_ref, proj_ref, keep_ref, tab_ref, v_ref, norm_ref, gain_ref,
        bias_ref, skip_ref, wout_ref, wglu_ref, h_ref, hlow_ref, carry_ref, slope_ref, act_ref, tile_ref, wide_ref)
    d = z.D
    b1, b2 = bglu_ref[0:1, 0:d], bglu_ref[0:1, d : 2 * d]

    def body(rows, c):
        z1 = wide_ref[rows, 0:d] + b1
        sig = jax.nn.sigmoid(wide_ref[rows, d : 2 * d] + b2)
        prod = z1 * sig
        sig_ref[rows, :] = sig
        gate_ref[rows, :] = prod * (1.0 - sig)
        v = v_ref[rows, :] + prod
        next_ref[rows, :] = v
        return c[0] + fold(v), c[1] + fold(v * v)

    zero = jnp.zeros((8, d), F32)
    s0, s1 = tiles(z, body, (zero, zero))
    pack(stat_tile, [jnp.sum(s0, 0, keepdims=True), jnp.sum(s1, 0, keepdims=True)])
    spread(stat_ref, stat_tile)


def descend(z, b, grad_bglu, dz_ref, slope_ref, v_ref, norm_ref, gain_ref, bias_ref, wglu_ref, wout_ref, keep_ref, chunk_ref, tab_ref,
            dy_ref, dylow_ref, dh_ref, ends_ref, send_ref, small_ref, tile_ref):
    dy_ref[...] = dot_t(dz_ref[...], wglu_ref[b])
    mean, rstd = norm_ref[0:1, :], norm_ref[1:2, :]
    gain, bias = gain_ref[b : b + 1, :], bias_ref[b : b + 1, :]

    def body(rows, c):
        xn = gain * ((v_ref[rows, :] - mean) * rstd) + bias
        dy = dy_ref[rows, :] * slope_ref[rows, :]
        dy_ref[rows, :] = dy
        dylow_ref[rows, :] = dy.astype(BF16)
        return c + fold(dy * xn)

    grad_skip = tiles(z, body, jnp.zeros((8, z.D), F32))
    small_ref[0:1, :] = jnp.sum(grad_skip, 0, keepdims=True)
    total = jnp.sum(grad_bglu, 0, keepdims=True)
    small_ref[1:2, :] = total[:, 0 : z.D]
    small_ref[2:3, :] = total[:, z.D : 2 * z.D]
    dh_ref[...] = dot_t(dylow_ref[...], wout_ref[b])
    lr, li, _, pr, pi = lam_rows(z, tab_ref, b)
    state = scan(z, dh_ref, None, lr, -li, keep_ref, zeros_state(z), b == 0)
    pack(tile_ref, end_state(z, state, ends_ref, chunk_ref, pr, -pi, b == 0))
    spread(send_ref, tile_ref)


def turn(z, recv_ref, dev_ref, power_ref, ends_ref, chunk_ref, proj_ref, keep_ref, tab_ref, v_ref, norm_ref, gain_ref,
         bias_ref, skip_ref, wout_ref, wglu_ref, bglu_ref, gout_ref, adj_keep_ref, adj_chunk_ref,
         h_ref, carry_ref, final_ref, dy_ref, dh_ref, adj_ends_ref, send_ref, small_ref, half_keep, half_send,
         tile_ref, wide_ref, slope_ref, hlow_ref, act_ref, dz_ref, dylow_ref):
    mix(z, 1, recv_ref, dev_ref, power_ref, ends_ref, chunk_ref, proj_ref, keep_ref, tab_ref, v_ref, norm_ref, gain_ref,
        bias_ref, skip_ref, wout_ref, wglu_ref, h_ref, hlow_ref, carry_ref, slope_ref, act_ref, tile_ref, wide_ref)
    d = z.D
    b1, b2 = bglu_ref[1:2, 0:d], bglu_ref[1:2, d : 2 * d]

    def body(rows, c):
        z1 = wide_ref[rows, 0:d] + b1
        sig = jax.nn.sigmoid(wide_ref[rows, d : 2 * d] + b2)
        prod = z1 * sig
        final_ref[rows, :] = v_ref[rows, :] + prod
        e = gout_ref[rows, :]
        d1, d2 = e * sig, e * (prod * (1.0 - sig))
        dz_ref[rows, 0:d] = d1.astype(BF16)
        dz_ref[rows, d : 2 * d] = d2.astype(BF16)
        return c[0] + fold(d1), c[1] + fold(d2)

    zero = jnp.zeros((8, d), F32)
    s0, s1 = tiles(z, body, (zero, zero))
    descend(z, 1, jnp.concatenate([s0, s1], axis=1), dz_ref, slope_ref, v_ref, norm_ref, gain_ref, bias_ref, wglu_ref, wout_ref,
            adj_keep_ref, adj_chunk_ref, tab_ref, dy_ref, dylow_ref, dh_ref, adj_ends_ref, send_ref, small_ref, tile_ref)
    split_strips(z, half_keep, half_send, units(act_ref, dz_ref, half_keep) + units(hlow_ref, dylow_ref, half_keep))


def finish(z, b, recv_ref, dev_ref, power_ref, ends_ref, chunk_ref, dh_ref, keep_ref, tab_ref, proj_ref, h_ref, carry_ref,
           fwd_keep_ref, dy_ref, v_ref, norm_ref, skip_ref, win_ref, emit,
           dplow_ref, dxn_ref, lam_ref, tile_ref, adj_carry_ref):
    lr, li, gamma, pr, pi = lam_rows(z, tab_ref, b)
    reverse = b == 0
    state = carries(z, recv_ref, dev_ref, power_ref, b, -1.0, ends_ref, chunk_ref, pr, -pi, tile_ref, adj_carry_ref, reverse)
    zero = jnp.zeros((CHUNKS, z.N), F32)
    sums = [zero, zero, zero]
    put = pair_store(z, dplow_ref)

    def visit(r, s, rows, gr, gi):
        put(r, s, gamma * gr, gamma * gi)
        sums[2] = sums[2] + gr * proj_ref[rows, 0 : z.N] + gi * proj_ref[rows, z.N : 2 * z.N]
        if s == (0 if b == 0 else z.L - 1):
            span = slice(r * CHUNKS, (r + 1) * CHUNKS)
            nr, ni = carry_ref[span, 0 : z.N], carry_ref[span, z.N : 2 * z.N]
        else:
            near = step_rows(z, r, s - 1 if b == 0 else s + 1)
            nr, ni = h_ref[near, 0 : z.N], h_ref[near, z.N : 2 * z.N]
        keep = wide(fwd_keep_ref[rows, :], z)
        nr, ni = keep * nr, keep * ni
        sums[0] = sums[0] + (gr * nr + gi * ni)
        sums[1] = sums[1] + (gi * nr - gr * ni)

    scan(z, dh_ref, None, lr, -li, keep_ref, state, reverse, visit)
    dr, di, dg = (jnp.sum(s, 0, keepdims=True) for s in sums)
    r0, i0 = lr[0:1, :], li[0:1, :]
    lam_ref[0:1, :] = dg * tab_ref[b * 8 + 5 : b * 8 + 6, :] - (dr * r0 + di * i0)
    lam_ref[1:2, :] = di * r0 - dr * i0

    dxn_ref[...] = dot_t(dplow_ref[...], win_ref[b])
    mean, rstd = norm_ref[0:1, :], norm_ref[1:2, :]
    skip = skip_ref[b : b + 1, :]

    def body(rows, c):
        xhat = (v_ref[rows, :] - mean) * rstd
        dxn = dxn_ref[rows, :] + skip * dy_ref[rows, :]
        dxn_ref[rows, :] = dxn
        return c[0] + fold(dxn), c[1] + fold(dxn * xhat)

    zero = jnp.zeros((8, z.D), F32)
    s0, s1 = tiles(z, body, (zero, zero))
    emit(jnp.sum(s0, 0, keepdims=True), jnp.sum(s1, 0, keepdims=True))


def norm_grad(z, b, bias_sum, gain_sum, norm_ref, gain_ref):
    mean, rstd = norm_ref[0:1, :], norm_ref[1:2, :]
    gain = gain_ref[b : b + 1, :]
    scale, shift, slope = rstd * gain, rstd * gain * bias_sum / z.tokens, rstd * gain * gain_sum / z.tokens

    def grad(dxn, v, up):
        return scale * dxn - shift - ((v - mean) * rstd) * slope + up

    return grad


def lower_block(z, stat_ref, dxn_ref, v1_ref, norm1_ref, gout_ref, sig_ref, gate_ref, slope_ref, v_ref, norm_ref, gain_ref, bias_ref,
                wglu_ref, wout_ref, keep_ref, chunk_ref, tab_ref, act_ref, hlow_ref,
                total_ref, e_ref, dy_ref, dh_ref, ends_ref, send_ref, small_ref, glu_keep, glu_send, out_keep, out_send,
                tile_ref, stat_tile, dz_ref, dylow_ref):
    bias_sum, gain_sum = two_sums(stat_ref, stat_tile, z)
    grad = norm_grad(z, 1, bias_sum, gain_sum, norm1_ref, gain_ref)
    total_ref[0:1, :] = bias_sum
    total_ref[1:2, :] = gain_sum
    d = z.D

    def body(rows, c):
        e = grad(dxn_ref[rows, :], v1_ref[rows, :], gout_ref[rows, :])
        e_ref[rows, :] = e
        d1, d2 = e * sig_ref[rows, :], e * gate_ref[rows, :]
        dz_ref[rows, 0:d] = d1.astype(BF16)
        dz_ref[rows, d : 2 * d] = d2.astype(BF16)
        return c[0] + fold(d1), c[1] + fold(d2)

    zero = jnp.zeros((8, d), F32)
    s0, s1 = tiles(z, body, (zero, zero))
    descend(z, 0, jnp.concatenate([s0, s1], axis=1), dz_ref, slope_ref, v_ref, norm_ref, gain_ref, bias_ref, wglu_ref, wout_ref,
            keep_ref, chunk_ref, tab_ref, dy_ref, dylow_ref, dh_ref, ends_ref, send_ref, small_ref, tile_ref)
    split_strips(z, glu_keep, glu_send, units(act_ref, dz_ref, glu_keep))
    split_strips(z, out_keep, out_send, units(hlow_ref, dylow_ref, out_keep))


def units(a_ref, b_ref, like):
    w = like.shape[1]

    def strip(i):
        return lambda: dot_0(a_ref[...], b_ref[:, i * w : (i + 1) * w])

    return [strip(i) for i in range(b_ref.shape[1] // w)]


def finish_upper(z, *refs):
    ins, low_ref, outs = refs[:17], refs[17], refs[18:]
    dxn_ref, stat_ref, lam_ref, keep_ref, send_ref, dplow_ref, tile_ref, carry_ref, stat_tile = outs

    def emit(bias_sum, gain_sum):
        pack(stat_tile, [bias_sum, gain_sum])
        spread(stat_ref, stat_tile)

    finish(z, 1, *ins, emit, dplow_ref, dxn_ref, lam_ref, tile_ref, carry_ref)
    split_strips(z, keep_ref, send_ref, units(low_ref, dplow_ref, keep_ref))


def finish_lower(z, *refs):
    ins, (low_ref, small0_ref, small1_ref, lam1_ref), outs = refs[:17], refs[17:21], refs[21:]
    dxn_ref, keep_ref, send_ref, dplow_ref, lam_ref, tile_ref, carry_ref = outs
    first = keep_ref.shape[0] - z.extra

    def emit(bias_sum, gain_sum):
        sums = [bias_sum, gain_sum]
        for small, lam in ((small0_ref, lam_ref), (small1_ref, lam1_ref)):
            sums += [small[0:1, :], small[1:2, :], small[2:3, :], lam[0:1, :], lam[1:2, :]]
        for ref in (keep_ref, send_ref):
            k = pack(ref, sums, first)
            if k < ref.shape[0]:
                ref[k:, :] = jnp.zeros((ref.shape[0] - k, ref.shape[1]), F32)

    finish(z, 0, *ins, emit, dplow_ref, dxn_ref, lam_ref, tile_ref, carry_ref)
    split_strips(z, keep_ref, send_ref, units(low_ref, dplow_ref, keep_ref))


def last(z, small_ref, dxn_ref, v_ref, norm_ref, gain_ref, e_ref, total1_ref, final_ref, out_ref, grad_ref, gain_out, bias_out, rate_out, phase_out, skip_out,
         bglu_out, natural_ref, work_ref):
    w = small_ref.shape[1]
    at = [0]

    def take(width):
        row = unpack(small_ref, at[0], width // w)
        at[0] += width // w
        return row

    bias_sum, gain_sum = take(z.D), take(z.D)
    grad = norm_grad(z, 0, bias_sum, gain_sum, norm_ref, gain_ref)
    bias_out[0:1, :] = bias_sum
    gain_out[0:1, :] = gain_sum
    bias_out[1:2, :] = total1_ref[0:1, :]
    gain_out[1:2, :] = total1_ref[1:2, :]
    for b in range(2):
        for ref, width in ((skip_out, z.D), (bglu_out, 2 * z.D), (rate_out, z.N), (phase_out, z.N)):
            ref[b : b + 1, :] = take(width)

    def body(rows, c):
        work_ref[rows, :] = grad(dxn_ref[rows, :], v_ref[rows, :], e_ref[rows, :])
        return c

    tiles(z, body, 0)
    to_time(z, work_ref, grad_ref, natural_ref)
    to_time(z, final_ref, out_ref, natural_ref)


GRAD_TILE = 64
SEQ = (0, 2, 4, 1, 3)
FIRST = ()
FLOPS = 20000000000
HINTED = ("halves", "join", "add", "total", "finish1", "lower_block", "finish0", "last")
WAIT = 3
FLAT = (1, 1, 1, 2, 1)
ORDERS = ((0, 1, 2, 3, 4), (0, 1, 2, 3, 4), (0, 1, 2, 3, 4), (0, 3, 1, 2, 4), (0, 3, 1, 2, 4))
STRIP = 256


def bit_of(z, place, parity):
    if place in (1, 2) and z.bits > 2:
        return place if parity else 3 - place
    return place


def own_bit(z, place):
    me = lax.axis_index("tm") * z.rows + lax.axis_index("rows")
    odd = me % 2
    return (me >> (odd * bit_of(z, place, 1) + (1 - odd) * bit_of(z, place, 0))) % 2


def pairs(z, place):
    return [(i, i ^ (1 << bit_of(z, place, i % 2))) for i in range(z.all)]


def split_strips(z, keep_ref, send_ref, strips):
    bit = own_bit(z, 0)
    cut = len(strips) // 2

    def write(ref, products):
        for i, product in enumerate(products):
            ref[i * z.D : (i + 1) * z.D, :] = product()

    @pl.when(bit == 0)
    def _():
        write(keep_ref, strips[:cut])
        write(send_ref, strips[cut:])

    @pl.when(bit == 1)
    def _():
        write(keep_ref, strips[cut:])
        write(send_ref, strips[:cut])


def strips_of(n):
    size = math.gcd(GRAD_TILE, n)

    def rows(part, i):
        return pl.ds(pl.multiple_of(part * n + i * size, math.gcd(size, 8)), size)

    return n // size, rows


def halves(z, step, extra, keep_ref, recv_ref, next_ref, send_ref):
    n = next_ref.shape[0] - extra
    bit = own_bit(z, step)
    count, rows = strips_of(n)

    def one(i, c):
        for ref, part in ((send_ref, 1 - bit), (next_ref, bit)):
            ref[rows(0, i), :] = keep_ref[rows(part, i), :] + recv_ref[rows(part, i), :]
        return c

    lax.fori_loop(0, count, one, 0)
    if extra:
        both = keep_ref[2 * n :, :] + recv_ref[2 * n :, :]
        next_ref[n:, :] = both
        send_ref[n:, :] = both


def total(extra, keep_ref, recv_ref, out_ref, *extra_ref):
    n = out_ref.shape[0]
    out_ref[...] = keep_ref[0:n, :] + recv_ref[0:n, :]
    if extra:
        extra_ref[0][...] = keep_ref[n:, :] + recv_ref[n:, :]


def join(z, step, own_ref, recv_ref, out_ref):
    n = own_ref.shape[0]
    bit = own_bit(z, step)
    count, rows = strips_of(n)

    def one(i, c):
        for ref, part in ((own_ref, bit), (recv_ref, 1 - bit)):
            out_ref[rows(part, i), :] = ref[rows(0, i), :]
        return c

    lax.fori_loop(0, count, one, 0)


def add(keep_ref, recv_ref, out_ref):
    out_ref[...] = keep_ref[...] + recv_ref[...]


class Exchange:
    def __init__(self, z, keep, send, extra=0, order=(), flat=1):
        self.z, self.keep, self.send, self.extra = z, keep, send, extra
        self.order = order if len(order) == z.bits else tuple(range(z.bits))
        self.width = keep.shape[1]
        self.small = None
        deep = z.bits - flat
        self.plan = [("halve", i) for i in range(deep)] + [("sum", i) for i in range(deep, z.bits)] + [("double", i) for i in range(deep - 1, -1, -1)]

    def go(self):
        self.got = lax.ppermute(self.send, ("tm", "rows"), pairs(self.z, self.order[self.plan[0][1]]))

    def settle(self):
        z, x = self.z, self.extra
        (kind, i), (after, j) = self.plan.pop(0), self.plan[0]
        n = self.keep.shape[0]
        both = (self.keep, self.got)
        if kind == "double":
            (self.keep,) = run(functools.partial(join, z, self.order[i]), "join", [((2 * n, self.width), F32)], both)
        elif after == "halve":
            half = (((n - x) // 2 + x, self.width), F32)
            self.keep, self.send = run(functools.partial(halves, z, self.order[j], x), "halves", [half, half], both)
            return
        elif after == "double" and x:
            self.keep, self.small = run(functools.partial(total, x), "total", [((n - x, self.width), F32), ((x, self.width), F32)], both)
        else:
            (self.keep,) = run(add, "add", [((n, self.width), F32)], both)
        self.send = self.keep

    @property
    def closing(self):
        return len(self.plan) == 1


def assemble(z, which, *refs):
    own, got, (win_out, wout_out, wglu_out, sem) = refs[0], refs[1], refs[-4:]
    bit = own_bit(z, 0)
    w = own.shape[1]

    def strips(out, b):
        return [out.at[b, :, i * w : (i + 1) * w] for i in range(out.shape[2] // w)]

    outs = (
        lambda: strips(wglu_out, 1) + strips(wout_out, 1),
        lambda: strips(wglu_out, 0),
        lambda: strips(win_out, 0),
        lambda: strips(wout_out, 0),
        lambda: strips(win_out, 1),
    )[which]()
    cut = len(outs) // 2

    def place(low, high):
        copies = []
        for ref, part in ((low, outs[:cut]), (high, outs[cut:])):
            for k, out in enumerate(part):
                copies.append(pltpu.make_async_copy(ref.at[k * z.D : (k + 1) * z.D, :], out, sem.at[len(copies)]))
        for c in copies:
            c.start()
        for c in copies:
            c.wait()

    @pl.when(bit == 0)
    def _():
        place(own, got)

    @pl.when(bit == 1)
    def _():
        place(got, own)


def run(kernel, name, outs, args, scratch=(), sems=0, source=pltpu.VMEM, target=pltpu.VMEM, onto=()):
    if source is pltpu.HBM:
        args = [pltpu.with_memory_space_constraint(a, source) for a in args]
    shapes = [pltpu.VMEM(s, t) if t != jnp.int32 else pltpu.SMEM(s, t) for s, t in scratch]
    return pl.pallas_call(
        kernel,
        out_shape=[jax.ShapeDtypeStruct(s, t) for s, t in outs],
        in_specs=[pl.BlockSpec(memory_space=source)] * len(args) + [pl.BlockSpec(memory_space=target)] * len(onto),
        out_specs=[pl.BlockSpec(memory_space=target)] * len(outs),
        scratch_shapes=shapes + ([pltpu.SemaphoreType.DMA((sems,))] if sems else []),
        compiler_params=pltpu.CompilerParams(vmem_limit_bytes=16 << 20),
        cost_estimate=pl.CostEstimate(flops=FLOPS, bytes_accessed=1, transcendentals=0) if name in HINTED else None,
        input_output_aliases={len(args) + i: i for i in range(len(onto))},
        name=name,
    )(*args, *onto)


def body(x_in, lengths, bn_gain, bn_bias, w_in, decay_rate, phase, w_out, skip_gain, w_glu, b_glu, grad_out):
    rows, steps, width = x_in.shape
    z = Sizes(rows, steps, width, w_in.shape[2] // 2, lax.axis_size("tm"), lax.axis_size("rows"), lengths.shape[1])
    T, D, N = z.T, z.D, z.N
    everyone = ("tm", "rows")

    def swap(a, axis):
        return lax.all_to_all(a, axis, 0, 0)

    stat_shape = ((z.all, z.stat, LANES), F32)
    send_shape = ((z.tm, z.packed, LANES), F32)
    tile = ((z.packed, LANES), F32)
    stat_tile = ((z.stat, LANES), F32)
    full, low = ((T, D), F32), ((T, D), BF16)
    full_n, low_n = ((T, 2 * N), F32), ((T, 2 * N), BF16)
    chunk = ((z.R * CHUNKS, 2 * N), F32)
    mask = ((T, LANES), F32)
    chunk_mask = ((z.R * CHUNKS, LANES), F32)
    norm_shape = ((8, D), F32)
    small_shape = ((8, D), F32)
    lam_shape = ((8, N), F32)
    wide_f, wide_b = ((T, 2 * D), F32), ((T, 2 * D), BF16)
    bind = functools.partial

    natural = ((D // LANES, T, LANES), F32)
    (x, gout, stat0, keep_f, keep_r, chunk_f, chunk_r, dev_f, dev_r, tab, power,
     bn_gain, bn_bias, skip_gain, b_glu, w_in, w_out, w_glu) = run(
        bind(prepare, z), "prepare",
        [full, full, stat_shape, mask, mask, chunk_mask, chunk_mask, send_shape, send_shape, ((16, N), F32), ((4, z.packed, LANES), F32)]
        + [(a.shape, a.dtype) for a in (bn_gain, bn_bias, skip_gain, b_glu, w_in, w_out, w_glu)],
        (lengths, x_in.reshape(T, D), grad_out.reshape(T, D), decay_rate, phase, bn_gain, bn_bias, skip_gain, b_glu, w_in, w_out, w_glu),
        [stat_tile, natural, low, low, ((2, N), F32), ((2, N), F32), (lengths.shape, jnp.int32)], sems=12, source=pltpu.HBM)
    stat0 = swap(stat0, everyone)
    norm0, low0, proj0, ends0, send0 = run(
        bind(enter, z, 0), "enter0", [norm_shape, low, full_n, chunk, send_shape],
        (stat0, x, bn_gain, bn_bias, w_in, keep_f, chunk_f, tab), [stat_tile, tile])
    send0 = swap(send0, "tm")
    h0, hlow0, carry0, slope0, act0, sig0, gate0, v1, stat1 = run(
        bind(middle, z), "middle", [full_n, low_n, chunk, full, low, full, full, full, stat_shape],
        (send0, dev_f, power, ends0, chunk_f, proj0, keep_f, tab, x, norm0, bn_gain, bn_bias, skip_gain, w_out, w_glu, b_glu),
        [tile, wide_f, stat_tile])
    stat1 = swap(stat1, everyone)
    norm1, low1, proj1, ends1, send1 = run(
        bind(enter, z, 1), "enter1", [norm_shape, low, full_n, chunk, send_shape],
        (stat1, v1, bn_gain, bn_bias, w_in, keep_r, chunk_r, tab), [stat_tile, tile])
    send1 = swap(send1, "tm")
    W = STRIP if D * D // STRIP % (8 * z.all) == 0 else LANES

    def part(count, extra=0):
        return ((count * D // W * D // 2 + extra, W), F32)

    def tie(*values):
        return lax.optimization_barrier(values)

    h1, carry1, v2, dy1, dh1, adj_ends1, adj1, small1, keep1, send1 = run(
        bind(turn, z), "turn",
        [full_n, chunk, full, full, full_n, chunk, send_shape, small_shape, part(3), part(3)],
        (send1, dev_r, power, ends1, chunk_r, proj1, keep_r, tab, v1, norm1, bn_gain, bn_bias, skip_gain, w_out, w_glu, b_glu, gout,
         keep_f, chunk_f), [tile, wide_f, full, low_n, low, wide_b, low])
    one = Exchange(z, keep1, send1, order=ORDERS[0], flat=FLAT[0])
    one.send, adj1 = tie(one.send, adj1)
    one.go()
    adj1 = swap(adj1, "tm")
    one.got, adj1 = tie(one.got, adj1)
    one.settle()
    _, adj1 = tie(one.send, adj1)
    dxn1, sum1, lam1, keepi, sendi = run(
        bind(finish_upper, z), "finish1", [full, stat_shape, lam_shape, part(1), part(1)],
        (adj1, dev_f, power, adj_ends1, chunk_f, dh1, keep_f, tab, proj1, h1, carry1, keep_r, dy1, v1, norm1, skip_gain, w_in, low1),
        [low_n, tile, chunk, stat_tile])
    five = Exchange(z, keepi, sendi, order=ORDERS[4], flat=FLAT[4])
    *_, sum1 = tie(one.send, five.send, sum1)
    one.go()
    five.go()
    sum1 = swap(sum1, everyone)
    one.got, five.got, sum1 = tie(one.got, five.got, sum1)
    one.settle()
    five.settle()
    *_, sum1 = tie(one.send, five.send, sum1)
    total1, e1, dy0, dh0, adj_ends0, adj0, small0, keepa, senda, keepo, sendo = run(
        bind(lower_block, z), "lower_block",
        [norm_shape, full, full, full_n, chunk, send_shape, small_shape, part(2), part(2), part(1), part(1)],
        (sum1, dxn1, v1, norm1, gout, sig0, gate0, slope0, x, norm0, bn_gain, bn_bias, w_glu, w_out, keep_r, chunk_r, tab, act0, hlow0),
        [tile, stat_tile, wide_b, low])
    two = Exchange(z, keepa, senda, order=ORDERS[1], flat=FLAT[1])
    four = Exchange(z, keepo, sendo, order=ORDERS[3], flat=FLAT[3])
    *_, adj0 = tie(one.send, two.send, four.send, five.send, adj0)
    one.go()
    five.go()
    two.go()
    four.go()
    adj0 = swap(adj0, "tm")
    one.got, two.got, four.got, five.got, adj0 = tie(one.got, two.got, four.got, five.got, adj0)
    rows_sum = (2 * D + 2 * (3 * D + 2 * N)) // W
    z.extra = -(-rows_sum // 8) * 8
    last_part = part(1, z.extra)
    dxn0, keepb, sendb = run(
        bind(finish_lower, z), "finish0", [full, last_part, last_part],
        (adj0, dev_r, power, adj_ends0, chunk_r, dh0, keep_r, tab, proj0, h0, carry0, keep_f, dy0, x, norm0, skip_gain, w_in,
         low0, small0, small1, lam1),
        [low_n, lam_shape, tile, chunk])
    one.settle()
    two.settle()
    four.settle()
    five.settle()
    three = Exchange(z, keepb, sendb, z.extra, ORDERS[2], FLAT[2])
    for e in (one, five, two, four, three):
        e.go()
    sets = (one, two, three, four, five)
    ahead = three.send
    sums = (((2, D), F32), ((2, D), F32), ((2, N), F32), ((2, N), F32), ((2, D), F32), ((2, 2 * D), F32))
    small_outs, wait = None, WAIT
    placed, done, queue = (), [], list(FIRST) if z.bits == 5 else []
    while len(done) < len(sets):
        for i in queue or SEQ:
            e = sets[i]
            if i in done:
                continue
            e.got, _ = tie(e.got, ahead)
            if e.closing:
                placed = run(
                    bind(assemble, z, i), "assemble", [((2, D, 2 * N), F32), ((2, 2 * N, D), F32), ((2, D, 2 * D), F32)],
                    (e.keep, e.got), sems=8 * (STRIP // W), target=pltpu.HBM, onto=placed)
                ahead = placed[0]
                done.append(i)
            else:
                e.settle()
                e.go()
                ahead = e.send
                wait -= e.small is not None
                if wait == 0 and small_outs is None:
                    small_outs = run(
                            bind(last, z), "last", [low, full, *sums], (three.small, dxn0, x, norm0, bn_gain, e1, total1, v2), [natural, full])
                    ahead = small_outs[2]
        queue = []
    gwin, gwout, gwglu = placed
    out, grad_x, gain_out, bias_out, rate_out, phase_out, skip_out, bglu_out = small_outs
    return (
        out.reshape(rows, steps, width),
        grad_x.reshape(rows, steps, width),
        gain_out,
        bias_out,
        gwin,
        rate_out,
        phase_out,
        gwout,
        skip_out,
        gwglu,
        bglu_out,
    )


def solution(mesh):
    split, rep = P("rows", "tm", None), P()
    return jax.shard_map(
        body,
        mesh=mesh,
        in_specs=(split, P("rows", None)) + (rep,) * 9 + (split,),
        out_specs=(split, split) + (rep,) * 9,
        check_vma=False,
    )
```

```python
import functools
import math

import jax
import jax.numpy as jnp
from jax import lax
from jax.experimental import pallas as pl
from jax.experimental.pallas import tpu as pltpu
from jax.sharding import PartitionSpec as P

EPS = 1e-05
LANES = 128
CHUNKS = 8
TILE = 64
UNROLL = 4
F32 = jnp.float32
BF16 = jnp.bfloat16
ROOT_HALF = 0.7071067811865476
ROOT_TWO_PI_INV = 0.3989422804014327


class Sizes:
    def __init__(self, rows, steps, width, states, count_tm, count_rows, per_row):
        self.R, self.S, self.D, self.N = rows, steps, width, states
        self.T = rows * steps
        self.L = steps // CHUNKS
        self.tm, self.rows = count_tm, count_rows
        self.all = count_tm * count_rows
        self.seqs = per_row
        self.half = states // LANES
        self.packed = rows * 2 * self.half
        self.stat = 2 * width // LANES
        self.tokens = self.T * self.all
        self.bits = self.all.bit_length() - 1
        self.extra = 0


def dot(a, b):
    return jnp.dot(a, b, preferred_element_type=F32)


def dot_t(a, b):
    return lax.dot_general(a, b, (((1,), (1,)), ((), ())), preferred_element_type=F32)


def dot_0(a, b):
    return lax.dot_general(a, b, (((0,), (0,)), ((), ())), preferred_element_type=F32)


def fold(a):
    return a.reshape(a.shape[0] // 8, 8, a.shape[1]).sum(0)


def wide(a, z):
    return jnp.concatenate([a] * z.half, axis=1)


def tiles(z, body, carry):
    def one(i, c):
        return body(pl.ds(pl.multiple_of(i * TILE, TILE), TILE), c)

    return lax.fori_loop(0, z.T // TILE, one, carry, unroll=UNROLL)


def pack(ref, rows, k=0):
    w = ref.shape[1]
    for row in rows:
        for i in range(row.shape[1] // w):
            ref[k : k + 1, :] = row[:, i * w : (i + 1) * w]
            k += 1
    return k


def unpack(ref, first, count):
    return jnp.concatenate([ref[first + i : first + i + 1, :] for i in range(count)], axis=1)


def spread(out_ref, tile_ref):
    value = tile_ref[...]
    for j in range(out_ref.shape[0]):
        out_ref[j] = value


def two_sums(recv_ref, tile_ref, z):
    tile_ref[...] = jnp.sum(recv_ref[...], axis=0)
    n = z.D // LANES
    return unpack(tile_ref, 0, n), unpack(tile_ref, n, n)


def step_rows(z, r, s):
    first = r * z.S + s * CHUNKS
    return slice(first, first + CHUNKS)


def to_steps(z, source, out_ref, natural_ref):
    lanes = z.D // LANES

    def split(rows, c):
        value = source(rows)
        for k in range(lanes):
            natural_ref[k, rows, :] = value[:, k * LANES : (k + 1) * LANES]
        return c

    tiles(z, split, 0)
    for r in range(z.R):
        for s in range(z.L):
            for k in range(lanes):
                out_ref[step_rows(z, r, s), k * LANES : (k + 1) * LANES] = natural_ref[k, pl.ds(r * z.S + s, CHUNKS, stride=z.L), :]


def to_time(z, source_ref, out_ref, natural_ref):
    lanes = z.D // LANES
    for r in range(z.R):
        for s in range(z.L):
            for k in range(lanes):
                natural_ref[k, pl.ds(r * z.S + s, CHUNKS, stride=z.L), :] = source_ref[step_rows(z, r, s), k * LANES : (k + 1) * LANES]

    def join(rows, c):
        value = jnp.concatenate([natural_ref[k, rows, :] for k in range(lanes)], axis=1)
        out_ref[rows, :] = value.astype(out_ref.dtype)
        return c

    tiles(z, join, 0)


def pair_store(z, ref):
    held = {}

    def put(r, s, re, im):
        if (r, s ^ 1) not in held:
            held[r, s] = (re, im)
            return
        other = held.pop((r, s ^ 1))
        low, high = (other, (re, im)) if s & 1 else ((re, im), other)
        rows = slice(r * z.S + (s & ~1) * CHUNKS, r * z.S + ((s & ~1) + 2) * CHUNKS)
        ref[rows, 0 : z.N] = jnp.concatenate([low[0], high[0]], axis=0).astype(ref.dtype)
        ref[rows, z.N : 2 * z.N] = jnp.concatenate([low[1], high[1]], axis=0).astype(ref.dtype)

    return put


def scan(z, drive_ref, gain, lr, li, keep_ref, state, reverse, visit=None):
    for step in range(z.L):
        s = z.L - 1 - step if reverse else step
        for r in range(z.R):
            rows = step_rows(z, r, s)
            keep = wide(keep_ref[rows, :], z)
            ur = drive_ref[rows, 0 : z.N]
            ui = drive_ref[rows, z.N : 2 * z.N]
            if gain is not None:
                ur, ui = ur * gain, ui * gain
            hr, hi = keep * state[r][0], keep * state[r][1]
            state[r] = (lr * hr - li * hi + ur, lr * hi + li * hr + ui)
            if visit is not None:
                visit(r, s, rows, *state[r])
    return state


def zeros_state(z):
    return [(jnp.zeros((CHUNKS, z.N), F32), jnp.zeros((CHUNKS, z.N), F32)) for _ in range(z.R)]


def chunk_order(reverse):
    return range(CHUNKS - 1, -1, -1) if reverse else range(CHUNKS)


def end_state(z, state, ends_ref, chunk_keep_ref, pr, pi, reverse):
    rows = []
    for r in range(z.R):
        ends_ref[r * CHUNKS : (r + 1) * CHUNKS, 0 : z.N] = state[r][0]
        ends_ref[r * CHUNKS : (r + 1) * CHUNKS, z.N : 2 * z.N] = state[r][1]
    for r in range(z.R):
        cr = ci = None
        for c in chunk_order(reverse):
            k = r * CHUNKS + c
            er, ei = ends_ref[k : k + 1, 0 : z.N], ends_ref[k : k + 1, z.N : 2 * z.N]
            if cr is None:
                cr, ci = er, ei
            else:
                keep = wide(chunk_keep_ref[k : k + 1, :], z)
                cr, ci = keep * cr, keep * ci
                cr, ci = pr * cr - pi * ci + er, pr * ci + pi * cr + ei
        rows += [cr, ci]
    return rows


def carries(z, recv_ref, device_keep_ref, power_ref, b, sign, ends_ref, chunk_keep_ref, pr, pi, tile_ref, carry_ref, reverse):
    place = lax.axis_index("tm")
    pow_re = power_ref[2 * b]
    pow_im = sign * power_ref[2 * b + 1]
    is_re = (lax.broadcasted_iota(jnp.int32, (z.packed, LANES), 0) // z.half) % 2 == 0

    def hop(i, c):
        j = z.tm - 1 - i if reverse else i
        other = jnp.where(is_re, pltpu.roll(c, z.packed - z.half, 0), pltpu.roll(c, z.half, 0))
        return device_keep_ref[j] * (pow_re * c + pow_im * other) + recv_ref[j]

    ahead = z.tm - 1 - place if reverse else place
    tile_ref[...] = lax.fori_loop(0, ahead, hop, jnp.zeros((z.packed, LANES), F32))
    for r in range(z.R):
        cr = unpack(tile_ref, r * 2 * z.half, z.half)
        ci = unpack(tile_ref, r * 2 * z.half + z.half, z.half)
        order = list(chunk_order(reverse))
        for c in order:
            k = r * CHUNKS + c
            carry_ref[k : k + 1, 0 : z.N] = cr
            carry_ref[k : k + 1, z.N : 2 * z.N] = ci
            if c != order[-1]:
                keep = wide(chunk_keep_ref[k : k + 1, :], z)
                er, ei = ends_ref[k : k + 1, 0 : z.N], ends_ref[k : k + 1, z.N : 2 * z.N]
                cr, ci = keep * cr, keep * ci
                cr, ci = pr * cr - pi * ci + er, pr * ci + pi * cr + ei
    state = []
    for r in range(z.R):
        span = slice(r * CHUNKS, (r + 1) * CHUNKS)
        state.append((carry_ref[span, 0 : z.N], carry_ref[span, z.N : 2 * z.N]))
    return state


def lam_rows(z, tab_ref, b):
    def row(i):
        return tab_ref[b * 8 + i : b * 8 + i + 1, :]

    def full(i):
        return jnp.broadcast_to(row(i), (CHUNKS, z.N))

    return full(0), full(1), full(2), row(3), row(4)


def prepare(z, len_hbm, x_hbm, gout_hbm, rate_hbm, phase_hbm, gain_hbm, bias_hbm, skip_hbm, bglu_hbm, win_hbm, wout_hbm, wglu_hbm,
            v_ref, up_ref, stat_ref, keep_f, keep_r, chunk_f, chunk_r, dev_f, dev_r, tab_ref, power_ref,
            gain_ref, bias_ref, skip_ref, bglu_ref, win_ref, wout_ref, wglu_ref,
            tile_ref, natural_ref, x_ref, gout_ref, rate_ref, phase_ref, len_ref, sem):
    moves = [(x_hbm, x_ref), (len_hbm, len_ref), (rate_hbm, rate_ref), (phase_hbm, phase_ref), (gout_hbm, gout_ref),
             (gain_hbm, gain_ref), (bias_hbm, bias_ref), (win_hbm, win_ref), (skip_hbm, skip_ref), (bglu_hbm, bglu_ref),
             (wout_hbm, wout_ref), (wglu_hbm, wglu_ref)]
    copies = [pltpu.make_async_copy(a, b, sem.at[i]) for i, (a, b) in enumerate(moves)]
    for c in copies:
        c.start()
    copies[0].wait()
    to_steps(z, lambda rows: x_ref[rows, :].astype(F32), v_ref, natural_ref)

    def body(rows, c):
        v = v_ref[rows, :]
        return c[0] + fold(v), c[1] + fold(v * v)

    zero = jnp.zeros((8, z.D), F32)
    s0, s1 = tiles(z, body, (zero, zero))
    pack(tile_ref, [jnp.sum(s0, 0, keepdims=True), jnp.sum(s1, 0, keepdims=True)])
    spread(stat_ref, tile_ref)
    for c in copies[1:5]:
        c.wait()
    to_steps(z, lambda rows: gout_ref[rows, :].astype(F32), up_ref, natural_ref)
    base = lax.axis_index("tm") * z.S
    place = lax.broadcasted_iota(jnp.int32, (z.S, LANES), 0)
    at = base + (place % CHUNKS) * z.L + place // CHUNKS
    chunk_at = base + z.L * lax.broadcasted_iota(jnp.int32, (CHUNKS, LANES), 0)
    dev_at = z.S * lax.broadcasted_iota(jnp.int32, (z.tm, LANES), 0)
    for r in range(z.R):
        end = jnp.int32(0)
        hit = [jnp.zeros(a.shape, jnp.bool_) for a in (at, at, chunk_at, chunk_at, dev_at, dev_at)]
        for q in range(z.seqs):
            start = end
            end = end + len_ref[r, q]
            last = end - 1
            hit[0] = hit[0] | (at == start)
            hit[1] = hit[1] | (at == last)
            for i, mark in ((2, start), (3, last)):
                hit[i] = hit[i] | ((chunk_at <= mark) & (mark < chunk_at + z.L))
            for i, mark in ((4, start), (5, last)):
                hit[i] = hit[i] | ((dev_at <= mark) & (mark < dev_at + z.S))
        keep = [1.0 - h.astype(F32) for h in hit]
        keep_f[r * z.S : (r + 1) * z.S, :] = keep[0]
        keep_r[r * z.S : (r + 1) * z.S, :] = keep[1]
        chunk_f[r * CHUNKS : (r + 1) * CHUNKS, :] = keep[2]
        chunk_r[r * CHUNKS : (r + 1) * CHUNKS, :] = keep[3]
        each = 2 * z.half
        for j in range(z.tm):
            for ref, k in ((dev_f, keep[4]), (dev_r, keep[5])):
                ref[j, r * each : (r + 1) * each, :] = jnp.broadcast_to(k[j : j + 1, :], (each, LANES))
    for b in range(2):
        rate, angle = rate_ref[b : b + 1, :], phase_ref[b : b + 1, :]
        size = jnp.exp(-rate)
        lr, li = size * jnp.cos(angle), size * jnp.sin(angle)
        gamma = jnp.sqrt(1.0 - jnp.exp(-2.0 * rate))

        def power(n):
            out, br, bi = None, lr, li
            while n:
                if n & 1:
                    out = (br, bi) if out is None else (out[0] * br - out[1] * bi, out[0] * bi + out[1] * br)
                br, bi = br * br - bi * bi, 2.0 * br * bi
                n >>= 1
            return out

        chunk_power, device_power = power(z.L), power(z.S)
        rows = [lr, li, gamma, chunk_power[0], chunk_power[1], jnp.exp(-2.0 * rate) / gamma]
        for i, row in enumerate(rows):
            tab_ref[b * 8 + i : b * 8 + i + 1, :] = row
        for i in range(6, 8):
            tab_ref[b * 8 + i : b * 8 + i + 1, :] = jnp.zeros_like(lr)
        pack(power_ref.at[2 * b], [device_power[0], device_power[0]] * z.R)
        pack(power_ref.at[2 * b + 1], [-device_power[1], device_power[1]] * z.R)
    for c in copies[5:]:
        c.wait()


def enter(z, b, stat_ref, v_ref, gain_ref, bias_ref, win_ref, keep_ref, chunk_ref, tab_ref,
          norm_ref, low_ref, proj_ref, ends_ref, send_ref, stat_tile, tile_ref):
    total, square = two_sums(stat_ref, stat_tile, z)
    mean = total / z.tokens
    rstd = lax.rsqrt(square / z.tokens - mean * mean + EPS)
    norm_ref[0:1, :] = mean
    norm_ref[1:2, :] = rstd
    gain, bias = gain_ref[b : b + 1, :], bias_ref[b : b + 1, :]

    def body(rows, c):
        xhat = (v_ref[rows, :] - mean) * rstd
        low_ref[rows, :] = (gain * xhat + bias).astype(BF16)
        return c

    tiles(z, body, 0)
    proj_ref[...] = dot(low_ref[...], win_ref[b])
    lr, li, gamma, pr, pi = lam_rows(z, tab_ref, b)
    state = scan(z, proj_ref, gamma, lr, li, keep_ref, zeros_state(z), b == 1)
    pack(tile_ref, end_state(z, state, ends_ref, chunk_ref, pr, pi, b == 1))
    spread(send_ref, tile_ref)


def gelu_pair(y):
    cdf = 0.5 + 0.5 * lax.erf(y * ROOT_HALF)
    return y * cdf, cdf + y * (ROOT_TWO_PI_INV * jnp.exp(-0.5 * y * y))


def mix(z, b, recv_ref, dev_ref, power_ref, ends_ref, chunk_ref, proj_ref, keep_ref, tab_ref, v_ref, norm_ref, gain_ref,
        bias_ref, skip_ref, wout_ref, wglu_ref, h_ref, hlow_ref, carry_ref, slope_ref, act_ref, tile_ref, wide_ref):
    lr, li, gamma, pr, pi = lam_rows(z, tab_ref, b)
    state = carries(z, recv_ref, dev_ref, power_ref, b, 1.0, ends_ref, chunk_ref, pr, pi, tile_ref, carry_ref, b == 1)

    put = pair_store(z, hlow_ref)

    def visit(r, s, rows, hr, hi):
        h_ref[rows, 0 : z.N] = hr
        h_ref[rows, z.N : 2 * z.N] = hi
        put(r, s, hr, hi)

    scan(z, proj_ref, gamma, lr, li, keep_ref, state, b == 1, visit)
    slope_ref[...] = dot(hlow_ref[...], wout_ref[b])
    mean, rstd = norm_ref[0:1, :], norm_ref[1:2, :]
    gain, bias, skip = gain_ref[b : b + 1, :], bias_ref[b : b + 1, :], skip_ref[b : b + 1, :]

    def body(rows, c):
        xn = gain * ((v_ref[rows, :] - mean) * rstd) + bias
        act, slope = gelu_pair(slope_ref[rows, :] + skip * xn)
        act_ref[rows, :] = act.astype(BF16)
        slope_ref[rows, :] = slope
        return c

    tiles(z, body, 0)
    wide_ref[...] = dot(act_ref[...], wglu_ref[b])


def middle(z, recv_ref, dev_ref, power_ref, ends_ref, chunk_ref, proj_ref, keep_ref, tab_ref, v_ref, norm_ref, gain_ref,
           bias_ref, skip_ref, wout_ref, wglu_ref, bglu_ref,
           h_ref, hlow_ref, carry_ref, slope_ref, act_ref, sig_ref, gate_ref, next_ref, stat_ref, tile_ref, wide_ref, stat_tile):
    mix(z, 0, recv_ref, dev_ref, power_ref, ends_ref, chunk_ref, proj_ref, keep_ref, tab_ref, v_ref, norm_ref, gain_ref,
        bias_ref, skip_ref, wout_ref, wglu_ref, h_ref, hlow_ref, carry_ref, slope_ref, act_ref, tile_ref, wide_ref)
    d = z.D
    b1, b2 = bglu_ref[0:1, 0:d], bglu_ref[0:1, d : 2 * d]

    def body(rows, c):
        z1 = wide_ref[rows, 0:d] + b1
        sig = jax.nn.sigmoid(wide_ref[rows, d : 2 * d] + b2)
        prod = z1 * sig
        sig_ref[rows, :] = sig
        gate_ref[rows, :] = prod * (1.0 - sig)
        v = v_ref[rows, :] + prod
        next_ref[rows, :] = v
        return c[0] + fold(v), c[1] + fold(v * v)

    zero = jnp.zeros((8, d), F32)
    s0, s1 = tiles(z, body, (zero, zero))
    pack(stat_tile, [jnp.sum(s0, 0, keepdims=True), jnp.sum(s1, 0, keepdims=True)])
    spread(stat_ref, stat_tile)


def descend(z, b, grad_bglu, dz_ref, slope_ref, v_ref, norm_ref, gain_ref, bias_ref, wglu_ref, wout_ref, keep_ref, chunk_ref, tab_ref,
            dy_ref, dylow_ref, dh_ref, ends_ref, send_ref, small_ref, tile_ref):
    dy_ref[...] = dot_t(dz_ref[...], wglu_ref[b])
    mean, rstd = norm_ref[0:1, :], norm_ref[1:2, :]
    gain, bias = gain_ref[b : b + 1, :], bias_ref[b : b + 1, :]

    def body(rows, c):
        xn = gain * ((v_ref[rows, :] - mean) * rstd) + bias
        dy = dy_ref[rows, :] * slope_ref[rows, :]
        dy_ref[rows, :] = dy
        dylow_ref[rows, :] = dy.astype(BF16)
        return c + fold(dy * xn)

    grad_skip = tiles(z, body, jnp.zeros((8, z.D), F32))
    small_ref[0:1, :] = jnp.sum(grad_skip, 0, keepdims=True)
    total = jnp.sum(grad_bglu, 0, keepdims=True)
    small_ref[1:2, :] = total[:, 0 : z.D]
    small_ref[2:3, :] = total[:, z.D : 2 * z.D]
    dh_ref[...] = dot_t(dylow_ref[...], wout_ref[b])
    lr, li, _, pr, pi = lam_rows(z, tab_ref, b)
    state = scan(z, dh_ref, None, lr, -li, keep_ref, zeros_state(z), b == 0)
    pack(tile_ref, end_state(z, state, ends_ref, chunk_ref, pr, -pi, b == 0))
    spread(send_ref, tile_ref)


def turn(z, recv_ref, dev_ref, power_ref, ends_ref, chunk_ref, proj_ref, keep_ref, tab_ref, v_ref, norm_ref, gain_ref,
         bias_ref, skip_ref, wout_ref, wglu_ref, bglu_ref, gout_ref, adj_keep_ref, adj_chunk_ref,
         h_ref, carry_ref, final_ref, dy_ref, dh_ref, adj_ends_ref, send_ref, small_ref, half_keep, half_send,
         tile_ref, wide_ref, slope_ref, hlow_ref, act_ref, dz_ref, dylow_ref):
    mix(z, 1, recv_ref, dev_ref, power_ref, ends_ref, chunk_ref, proj_ref, keep_ref, tab_ref, v_ref, norm_ref, gain_ref,
        bias_ref, skip_ref, wout_ref, wglu_ref, h_ref, hlow_ref, carry_ref, slope_ref, act_ref, tile_ref, wide_ref)
    d = z.D
    b1, b2 = bglu_ref[1:2, 0:d], bglu_ref[1:2, d : 2 * d]

    def body(rows, c):
        z1 = wide_ref[rows, 0:d] + b1
        sig = jax.nn.sigmoid(wide_ref[rows, d : 2 * d] + b2)
        prod = z1 * sig
        final_ref[rows, :] = v_ref[rows, :] + prod
        e = gout_ref[rows, :]
        d1, d2 = e * sig, e * (prod * (1.0 - sig))
        dz_ref[rows, 0:d] = d1.astype(BF16)
        dz_ref[rows, d : 2 * d] = d2.astype(BF16)
        return c[0] + fold(d1), c[1] + fold(d2)

    zero = jnp.zeros((8, d), F32)
    s0, s1 = tiles(z, body, (zero, zero))
    descend(z, 1, jnp.concatenate([s0, s1], axis=1), dz_ref, slope_ref, v_ref, norm_ref, gain_ref, bias_ref, wglu_ref, wout_ref,
            adj_keep_ref, adj_chunk_ref, tab_ref, dy_ref, dylow_ref, dh_ref, adj_ends_ref, send_ref, small_ref, tile_ref)
    split_strips(z, half_keep, half_send, units(act_ref, dz_ref, half_keep) + units(hlow_ref, dylow_ref, half_keep))


def finish(z, b, recv_ref, dev_ref, power_ref, ends_ref, chunk_ref, dh_ref, keep_ref, tab_ref, proj_ref, h_ref, carry_ref,
           fwd_keep_ref, dy_ref, v_ref, norm_ref, skip_ref, win_ref, emit,
           dplow_ref, dxn_ref, lam_ref, tile_ref, adj_carry_ref):
    lr, li, gamma, pr, pi = lam_rows(z, tab_ref, b)
    reverse = b == 0
    state = carries(z, recv_ref, dev_ref, power_ref, b, -1.0, ends_ref, chunk_ref, pr, -pi, tile_ref, adj_carry_ref, reverse)
    zero = jnp.zeros((CHUNKS, z.N), F32)
    sums = [zero, zero, zero]
    put = pair_store(z, dplow_ref)

    def visit(r, s, rows, gr, gi):
        put(r, s, gamma * gr, gamma * gi)
        sums[2] = sums[2] + gr * proj_ref[rows, 0 : z.N] + gi * proj_ref[rows, z.N : 2 * z.N]
        if s == (0 if b == 0 else z.L - 1):
            span = slice(r * CHUNKS, (r + 1) * CHUNKS)
            nr, ni = carry_ref[span, 0 : z.N], carry_ref[span, z.N : 2 * z.N]
        else:
            near = step_rows(z, r, s - 1 if b == 0 else s + 1)
            nr, ni = h_ref[near, 0 : z.N], h_ref[near, z.N : 2 * z.N]
        keep = wide(fwd_keep_ref[rows, :], z)
        nr, ni = keep * nr, keep * ni
        sums[0] = sums[0] + (gr * nr + gi * ni)
        sums[1] = sums[1] + (gi * nr - gr * ni)

    scan(z, dh_ref, None, lr, -li, keep_ref, state, reverse, visit)
    dr, di, dg = (jnp.sum(s, 0, keepdims=True) for s in sums)
    r0, i0 = lr[0:1, :], li[0:1, :]
    lam_ref[0:1, :] = dg * tab_ref[b * 8 + 5 : b * 8 + 6, :] - (dr * r0 + di * i0)
    lam_ref[1:2, :] = di * r0 - dr * i0

    dxn_ref[...] = dot_t(dplow_ref[...], win_ref[b])
    mean, rstd = norm_ref[0:1, :], norm_ref[1:2, :]
    skip = skip_ref[b : b + 1, :]

    def body(rows, c):
        xhat = (v_ref[rows, :] - mean) * rstd
        dxn = dxn_ref[rows, :] + skip * dy_ref[rows, :]
        dxn_ref[rows, :] = dxn
        return c[0] + fold(dxn), c[1] + fold(dxn * xhat)

    zero = jnp.zeros((8, z.D), F32)
    s0, s1 = tiles(z, body, (zero, zero))
    emit(jnp.sum(s0, 0, keepdims=True), jnp.sum(s1, 0, keepdims=True))


def norm_grad(z, b, bias_sum, gain_sum, norm_ref, gain_ref):
    mean, rstd = norm_ref[0:1, :], norm_ref[1:2, :]
    gain = gain_ref[b : b + 1, :]
    scale, shift, slope = rstd * gain, rstd * gain * bias_sum / z.tokens, rstd * gain * gain_sum / z.tokens

    def grad(dxn, v, up):
        return scale * dxn - shift - ((v - mean) * rstd) * slope + up

    return grad


def lower_block(z, stat_ref, dxn_ref, v1_ref, norm1_ref, gout_ref, sig_ref, gate_ref, slope_ref, v_ref, norm_ref, gain_ref, bias_ref,
                wglu_ref, wout_ref, keep_ref, chunk_ref, tab_ref, act_ref, hlow_ref,
                total_ref, e_ref, dy_ref, dh_ref, ends_ref, send_ref, small_ref, glu_keep, glu_send, out_keep, out_send,
                tile_ref, stat_tile, dz_ref, dylow_ref):
    bias_sum, gain_sum = two_sums(stat_ref, stat_tile, z)
    grad = norm_grad(z, 1, bias_sum, gain_sum, norm1_ref, gain_ref)
    total_ref[0:1, :] = bias_sum
    total_ref[1:2, :] = gain_sum
    d = z.D

    def body(rows, c):
        e = grad(dxn_ref[rows, :], v1_ref[rows, :], gout_ref[rows, :])
        e_ref[rows, :] = e
        d1, d2 = e * sig_ref[rows, :], e * gate_ref[rows, :]
        dz_ref[rows, 0:d] = d1.astype(BF16)
        dz_ref[rows, d : 2 * d] = d2.astype(BF16)
        return c[0] + fold(d1), c[1] + fold(d2)

    zero = jnp.zeros((8, d), F32)
    s0, s1 = tiles(z, body, (zero, zero))
    descend(z, 0, jnp.concatenate([s0, s1], axis=1), dz_ref, slope_ref, v_ref, norm_ref, gain_ref, bias_ref, wglu_ref, wout_ref,
            keep_ref, chunk_ref, tab_ref, dy_ref, dylow_ref, dh_ref, ends_ref, send_ref, small_ref, tile_ref)
    split_strips(z, glu_keep, glu_send, units(act_ref, dz_ref, glu_keep))
    split_strips(z, out_keep, out_send, units(hlow_ref, dylow_ref, out_keep))


def units(a_ref, b_ref, like):
    w = like.shape[1]

    def strip(i):
        return lambda: dot_0(a_ref[...], b_ref[:, i * w : (i + 1) * w])

    return [strip(i) for i in range(b_ref.shape[1] // w)]


def finish_upper(z, *refs):
    ins, low_ref, outs = refs[:17], refs[17], refs[18:]
    dxn_ref, stat_ref, lam_ref, keep_ref, send_ref, dplow_ref, tile_ref, carry_ref, stat_tile = outs

    def emit(bias_sum, gain_sum):
        pack(stat_tile, [bias_sum, gain_sum])
        spread(stat_ref, stat_tile)

    finish(z, 1, *ins, emit, dplow_ref, dxn_ref, lam_ref, tile_ref, carry_ref)
    split_strips(z, keep_ref, send_ref, units(low_ref, dplow_ref, keep_ref))


def finish_lower(z, *refs):
    ins, (low_ref, small0_ref, small1_ref, lam1_ref), outs = refs[:17], refs[17:21], refs[21:]
    dxn_ref, keep_ref, send_ref, dplow_ref, lam_ref, tile_ref, carry_ref = outs
    first = keep_ref.shape[0] - z.extra

    def emit(bias_sum, gain_sum):
        sums = [bias_sum, gain_sum]
        for small, lam in ((small0_ref, lam_ref), (small1_ref, lam1_ref)):
            sums += [small[0:1, :], small[1:2, :], small[2:3, :], lam[0:1, :], lam[1:2, :]]
        for ref in (keep_ref, send_ref):
            k = pack(ref, sums, first)
            if k < ref.shape[0]:
                ref[k:, :] = jnp.zeros((ref.shape[0] - k, ref.shape[1]), F32)

    finish(z, 0, *ins, emit, dplow_ref, dxn_ref, lam_ref, tile_ref, carry_ref)
    split_strips(z, keep_ref, send_ref, units(low_ref, dplow_ref, keep_ref))


def last(z, small_ref, dxn_ref, v_ref, norm_ref, gain_ref, e_ref, total1_ref, final_ref, out_ref, grad_ref, gain_out, bias_out, rate_out, phase_out, skip_out,
         bglu_out, natural_ref, work_ref):
    w = small_ref.shape[1]
    at = [0]

    def take(width):
        row = unpack(small_ref, at[0], width // w)
        at[0] += width // w
        return row

    bias_sum, gain_sum = take(z.D), take(z.D)
    grad = norm_grad(z, 0, bias_sum, gain_sum, norm_ref, gain_ref)
    bias_out[0:1, :] = bias_sum
    gain_out[0:1, :] = gain_sum
    bias_out[1:2, :] = total1_ref[0:1, :]
    gain_out[1:2, :] = total1_ref[1:2, :]
    for b in range(2):
        for ref, width in ((skip_out, z.D), (bglu_out, 2 * z.D), (rate_out, z.N), (phase_out, z.N)):
            ref[b : b + 1, :] = take(width)

    def body(rows, c):
        work_ref[rows, :] = grad(dxn_ref[rows, :], v_ref[rows, :], e_ref[rows, :])
        return c

    tiles(z, body, 0)
    to_time(z, work_ref, grad_ref, natural_ref)
    to_time(z, final_ref, out_ref, natural_ref)


GRAD_TILE = 64
SEQ = (0, 2, 4, 1, 3)
FIRST = ()
FLOPS = 20000000000
HINTED = ("halves", "join", "add", "total", "finish1", "lower_block", "finish0", "last")
WAIT = 3
FLAT = (1, 1, 1, 2, 1)
ORDERS = ((0, 1, 2, 3, 4), (0, 1, 2, 3, 4), (0, 1, 2, 3, 4), (0, 3, 1, 2, 4), (0, 3, 1, 2, 4))
STRIP = 256


def bit_of(z, place, parity):
    if place in (1, 2) and z.bits > 2:
        return place if parity else 3 - place
    return place


def own_bit(z, place):
    me = lax.axis_index("tm") * z.rows + lax.axis_index("rows")
    odd = me % 2
    return (me >> (odd * bit_of(z, place, 1) + (1 - odd) * bit_of(z, place, 0))) % 2


def pairs(z, place):
    return [(i, i ^ (1 << bit_of(z, place, i % 2))) for i in range(z.all)]


def split_strips(z, keep_ref, send_ref, strips):
    bit = own_bit(z, 0)
    cut = len(strips) // 2

    def write(ref, products):
        for i, product in enumerate(products):
            ref[i * z.D : (i + 1) * z.D, :] = product()

    @pl.when(bit == 0)
    def _():
        write(keep_ref, strips[:cut])
        write(send_ref, strips[cut:])

    @pl.when(bit == 1)
    def _():
        write(keep_ref, strips[cut:])
        write(send_ref, strips[:cut])


def strips_of(n):
    size = math.gcd(GRAD_TILE, n)

    def rows(part, i):
        return pl.ds(pl.multiple_of(part * n + i * size, math.gcd(size, 8)), size)

    return n // size, rows


def halves(z, step, extra, keep_ref, recv_ref, next_ref, send_ref):
    n = next_ref.shape[0] - extra
    bit = own_bit(z, step)
    count, rows = strips_of(n)

    def one(i, c):
        for ref, part in ((send_ref, 1 - bit), (next_ref, bit)):
            ref[rows(0, i), :] = keep_ref[rows(part, i), :] + recv_ref[rows(part, i), :]
        return c

    lax.fori_loop(0, count, one, 0)
    if extra:
        both = keep_ref[2 * n :, :] + recv_ref[2 * n :, :]
        next_ref[n:, :] = both
        send_ref[n:, :] = both


def total(extra, keep_ref, recv_ref, out_ref, *extra_ref):
    n = out_ref.shape[0]
    out_ref[...] = keep_ref[0:n, :] + recv_ref[0:n, :]
    if extra:
        extra_ref[0][...] = keep_ref[n:, :] + recv_ref[n:, :]


def join(z, step, own_ref, recv_ref, out_ref):
    n = own_ref.shape[0]
    bit = own_bit(z, step)
    count, rows = strips_of(n)

    def one(i, c):
        for ref, part in ((own_ref, bit), (recv_ref, 1 - bit)):
            out_ref[rows(part, i), :] = ref[rows(0, i), :]
        return c

    lax.fori_loop(0, count, one, 0)


def add(keep_ref, recv_ref, out_ref):
    out_ref[...] = keep_ref[...] + recv_ref[...]


class Exchange:
    def __init__(self, z, keep, send, extra=0, order=(), flat=1):
        self.z, self.keep, self.send, self.extra = z, keep, send, extra
        self.order = order if len(order) == z.bits else tuple(range(z.bits))
        self.width = keep.shape[1]
        self.small = None
        deep = z.bits - flat
        self.plan = [("halve", i) for i in range(deep)] + [("sum", i) for i in range(deep, z.bits)] + [("double", i) for i in range(deep - 1, -1, -1)]

    def go(self):
        self.got = lax.ppermute(self.send, ("tm", "rows"), pairs(self.z, self.order[self.plan[0][1]]))

    def settle(self):
        z, x = self.z, self.extra
        (kind, i), (after, j) = self.plan.pop(0), self.plan[0]
        n = self.keep.shape[0]
        both = (self.keep, self.got)
        if kind == "double":
            (self.keep,) = run(functools.partial(join, z, self.order[i]), "join", [((2 * n, self.width), F32)], both)
        elif after == "halve":
            half = (((n - x) // 2 + x, self.width), F32)
            self.keep, self.send = run(functools.partial(halves, z, self.order[j], x), "halves", [half, half], both)
            return
        elif after == "double" and x:
            self.keep, self.small = run(functools.partial(total, x), "total", [((n - x, self.width), F32), ((x, self.width), F32)], both)
        else:
            (self.keep,) = run(add, "add", [((n, self.width), F32)], both)
        self.send = self.keep

    @property
    def closing(self):
        return len(self.plan) == 1


def assemble(z, which, *refs):
    own, got, (win_out, wout_out, wglu_out, sem) = refs[0], refs[1], refs[-4:]
    bit = own_bit(z, 0)
    w = own.shape[1]

    def strips(out, b):
        return [out.at[b, :, i * w : (i + 1) * w] for i in range(out.shape[2] // w)]

    outs = (
        lambda: strips(wglu_out, 1) + strips(wout_out, 1),
        lambda: strips(wglu_out, 0),
        lambda: strips(win_out, 0),
        lambda: strips(wout_out, 0),
        lambda: strips(win_out, 1),
    )[which]()
    cut = len(outs) // 2

    def place(low, high):
        copies = []
        for ref, part in ((low, outs[:cut]), (high, outs[cut:])):
            for k, out in enumerate(part):
                copies.append(pltpu.make_async_copy(ref.at[k * z.D : (k + 1) * z.D, :], out, sem.at[len(copies)]))
        for c in copies:
            c.start()
        for c in copies:
            c.wait()

    @pl.when(bit == 0)
    def _():
        place(own, got)

    @pl.when(bit == 1)
    def _():
        place(got, own)


def run(kernel, name, outs, args, scratch=(), sems=0, source=pltpu.VMEM, target=pltpu.VMEM, onto=()):
    if source is pltpu.HBM:
        args = [pltpu.with_memory_space_constraint(a, source) for a in args]
    shapes = [pltpu.VMEM(s, t) if t != jnp.int32 else pltpu.SMEM(s, t) for s, t in scratch]
    return pl.pallas_call(
        kernel,
        out_shape=[jax.ShapeDtypeStruct(s, t) for s, t in outs],
        in_specs=[pl.BlockSpec(memory_space=source)] * len(args) + [pl.BlockSpec(memory_space=target)] * len(onto),
        out_specs=[pl.BlockSpec(memory_space=target)] * len(outs),
        scratch_shapes=shapes + ([pltpu.SemaphoreType.DMA((sems,))] if sems else []),
        compiler_params=pltpu.CompilerParams(vmem_limit_bytes=16 << 20),
        cost_estimate=pl.CostEstimate(flops=FLOPS, bytes_accessed=1, transcendentals=0) if name in HINTED else None,
        input_output_aliases={len(args) + i: i for i in range(len(onto))},
        name=name,
    )(*args, *onto)


def body(x_in, lengths, bn_gain, bn_bias, w_in, decay_rate, phase, w_out, skip_gain, w_glu, b_glu, grad_out):
    rows, steps, width = x_in.shape
    z = Sizes(rows, steps, width, w_in.shape[2] // 2, lax.axis_size("tm"), lax.axis_size("rows"), lengths.shape[1])
    T, D, N = z.T, z.D, z.N
    everyone = ("tm", "rows")

    def swap(a, axis):
        return lax.all_to_all(a, axis, 0, 0)

    stat_shape = ((z.all, z.stat, LANES), F32)
    send_shape = ((z.tm, z.packed, LANES), F32)
    tile = ((z.packed, LANES), F32)
    stat_tile = ((z.stat, LANES), F32)
    full, low = ((T, D), F32), ((T, D), BF16)
    full_n, low_n = ((T, 2 * N), F32), ((T, 2 * N), BF16)
    chunk = ((z.R * CHUNKS, 2 * N), F32)
    mask = ((T, LANES), F32)
    chunk_mask = ((z.R * CHUNKS, LANES), F32)
    norm_shape = ((8, D), F32)
    small_shape = ((8, D), F32)
    lam_shape = ((8, N), F32)
    wide_f, wide_b = ((T, 2 * D), F32), ((T, 2 * D), BF16)
    bind = functools.partial

    natural = ((D // LANES, T, LANES), F32)
    (x, gout, stat0, keep_f, keep_r, chunk_f, chunk_r, dev_f, dev_r, tab, power,
     bn_gain, bn_bias, skip_gain, b_glu, w_in, w_out, w_glu) = run(
        bind(prepare, z), "prepare",
        [full, full, stat_shape, mask, mask, chunk_mask, chunk_mask, send_shape, send_shape, ((16, N), F32), ((4, z.packed, LANES), F32)]
        + [(a.shape, a.dtype) for a in (bn_gain, bn_bias, skip_gain, b_glu, w_in, w_out, w_glu)],
        (lengths, x_in.reshape(T, D), grad_out.reshape(T, D), decay_rate, phase, bn_gain, bn_bias, skip_gain, b_glu, w_in, w_out, w_glu),
        [stat_tile, natural, low, low, ((2, N), F32), ((2, N), F32), (lengths.shape, jnp.int32)], sems=12, source=pltpu.HBM)
    stat0 = swap(stat0, everyone)
    norm0, low0, proj0, ends0, send0 = run(
        bind(enter, z, 0), "enter0", [norm_shape, low, full_n, chunk, send_shape],
        (stat0, x, bn_gain, bn_bias, w_in, keep_f, chunk_f, tab), [stat_tile, tile])
    send0 = swap(send0, "tm")
    h0, hlow0, carry0, slope0, act0, sig0, gate0, v1, stat1 = run(
        bind(middle, z), "middle", [full_n, low_n, chunk, full, low, full, full, full, stat_shape],
        (send0, dev_f, power, ends0, chunk_f, proj0, keep_f, tab, x, norm0, bn_gain, bn_bias, skip_gain, w_out, w_glu, b_glu),
        [tile, wide_f, stat_tile])
    stat1 = swap(stat1, everyone)
    norm1, low1, proj1, ends1, send1 = run(
        bind(enter, z, 1), "enter1", [norm_shape, low, full_n, chunk, send_shape],
        (stat1, v1, bn_gain, bn_bias, w_in, keep_r, chunk_r, tab), [stat_tile, tile])
    send1 = swap(send1, "tm")
    W = STRIP if D * D // STRIP % (8 * z.all) == 0 else LANES

    def part(count, extra=0):
        return ((count * D // W * D // 2 + extra, W), F32)

    def tie(*values):
        return lax.optimization_barrier(values)

    h1, carry1, v2, dy1, dh1, adj_ends1, adj1, small1, keep1, send1 = run(
        bind(turn, z), "turn",
        [full_n, chunk, full, full, full_n, chunk, send_shape, small_shape, part(3), part(3)],
        (send1, dev_r, power, ends1, chunk_r, proj1, keep_r, tab, v1, norm1, bn_gain, bn_bias, skip_gain, w_out, w_glu, b_glu, gout,
         keep_f, chunk_f), [tile, wide_f, full, low_n, low, wide_b, low])
    one = Exchange(z, keep1, send1, order=ORDERS[0], flat=FLAT[0])
    one.send, adj1 = tie(one.send, adj1)
    one.go()
    adj1 = swap(adj1, "tm")
    one.got, adj1 = tie(one.got, adj1)
    one.settle()
    _, adj1 = tie(one.send, adj1)
    dxn1, sum1, lam1, keepi, sendi = run(
        bind(finish_upper, z), "finish1", [full, stat_shape, lam_shape, part(1), part(1)],
        (adj1, dev_f, power, adj_ends1, chunk_f, dh1, keep_f, tab, proj1, h1, carry1, keep_r, dy1, v1, norm1, skip_gain, w_in, low1),
        [low_n, tile, chunk, stat_tile])
    five = Exchange(z, keepi, sendi, order=ORDERS[4], flat=FLAT[4])
    *_, sum1 = tie(one.send, five.send, sum1)
    one.go()
    five.go()
    sum1 = swap(sum1, everyone)
    one.got, five.got, sum1 = tie(one.got, five.got, sum1)
    one.settle()
    five.settle()
    *_, sum1 = tie(one.send, five.send, sum1)
    total1, e1, dy0, dh0, adj_ends0, adj0, small0, keepa, senda, keepo, sendo = run(
        bind(lower_block, z), "lower_block",
        [norm_shape, full, full, full_n, chunk, send_shape, small_shape, part(2), part(2), part(1), part(1)],
        (sum1, dxn1, v1, norm1, gout, sig0, gate0, slope0, x, norm0, bn_gain, bn_bias, w_glu, w_out, keep_r, chunk_r, tab, act0, hlow0),
        [tile, stat_tile, wide_b, low])
    two = Exchange(z, keepa, senda, order=ORDERS[1], flat=FLAT[1])
    four = Exchange(z, keepo, sendo, order=ORDERS[3], flat=FLAT[3])
    *_, adj0 = tie(one.send, two.send, four.send, five.send, adj0)
    one.go()
    five.go()
    two.go()
    four.go()
    adj0 = swap(adj0, "tm")
    one.got, two.got, four.got, five.got, adj0 = tie(one.got, two.got, four.got, five.got, adj0)
    rows_sum = (2 * D + 2 * (3 * D + 2 * N)) // W
    z.extra = -(-rows_sum // 8) * 8
    last_part = part(1, z.extra)
    dxn0, keepb, sendb = run(
        bind(finish_lower, z), "finish0", [full, last_part, last_part],
        (adj0, dev_r, power, adj_ends0, chunk_r, dh0, keep_r, tab, proj0, h0, carry0, keep_f, dy0, x, norm0, skip_gain, w_in,
         low0, small0, small1, lam1),
        [low_n, lam_shape, tile, chunk])
    one.settle()
    two.settle()
    four.settle()
    five.settle()
    three = Exchange(z, keepb, sendb, z.extra, ORDERS[2], FLAT[2])
    for e in (one, five, two, four, three):
        e.go()
    sets = (one, two, three, four, five)
    ahead = three.send
    sums = (((2, D), F32), ((2, D), F32), ((2, N), F32), ((2, N), F32), ((2, D), F32), ((2, 2 * D), F32))
    small_outs, wait = None, WAIT
    placed, done, queue = (), [], list(FIRST) if z.bits == 5 else []
    while len(done) < len(sets):
        for i in queue or SEQ:
            e = sets[i]
            if i in done:
                continue
            e.got, _ = tie(e.got, ahead)
            if e.closing:
                placed = run(
                    bind(assemble, z, i), "assemble", [((2, D, 2 * N), F32), ((2, 2 * N, D), F32), ((2, D, 2 * D), F32)],
                    (e.keep, e.got), sems=8 * (STRIP // W), target=pltpu.HBM, onto=placed)
                ahead = placed[0]
                done.append(i)
            else:
                e.settle()
                e.go()
                ahead = e.send
                wait -= e.small is not None
                if wait == 0 and small_outs is None:
                    small_outs = run(
                            bind(last, z), "last", [low, full, *sums], (three.small, dxn0, x, norm0, bn_gain, e1, total1, v2), [natural, full])
                    ahead = small_outs[2]
        queue = []
    gwin, gwout, gwglu = placed
    out, grad_x, gain_out, bias_out, rate_out, phase_out, skip_out, bglu_out = small_outs
    return (
        out.reshape(rows, steps, width),
        grad_x.reshape(rows, steps, width),
        gain_out,
        bias_out,
        gwin,
        rate_out,
        phase_out,
        gwout,
        skip_out,
        gwglu,
        bglu_out,
    )


def solution(mesh):
    split, rep = P("rows", "tm", None), P()
    return jax.shard_map(
        body,
        mesh=mesh,
        in_specs=(split, P("rows", None)) + (rep,) * 9 + (split,),
        out_specs=(split, split) + (rep,) * 9,
        check_vma=False,
    )
```
